256 devices in a mesh: ctx: 16 (over y, x), tp: 16 (over z, core).
Axes of the slice: x: 4, y: 4, z: 8, core: 2. Of those that a mesh axis runs over, the one named last changes fastest.
Arguments:
- residual: bfloat16 [2048, 6144], P('ctx', 'tp'), may hold values from -65 to 65
- query_rows: bfloat16 [2048, 8192], P('ctx', 'tp'), may hold values from -6 to 6
- key_rows: bfloat16 [2048, 8192], P('ctx', 'tp'), may hold values from -6 to 6
- value_rows: bfloat16 [2048, 8192], P('ctx', 'tp'), may hold values from -6 to 6
- head_rates: float32 [64], replicated, may hold values from 0 to 1
- doc_lengths: int32 [4], replicated, may hold values from 1 to 1024, 2048 in all
- attn_gain: float32 [8192], P('tp'), may hold values from 0.1 to 1.9
- out_weight: bfloat16 [8192, 6144], P('tp', 'ctx'), may hold values from -0.09375 to 0.09375
- moe_gain: float32 [6144], P('tp'), may hold values from 0.1 to 1.9
- expert_ids: int32 [2048, 2], P('ctx'), may hold values from 0 to 15, all different within a row; in each aligned block of 128 rows (0 to 127, 128 to 255, ...) at most 24 rows name the same one
- expert_weights: float32 [2048, 2], P('ctx'), may hold values from 0.2 to 1
- gate_weight: bfloat16 [16, 6144, 4608], P('ctx', None, 'tp'), may hold values from -0.078125 to 0.078125
- up_weight: bfloat16 [16, 6144, 4608], P('ctx', None, 'tp'), may hold values from -0.078125 to 0.078125
- down_weight: bfloat16 [16, 4608, 6144], P('ctx', 'tp'), may hold values from -0.125 to 0.125
Outputs:
- output: bfloat16 [2048, 6144], P('ctx', 'tp')
The draws below stay inside these ranges and needn't reach their ends.
Inputs may be any that keep to these rules, and one draw needn't show every extreme that they name: `expert_ids`: each token names 2 different experts; among the tokens of one device (aligned blocks of 128 rows) no expert is named more than 24 times, a bound that some block reaches. `doc_lengths`: the longest document holds exactly 1024 positions.
All inputs are finite; a program needn't handle non-finite values.
Results may differ from the reference program's by a relative error of at most 0.015.
Values may be sent and summed in bfloat16 or wider, within the bound.
A program may use at most 64 MiB of HBM per device.

```python
import math
import jax
import jax.numpy as jnp
import numpy as np
from jax import lax

D = 6144
H = 64
HD = 128
FFW = 4608
TOP = 2
DOCS = 4
TOK_DEV = 128
TOKENS = 2048
EXPERTS = 16
CAP = 24
N_CTX = 16
N_TP = 16


def draw_head_rates(key, part):
    pick_key, quick_key, slow_key = jax.random.split(key, 3)
    quick_share = 0.5
    quick_heads = jax.random.bernoulli(pick_key, quick_share, (H,))
    quick_rate = jax.random.uniform(quick_key, (H,), jnp.float32, 1.0 / 50.0, 1.0 / 30.0)
    slow_rate = jnp.exp(jax.random.uniform(slow_key, (H,), jnp.float32, math.log(0.2 / TOKENS), math.log(2.0 / TOKENS)))
    return jnp.where(quick_heads, quick_rate, slow_rate).astype(jnp.float32)


def draw_residual(key, part):
    base_key, row_key, col_key = jax.random.split(key, 3)
    row_scale = jnp.exp(jax.random.uniform(row_key, (TOKENS, 1), jnp.float32, math.log(0.3), math.log(3.0)))
    ramp = jnp.exp(math.log(3.0) * jnp.arange(D, dtype=jnp.float32) / D)[None, :]
    col_scale = ramp * jnp.exp(jax.random.uniform(col_key, (1, D), jnp.float32, 0.0, math.log(3.0)))
    base_values = jnp.clip(jax.random.normal(base_key, (TOKENS, D), jnp.float32), -6.0, 6.0)
    return (0.4 * base_values * row_scale * col_scale).astype(jnp.bfloat16)


def spiked(array, key, source, target, parts, factor):
    owner, partner = [(jnp.arange(array.shape[position]) // (array.shape[position] // parts)).reshape([-1 if axis == position else 1 for axis in range(array.ndim)]) for position in (source, target)]
    chosen = jax.random.permutation(key, parts)[partner]
    strong = (owner == chosen) | (owner == (partner + parts // 2) % parts)
    return jnp.where(strong, factor * array, array)


def level_of(stream_key, extent, cuts, smallest, high):
    def one(dim, shards_of):
        draws = jax.random.uniform(jax.random.fold_in(jax.random.fold_in(stream_key, 6), dim), (shards_of,), jnp.float32, smallest / len(cuts), high / len(cuts))
        return jnp.repeat(jnp.exp(draws), extent[dim] // shards_of).reshape((-1,) + (1,) * (len(extent) - dim - 1))

    level = one(*cuts[0])
    for cut in cuts[1:]:
        level = level * one(*cut)
    return level


def length_profile(number_of, total, limit, slope):
    loads = [(1 << 20) // math.isqrt(standing ** slope) + 1 for standing in range(2, number_of + 1)]
    surplus, holding = total - limit - (number_of - 1), [1] * (number_of - 1)
    while surplus > 0:
        movable = [i for i in range(number_of - 1) if holding[i] < limit]
        whole, left = sum([loads[i] for i in movable]), surplus
        for i in movable:
            addition = min(limit - holding[i], max(1, left * loads[i] // whole), surplus)
            holding[i] = holding[i] + addition
            surplus = surplus - addition
    return np.array([limit] + holding)


def uneven(stream_key, count, total, most, slope):
    if count == 2:
        one = jax.random.randint(stream_key, (), max(1, total - most), min(most, total - 1) + 1)
        return jnp.stack([one, total - one])
    lengths = jnp.asarray(length_profile(count, total, most, slope), jnp.int32)
    pairs = (count - 1) // 2
    donor, sink = lengths[1:1 + 2 * pairs:2], lengths[2:2 + 2 * pairs:2]
    slack = jnp.minimum(donor - 1, most - sink)
    moved = jax.random.randint(jax.random.fold_in(stream_key, 1), (pairs,), 0, 1 << 20) % (slack + 1)
    lengths = lengths.at[1:1 + 2 * pairs:2].set(donor - moved).at[2:2 + 2 * pairs:2].set(sink + moved)
    return lengths[jax.random.permutation(jax.random.fold_in(stream_key, 2), count)]


def deal_out(stream_key, own, number, rows, count, top, bound, slope):
    ranking = jax.random.permutation(stream_key, count)
    crowded, common = shares(count, rows * top, bound, slope, True), shares(count, rows * top, bound, slope, False)
    places = jnp.arange(count)

    def named(tallies, turn):
        used = int((tallies > 0).sum())
        fixed = max(1, used // 4)
        moved = fixed + (places - fixed + turn * (used - fixed)) % max(1, count - fixed)
        return jnp.zeros((count,), jnp.int32).at[ranking[jnp.where(places < fixed, places, moved)]].set(jnp.asarray(tallies, jnp.int32))

    tallies = jnp.where(number % 4 == 0, named(crowded, number // 4), named(common, number - number // 4 - 1))
    mixed = jax.random.permutation(jax.random.fold_in(own, 3), count)
    source_of, receiver = mixed[0:count // 2 * 2:2], mixed[1:count // 2 * 2:2]
    margin = jnp.minimum(tallies[source_of] - 1, bound - tallies[receiver]) // 2
    margin = jnp.where((source_of == ranking[0]) | (receiver == ranking[0]) | (tallies[receiver] == 0), 0, jnp.maximum(margin, 0))
    moved = jax.random.randint(jax.random.fold_in(own, 4), (count // 2,), 0, 1 << 20) % (margin + 1)
    tallies = tallies.at[source_of].add(-moved).at[receiver].add(moved)
    items = jnp.searchsorted(jnp.cumsum(tallies), jnp.arange(rows * top), side="right").astype(jnp.int32)
    grid = items.reshape(top, rows).T
    grid = grid[jax.random.permutation(jax.random.fold_in(own, 1), rows)]
    turn = jax.random.randint(jax.random.fold_in(own, 2), (rows, 1), 0, top)
    return jnp.take_along_axis(grid, (jnp.arange(top)[None, :] + turn) % top, axis=1)


def shares(count, total, most, lean, full):
    loads = [(1 << 20) // math.isqrt(grade ** lean) + 1 for grade in range(1, count + 1)]
    largest = most if full else min(most, max(-(-total // count), total * loads[0] // sum(loads)))
    least = 1 if total - largest >= count - 1 else 0
    given, rest = [largest] + [least] * (count - 1), total - largest - least * (count - 1)
    while rest > 0:
        free = [i for i in range(1, count) if given[i] < largest] or [i for i in range(1, count) if given[i] < most]
        pool, remaining = sum([loads[i] for i in free]), rest
        for i in free:
            extra = min(most - given[i], max(1, remaining * loads[i] // pool), rest)
            given[i] = given[i] + extra
            rest = rest - extra
    return np.array(given)


def scatter_about(rng, extent, width, bound, shards=(), held_as=jnp.bfloat16):
    drawn = jax.random.normal(rng, extent, jnp.float32) * width
    if len(shards) > 0:
        drawn = level_of(rng, extent, shards, -0.22, 0.18) * drawn
    return jnp.clip(drawn, min=-bound, max=bound).astype(held_as)


def heavy_noise(stream_key, extent, deviation, bound, shards, heavy, kind=jnp.bfloat16):
    values = deviation * jax.random.normal(stream_key, extent, jnp.float32)
    if shards:
        values = values * level_of(stream_key, extent, shards, -0.22, 0.18)
    return jnp.clip(spiked(values, jax.random.fold_in(stream_key, 3), *heavy), -bound, bound).astype(kind)


def setup_inputs(seed: int = 0) -> dict:
    keys = jax.random.split(jax.random.key(seed), 15)
    residual = draw_residual(jax.random.fold_in(keys[14], 71), 0)
    query_rows = scatter_about(keys[1], (TOKENS, H * HD), 1.0, 6.0, ((0, 16), (1, 16)))
    key_rows = scatter_about(keys[2], (TOKENS, H * HD), 1.0, 6.0, ((0, 16), (1, 16)))
    value_rows = scatter_about(keys[3], (TOKENS, H * HD), 1.0, 6.0, ((0, 16), (1, 16)))
    head_rates = draw_head_rates(jax.random.fold_in(keys[14], 71), 0)
    doc_lengths = uneven(keys[5], DOCS, TOKENS, TOKENS // 2, 1).astype(jnp.int32)
    attn_gain = jnp.clip(1.0 + 0.18 * jax.random.normal(keys[6], (H * HD,), jnp.float32), 0.1, 1.9)
    out_weight = heavy_noise(keys[7], (H * HD, D), (H * HD) ** -0.5, 0.09375, ((0, 16), (1, 16)), (0, 1, 16, 2.0))
    moe_gain = jnp.clip(1.0 + 0.18 * jax.random.normal(keys[8], (D,), jnp.float32), 0.1, 1.9)
    expert_ids_keys = jax.random.split(jax.random.fold_in(keys[9], 1), TOKENS // TOK_DEV)
    expert_ids_turns = jax.random.permutation(jax.random.fold_in(keys[9], 3), TOKENS // TOK_DEV)
    expert_ids = jax.vmap(lambda own, number: deal_out(jax.random.fold_in(keys[9], 2), own, number, TOK_DEV, EXPERTS, TOP, CAP, 2))(expert_ids_keys, expert_ids_turns).reshape((TOKENS, TOP))
    expert_weights = jnp.clip(0.2 + 0.8 * jax.random.uniform(keys[10], (TOKENS, TOP), jnp.float32) ** level_of(keys[10], (TOKENS, TOP), ((0, 16),), -0.2, 0.2), 0.2, 1.0)
    gate_weight = scatter_about(keys[11], (EXPERTS, D, FFW), D ** -0.5, 0.078125, ((0, 16), (2, 16)))
    up_weight = scatter_about(keys[12], (EXPERTS, D, FFW), D ** -0.5, 0.078125, ((0, 16), (2, 16)))
    down_weight = heavy_noise(keys[13], (EXPERTS, FFW, D), FFW ** -0.5, 0.125, ((0, 16), (1, 16)), (1, 2, 16, 2.0))
    return dict(residual=residual, query_rows=query_rows, key_rows=key_rows, value_rows=value_rows, head_rates=head_rates, doc_lengths=doc_lengths, attn_gain=attn_gain, out_weight=out_weight, moe_gain=moe_gain, expert_ids=expert_ids, expert_weights=expert_weights, gate_weight=gate_weight, up_weight=up_weight, down_weight=down_weight)


def segment_of(doc_lengths, positions):
    doc_ends = jnp.cumsum(doc_lengths).astype(jnp.int32)
    doc_starts = (doc_ends - doc_lengths).astype(jnp.int32)
    return (lax.optimization_barrier(jnp.sum((positions[:, None] >= doc_starts[None, :]).astype(jnp.int32), axis=1)) - 1).astype(jnp.int32)

def local_attention(query_h, key_h, value_h, head_decay, segments, seg_before):
    length = query_h.shape[0]
    offsets = jnp.arange(length, dtype=jnp.int32)
    distance = (offsets[:, None] - offsets[None, :]).astype(jnp.float32)
    allowed = (offsets[:, None] >= offsets[None, :]) & (segments[:, None] == segments[None, :])
    decay_mask = jnp.where(allowed[None], jnp.exp(-head_decay[:, None, None] * jnp.maximum(distance, 0.0)[None]), 0.0)
    scores = jnp.einsum('ihd,jhd->hij', query_h.astype(jnp.float32), key_h.astype(jnp.float32), precision=lax.Precision.HIGHEST)
    weights = (scores * decay_mask).astype(jnp.bfloat16)
    within = jnp.einsum('hij,jhd->ihd', weights.astype(jnp.float32), value_h.astype(jnp.float32), precision=lax.Precision.HIGHEST)
    last_seg = segments[length - 1]
    fading = jnp.where((segments == last_seg)[:, None], jnp.exp(-head_decay[None, :] * (length - 1 - offsets).astype(jnp.float32)[:, None]), 0.0)
    weighted_keys = key_h.astype(jnp.float32) * fading[:, :, None]
    local_state = jnp.einsum('jhd,jhe->hde', weighted_keys, value_h.astype(jnp.float32), precision=lax.Precision.HIGHEST)
    carry_factor = jnp.where(last_seg == seg_before, jnp.exp(-head_decay * length), 0.0)
    reaching = jnp.where((segments == seg_before)[:, None], jnp.exp(-head_decay[None, :] * (offsets + 1).astype(jnp.float32)[:, None]), 0.0)
    return (within, local_state, carry_factor, reaching)

def reference(residual, query_rows, key_rows, value_rows, head_rates, doc_lengths, attn_gain, out_weight, moe_gain, expert_ids, expert_weights, gate_weight, up_weight, down_weight):
    blocks_all = TOKENS // TOK_DEV
    query_b = query_rows.reshape(blocks_all, TOK_DEV, H, HD)
    key_b = key_rows.reshape(blocks_all, TOK_DEV, H, HD)
    value_b = value_rows.reshape(blocks_all, TOK_DEV, H, HD)

    def attend(state_now, inputs):
        block_index, query_h, key_h, value_h = inputs
        first_pos = block_index * TOK_DEV
        positions = first_pos + jnp.arange(TOK_DEV, dtype=jnp.int32)
        segments = segment_of(doc_lengths, positions)
        seg_before = segment_of(doc_lengths, jnp.reshape(first_pos - 1, (1,)).astype(jnp.int32))[0]
        within, local_state, carry_factor, reaching = local_attention(query_h, key_h, value_h, head_rates, segments, seg_before)
        inter = jnp.einsum('ihd,hde->ihe', query_h.astype(jnp.float32), state_now, precision=lax.Precision.HIGHEST) * reaching[:, :, None]
        state_next = carry_factor[:, None, None] * state_now + local_state
        return (state_next, within + inter)
    _, mixed_out = lax.scan(attend, jnp.zeros((H, HD, HD), jnp.float32), (jnp.arange(blocks_all, dtype=jnp.int32), query_b, key_b, value_b))
    mixed_out = mixed_out.reshape(TOKENS, H, HD)
    scaled = mixed_out * lax.rsqrt(lax.optimization_barrier(jnp.mean(mixed_out * mixed_out, axis=-1, keepdims=True)) + 1e-06)
    heads_out = (scaled.reshape(TOKENS, H * HD) * attn_gain).astype(jnp.bfloat16)
    group_cols = H * HD // N_TP

    def add_heads(running, group_index):
        piece_in = lax.dynamic_slice_in_dim(heads_out, group_index * group_cols, group_cols, 1)
        piece_weight = lax.dynamic_slice_in_dim(out_weight, group_index * group_cols, group_cols, 0)
        term = lax.optimization_barrier(jnp.dot(piece_in, piece_weight, preferred_element_type=jnp.float32).astype(jnp.bfloat16))
        return (running + term.astype(jnp.float32), None)
    attn_out, _ = lax.scan(add_heads, jnp.zeros((TOKENS, D), jnp.float32), jnp.arange(N_TP, dtype=jnp.int32))
    hidden_state = (residual.astype(jnp.float32) + attn_out).astype(jnp.bfloat16)
    widened = hidden_state.astype(jnp.float32)
    moe_input = (widened * lax.rsqrt(lax.optimization_barrier(jnp.mean(widened * widened, axis=1, keepdims=True)) + 1e-05) * moe_gain).astype(jnp.bfloat16)
    ids_blocks = expert_ids.reshape(N_CTX, TOK_DEV * TOP)
    onehot = (ids_blocks[:, :, None] == jnp.arange(EXPERTS, dtype=jnp.int32)[None, None, :]).astype(jnp.int32)
    slot_ranks = lax.optimization_barrier(jnp.sum((jnp.cumsum(onehot, axis=1) - onehot) * onehot, axis=2))
    slot_index = (jnp.arange(N_CTX, dtype=jnp.int32)[:, None] * CAP + slot_ranks).reshape(-1).astype(jnp.int32)
    flat_ids = ids_blocks.reshape(-1).astype(jnp.int32)
    token_index = (jnp.arange(TOKENS * TOP, dtype=jnp.int32) // TOP).astype(jnp.int32)
    rows_in = jnp.zeros((EXPERTS, N_CTX * CAP, D), jnp.bfloat16).at[flat_ids, slot_index].set(moe_input[token_index])
    hidden_cols = FFW // N_TP

    def expert(inputs):
        slot_rows, gate_e, up_e, down_e = inputs
        gate_pre = jnp.dot(slot_rows, gate_e, preferred_element_type=jnp.float32)
        up_pre = jnp.dot(slot_rows, up_e, preferred_element_type=jnp.float32)
        activated = (jax.nn.silu(gate_pre) * up_pre).astype(jnp.bfloat16)

        def add_hidden(running, group_index):
            piece_in = lax.dynamic_slice_in_dim(activated, group_index * hidden_cols, hidden_cols, 1)
            piece_weight = lax.dynamic_slice_in_dim(down_e, group_index * hidden_cols, hidden_cols, 0)
            term = lax.optimization_barrier(jnp.dot(piece_in, piece_weight, preferred_element_type=jnp.float32).astype(jnp.bfloat16))
            return (running + term.astype(jnp.float32), None)
        summed, _ = lax.scan(add_hidden, jnp.zeros((slot_rows.shape[0], D), jnp.float32), jnp.arange(N_TP, dtype=jnp.int32))
        return summed.astype(jnp.bfloat16)
    expert_out = lax.map(expert, (rows_in, gate_weight, up_weight, down_weight))
    picked = expert_out[flat_ids, slot_index].reshape(TOKENS, TOP, D).astype(jnp.float32)
    mixture = lax.optimization_barrier(jnp.sum(picked * expert_weights[:, :, None], axis=1))
    return (widened + mixture).astype(jnp.bfloat16)
```

```python
import jax
import jax.numpy as jnp
from jax import lax
from jax.experimental import pallas as pl
from jax.experimental.pallas import tpu as pltpu
from jax.sharding import Mesh
from jax.sharding import PartitionSpec as P

D = 6144
HD = 128
CAP = 24
BLOCKS = 16
ROWS = 128
FEAT = 384
HID = 288
SLOTS = BLOCKS * CAP
CTX = ("ctx_0", "ctx_1")
TP = ("tp_0", "tp_1")
AXES = CTX + TP
ORDER = (4, 3, 5, 2, 6, 1, 7, 0)
BF = jnp.bfloat16
F32 = jnp.float32


def remote(src, dst, send_sem, recv_sem, to):
    return pltpu.make_async_remote_copy(
        src_ref=src,
        dst_ref=dst,
        send_sem=send_sem,
        recv_sem=recv_sem,
        device_id=to,
        device_id_type=pl.DeviceIdType.MESH,
    )


def place():
    return tuple(lax.axis_index(a) for a in AXES)


def partner_of(y, x, z, k):
    low = 2 * (z % 2) + k
    return low, (y, low, 2 * (z // 2) + x // 2, x % 2)


def greet(y, x, z, k):
    sem = pltpu.get_barrier_semaphore()
    for i in range(1, 16):
        c = (4 * y + x + i) % 16
        pl.semaphore_signal(
            sem, inc=1, device_id=(c // 4, c % 4, z, k), device_id_type=pl.DeviceIdType.MESH
        )
    for i in range(1, 16):
        t = (2 * z + k + i) % 16
        pl.semaphore_signal(
            sem, inc=1, device_id=(y, x, t // 2, t % 2), device_id_type=pl.DeviceIdType.MESH
        )
    low, partner = partner_of(y, x, z, k)

    @pl.when(low != x)
    def _():
        pl.semaphore_signal(sem, inc=1, device_id=partner, device_id_type=pl.DeviceIdType.MESH)

    pl.semaphore_wait(sem, 30 + ((low - x + 4) % 4 + 3) // 4)


class RingGather:
    def __init__(self, buf, ssem, rsem, me, device_at, half):
        self.buf, self.ssem, self.rsem = buf, ssem, rsem
        self.me, self.at, self.half = me, device_at, half

    def piece(self, member, part):
        return self.buf.at[member % 4, pl.ds(part * self.half, self.half)]

    def first(self, part, own):
        out = []
        for d, step in enumerate((1, -1)):
            cp = remote(
                own.at[pl.ds(part * self.half, self.half)],
                self.piece(self.me, part),
                self.ssem.at[d, part],
                self.rsem.at[d, part],
                self.at((self.me + step) % 4),
            )
            cp.start()
            out.append(cp)
        return out

    def arrived(self, d, part):
        step = (1, -1)[d]
        ref = self.piece(self.me + 4 - step, part)
        remote(
            ref, ref, self.ssem.at[d, part], self.rsem.at[d, part], self.at((self.me + step) % 4)
        ).wait_recv()

    def forward(self, d):
        step = (1, -1)[d]
        ref = self.piece(self.me + 4 - step, d)
        cp = remote(
            ref, ref, self.ssem.at[d, 2], self.rsem.at[d, 2], self.at((self.me + step) % 4)
        )
        cp.start()
        return cp

    def forwarded(self, d):
        step = (1, -1)[d]
        ref = self.piece(self.me + 2, d)
        remote(
            ref, ref, self.ssem.at[d, 2], self.rsem.at[d, 2], self.at((self.me + step) % 4)
        ).wait_recv()


class RingSum:
    def __init__(self, spot, rows, own, out, got, tbuf, rbuf, xs, xr, ssem, rsem):
        self.y, self.x, self.z, self.k = spot
        self.half = rows // 2
        self.own, self.out, self.got = own, out, got
        self.tbuf, self.rbuf = tbuf, rbuf
        self.xs, self.xr, self.ssem, self.rsem = xs, xr, ssem, rsem
        self.sent = []

    def swap(self, i):
        d = ORDER[i]
        cp = remote(
            self.out.at[i],
            self.got.at[i],
            self.xs.at[i],
            self.xr.at[i],
            (self.y, self.x, self.z, 1 - self.k),
        )
        cp.start()
        self.sent.append(cp)

    def swapped(self, i):
        remote(
            self.out.at[i],
            self.got.at[i],
            self.xs.at[i],
            self.xr.at[i],
            (self.y, self.x, self.z, 1 - self.k),
        ).wait_recv()

    def local(self, i, part):
        rows = pl.ds(part * self.half, self.half)
        return self.own[i, rows, :].astype(F32) + self.got[i, rows, :].astype(F32)

    def hop(self, d, s, part):
        to = (self.z + (1, 7)[d]) % 8
        return remote(
            self.tbuf.at[d, s, part],
            self.rbuf.at[d, s, part],
            self.ssem.at[d, s, part],
            self.rsem.at[d, s, part],
            (self.y, self.x, to, self.k),
        )

    def send(self, d, s, part, value):
        self.tbuf[d, s, part] = value.astype(BF)
        cp = self.hop(d, s, part)
        cp.start()
        self.sent.append(cp)

    def run(self, produce):
        produce(0)
        self.swap(0)
        produce(1)
        self.swap(1)
        produce(2)
        self.swap(2)
        self.swapped(0)
        self.send(0, 0, 0, self.local(0, 0))
        self.send(1, 0, 1, self.local(0, 1))
        self.swapped(1)
        self.send(0, 1, 1, self.local(1, 1))
        self.swapped(2)
        self.send(1, 1, 0, self.local(2, 0))
        for i in range(3, 8):
            produce(i)
            self.swap(i)
        self.hop(0, 0, 0).wait_recv()
        self.send(0, 1, 0, self.local(1, 0) + self.rbuf[0, 0, 0].astype(F32))
        self.hop(1, 0, 1).wait_recv()
        self.send(1, 1, 1, self.local(2, 1) + self.rbuf[1, 0, 1].astype(F32))
        for s in (2, 3):
            self.swapped(2 * s - 1)
            self.swapped(2 * s)
            for j in range(2):
                for d in range(2):
                    part = (1 - j) if d == 0 else j
                    self.hop(d, s - 1, part).wait_recv()
                    self.send(
                        d,
                        s,
                        part,
                        self.local(2 * s - 1 + d, part) + self.rbuf[d, s - 1, part].astype(F32),
                    )
        self.swapped(7)

    def result(self, part):
        self.hop(0, 3, part).wait_recv()
        self.hop(1, 3, part).wait_recv()
        return (
            self.local(7, part)
            + self.rbuf[0, 3, part].astype(F32)
            + self.rbuf[1, 3, part].astype(F32)
        )

    def finish(self):
        for cp in self.sent:
            cp.wait_send()


def mixer(
    rates, docs, q, k_in, v, again, w, res, mgain, ids,
    h_out, ids_out, gain_out,
    wbuf, hbuf, state, arrived, onward, incoming, resbuf, within,
    own, out, got, tbuf, rbuf,
    wss, wrs, hss, hrs, a1s, a1r, a2s, a2r, gs, gr, ps, pr, xs, xr, ts, tr, loc,
):
    spot = y, x, z, k = place()
    me, t = 4 * y + x, 2 * z + k
    low, partner = partner_of(*spot)
    sent = []
    greet(*spot)

    weights = RingGather(wbuf, wss, wrs, y, lambda i: (i, x, z, k), 256)
    heads = RingGather(hbuf, hss, hrs, x, lambda i: (y, i, z, k), 64)
    own_w = pltpu.make_async_copy(w, wbuf.at[y], loc.at[0])
    own_w.start()
    sent += weights.first(0, w)

    handed = [
        remote(res, resbuf, ps.at[0], pr.at[0], partner),
        remote(ids, ids_out, ps.at[1], pr.at[1], partner),
    ]
    kept = [
        pltpu.make_async_copy(res, resbuf, loc.at[1]),
        pltpu.make_async_copy(ids, ids_out, loc.at[2]),
    ]

    @pl.when(low != x)
    def _():
        for cp in handed:
            cp.start()

    @pl.when(low == x)
    def _():
        for cp in kept:
            cp.start()

    own_gain = pltpu.make_async_copy(mgain, gain_out.at[t], loc.at[3])
    own_gain.start()
    for i in range(1, 16):
        to = (t + i) % 16
        cp = remote(mgain, gain_out.at[t], gs.at[i], gr.at[i], (y, x, to // 2, to % 2))
        cp.start()
        sent.append(cp)

    start1 = docs[0]
    start2 = start1 + docs[1]
    start3 = start2 + docs[2]

    def seg(p):
        def past(s):
            return jnp.where(p >= s, 1, 0)

        base = jnp.where(p >= 0, 0, -1)
        return base + past(start1) + past(start2) + past(start3)

    first = me * ROWS
    last_seg = seg(first + ROWS - 1)
    before = seg(first - 1)
    row = lax.broadcasted_iota(jnp.int32, (ROWS, HD), 0)
    col = lax.broadcasted_iota(jnp.int32, (ROWS, HD), 1)
    seg_row, seg_col = seg(first + row), seg(first + col)
    rowf = row.astype(F32)
    at_end = jnp.where(seg_row == last_seg, 1.0, 0.0)
    for h in range(4):
        rate = rates[4 * t + h]
        cols = slice(h * HD, (h + 1) * HD)
        fading = at_end * jnp.exp(-rate * (ROWS - 1.0 - rowf))
        faded = (k_in[:, cols].astype(F32) * fading).astype(BF)
        state[h * HD : (h + 1) * HD, :] = lax.dot_general(
            faded, v[:, cols], (((0,), (0,)), ((), ())), preferred_element_type=F32
        ).astype(BF)

    own_state = pltpu.make_async_copy(
        state.at[pl.ds(pl.multiple_of(me * 32, 32), 32)], arrived.at[me], loc.at[4]
    )
    own_state.start()
    for i in range(1, 16):
        to = (me + i) % 16
        cp = remote(
            state.at[pl.ds(pl.multiple_of(to * 32, 32), 32)],
            arrived.at[me],
            a1s.at[i],
            a1r.at[i],
            (to // 4, to % 4, z, k),
        )
        cp.start()
        sent.append(cp)
    sent += weights.first(1, w)

    allowed = jnp.where((row >= col) & (seg_row == seg_col), 1.0, 0.0)
    gap = jnp.maximum(row - col, 0).astype(F32)
    for h in range(4):
        rate = rates[4 * t + h]
        cols = slice(h * HD, (h + 1) * HD)
        scores = lax.dot_general(
            q[:, cols], k_in[:, cols], (((1,), (1,)), ((), ())), preferred_element_type=F32
        )
        mixed = (scores * (allowed * jnp.exp(-rate * gap))).astype(BF)
        within[:, cols] = jnp.dot(mixed, v[:, cols], preferred_element_type=F32)

    own_state.wait()
    for i in range(1, 16):
        ref = arrived.at[(me - i + 16) % 16]
        remote(ref, ref, a1s.at[i], a1r.at[i], (y, x, z, 1 - k)).wait_recv()
    decay = jnp.exp(jnp.zeros((32, HD), F32) - rates[4 * t + y] * ROWS)
    running = jnp.zeros((32, HD), F32)
    for b in range(BLOCKS):
        onward[b] = running.astype(BF)
        same = seg(jnp.int32(b * ROWS + ROWS - 1)) == seg(jnp.int32(b * ROWS - 1))
        running = running * (decay * jnp.where(same, 1.0, 0.0)) + arrived[b].astype(F32)
    own_onward = pltpu.make_async_copy(onward.at[me], incoming.at[me], loc.at[5])
    own_onward.start()
    for i in range(1, 16):
        to = (me + i) % 16
        cp = remote(
            onward.at[to], incoming.at[me], a2s.at[i], a2r.at[i], (to // 4, to % 4, z, k)
        )
        cp.start()
        sent.append(cp)
    for d in range(2):
        for part in range(2):
            weights.arrived(d, part)
    for d in range(2):
        sent.append(weights.forward(d))
    own_onward.wait()
    for i in range(1, 16):
        ref = incoming.at[(me - i + 16) % 16]
        remote(ref, ref, a2s.at[i], a2r.at[i], (y, x, z, 1 - k)).wait_recv()

    reached = jnp.where(seg_row == before, 1.0, 0.0)
    for h in range(4):
        rate = rates[4 * t + h]
        cols = slice(h * HD, (h + 1) * HD)
        inc = incoming[4 * h : 4 * h + 4].reshape(HD, HD)
        inter = jnp.dot(q[:, cols], inc, preferred_element_type=F32)
        both = within[:, cols] + inter * (reached * jnp.exp(-rate * (rowf + 1.0)))
        scale = lax.rsqrt(jnp.mean(both * both, axis=1, keepdims=True) + 1e-06)
        within[:, cols] = both * scale * again[:, cols]
    hbuf[x] = within[...].astype(BF)
    sent += heads.first(0, hbuf.at[x])
    sent += heads.first(1, hbuf.at[x])
    heads.arrived(0, 0)
    sent.append(heads.forward(0))
    heads.arrived(1, 1)
    sent.append(heads.forward(1))
    heads.arrived(0, 1)
    heads.arrived(1, 0)
    own_w.wait()
    for d in range(2):
        weights.forwarded(d)
    for d in range(2):
        heads.forwarded(d)

    total = RingSum(spot, ROWS, own, out, got, tbuf, rbuf, xs, xr, ts, tr)

    def produce(i):
        chunk = (z + ORDER[i]) % 8
        pair = 2 * (chunk % 2)
        wide = wbuf[chunk // 2]
        out[i] = jnp.dot(hbuf[pair + 1 - k], wide, preferred_element_type=F32).astype(BF)
        own[i] = jnp.dot(hbuf[pair + k], wide, preferred_element_type=F32).astype(BF)

    total.run(produce)

    @pl.when(low != x)
    def _():
        for cp in handed:
            cp.wait()

    @pl.when(low == x)
    def _():
        for cp in kept:
            cp.wait()

    for part in range(2):
        rows = slice(part * 64, part * 64 + 64)
        h_out[rows, :] = (resbuf[rows, :].astype(F32) + total.result(part)).astype(BF)
    own_gain.wait()
    for i in range(1, 16):
        ref = gain_out.at[(t - i + 16) % 16]
        remote(ref, ref, gs.at[i], gr.at[i], (y, x, z, 1 - k)).wait_recv()
    for cp in sent:
        cp.wait_send()
    total.finish()


def slot_hits(ids):
    expert = lax.broadcasted_iota(jnp.int32, (BLOCKS, CAP, ROWS), 0).reshape(SLOTS, ROWS)
    place_in = lax.broadcasted_iota(jnp.int32, (BLOCKS, CAP, ROWS), 1).reshape(SLOTS, ROWS)
    hit0 = expert == ids[0:1, :]
    hit1 = expert == ids[1:2, :]
    named = jnp.where(hit0 | hit1, 1.0, 0.0)
    earlier = lax.broadcasted_iota(jnp.int32, (ROWS, ROWS), 0)
    later = lax.broadcasted_iota(jnp.int32, (ROWS, ROWS), 1)
    rank = jnp.dot(
        named.astype(BF),
        jnp.where(earlier < later, 1.0, 0.0).astype(BF),
        preferred_element_type=F32,
    )
    here = rank == place_in.astype(F32)
    return hit0 & here, hit1 & here


def experts(
    h, ids_p, gains, ids_n, wts, wg_hbm, wu_hbm, wd_hbm,
    o_ref,
    wgu, wd, ds, xb, lhs, acc, squares, act, hn, qs, rb,
    own, out, got, tbuf, rbuf,
    dss, dsr, fs, fr, cs, cr, qss, qsr, ps, pr, xs, xr, ts, tr, loc,
):
    spot = y, x, z, k = place()
    me, t = 4 * y + x, 2 * z + k
    low, partner = partner_of(*spot)
    peer = (y, x, z, 1 - k)
    sent = []
    loads = [
        pltpu.make_async_copy(wg_hbm, wgu.at[pl.ds(0, HID)], loc.at[0]),
        pltpu.make_async_copy(wu_hbm, wgu.at[pl.ds(FEAT, HID)], loc.at[1]),
        pltpu.make_async_copy(wd_hbm, wd, loc.at[2]),
    ]
    for cp in loads:
        cp.start()

    hit0, hit1 = slot_hits(ids_p)
    pick = jnp.where(hit0 | hit1, 1.0, 0.0).astype(BF)
    picked = jnp.dot(pick, h[...], preferred_element_type=F32)
    ds[...] = picked.reshape(BLOCKS, CAP, FEAT).astype(BF)
    greet(*spot)

    mine = 4 * x + y
    own_rows = pltpu.make_async_copy(ds.at[me], xb.at[t, mine], loc.at[3])
    own_rows.start()
    for i in range(1, 16):
        to = (me + i) % 16
        cp = remote(ds.at[to], xb.at[t, mine], dss.at[i], dsr.at[i], (to // 4, to % 4, z, k))
        cp.start()
        sent.append(cp)
    handed = remote(h, hn, ps.at[0], pr.at[0], partner)
    kept = pltpu.make_async_copy(h, hn, loc.at[4])

    @pl.when(low != x)
    def _():
        handed.start()

    @pl.when(low == x)
    def _():
        kept.start()

    own_rows.wait()
    for i in range(1, 16):
        c = (me - i + 16) % 16
        ref = xb.at[t, 4 * (c % 4) + c // 4]
        remote(ref, ref, dss.at[i], dsr.at[i], peer).wait_recv()

    def half(zz, kk, part):
        return xb.at[2 * ((zz + 8) % 8) + kk, pl.ds(part * 8, 8)]

    def ring(d, s, part, ref):
        to = (z + (1, 7)[d]) % 8
        return remote(ref, ref, fs.at[d, s, part], fr.at[d, s, part], (y, x, to, k))

    def over(slot, part, ref):
        return remote(ref, ref, cs.at[slot, part], cr.at[slot, part], peer)

    def push(cp):
        cp.start()
        sent.append(cp)

    def crossed(slot, dist):
        for part in range(2):
            over(slot, part, half(z + dist, 1 - k, part)).wait_recv()

    for part in range(2):
        ref = half(z, k, part)
        push(ring(0, 0, part, ref))
        push(ring(1, 0, part, ref))
        push(over(0, part, ref))

    wgu[HID:FEAT, :] = jnp.zeros((FEAT - HID, D), BF)
    acc[...] = jnp.zeros_like(acc)
    squares[...] = jnp.zeros_like(squares)

    def multiply(group):
        for xx in range(4):
            gain = gains[4 * group + xx]
            for xp in range(4):
                rows = slice(96 * xp, 96 * xp + 96)
                piece = xb[4 * group + xp, 4 * xx : 4 * xx + 4].astype(F32).reshape(96, FEAT)
                sq = piece * piece
                squares[rows, :] += sq[:, 0:128] + sq[:, 128:256] + sq[:, 256:384]
                lhs[rows, xx * FEAT : (xx + 1) * FEAT] = (piece * gain).astype(BF)
        cols = pl.ds(pl.multiple_of(group * 1536, 1536), 1536)
        acc[...] += lax.dot_general(
            lhs[...], wgu[:, cols], (((1,), (1,)), ((), ())), preferred_element_type=F32
        )

    side = jnp.where(z % 2 == 0, 3, 1)
    pair = z // 2
    for s in (1, 2, 3):
        for part in range(2):
            for d in range(2):
                behind = -s if d == 0 else s
                ref = half(z + behind, k, part)
                ring(d, s - 1, part, ref).wait_recv()
                if s < 3 or part == d:
                    push(ring(d, s, part, ref))
                push(over(2 * s - 1 + d, part, ref))
        if s == 1:
            crossed(0, 0)
            crossed(1, -1)
            crossed(2, 1)
            loads[0].wait()
            loads[1].wait()
            multiply(pair)
        elif s == 2:
            crossed(3, -2)
            crossed(4, 2)
            multiply((pair + side) % 4)
        else:
            crossed(5, -3)
            crossed(6, 3)
            multiply((pair + 4 - side) % 4)
    for d in range(2):
        ref = half(z + 4, k, d)
        ring(d, 3, d, ref).wait_recv()
        push(over(7, d, ref))
    crossed(7, 4)
    multiply((pair + 2) % 4)

    total_sq = jnp.sum(squares[...], axis=1, keepdims=True)
    scale = lax.rsqrt(total_sq / D + 1e-05)
    gate = acc[:, :HID] * scale
    lifted = acc[:, FEAT:] * scale
    act[...] = (gate / (1.0 + jnp.exp(-gate)) * lifted).astype(BF)
    loads[2].wait()

    total = RingSum(spot, SLOTS, own, out, got, tbuf, rbuf, xs, xr, ts, tr)

    def produce(i):
        chunk = (z + ORDER[i]) % 8

        def tile(lane):
            cols = pl.ds(pl.multiple_of((2 * chunk + lane) * FEAT, FEAT), FEAT)
            return jnp.dot(act[...], wd[:, cols], preferred_element_type=F32).astype(BF)

        out[i] = tile(1 - k)
        own[i] = tile(k)

    total.run(produce)
    for part in range(2):
        qs[part * 8 : part * 8 + 8] = total.result(part).reshape(8, CAP, FEAT).astype(BF)
    own_back = pltpu.make_async_copy(qs.at[mine], rb.at[me], loc.at[5])
    own_back.start()
    for i in range(1, 16):
        to = (me + i) % 16
        push(
            remote(
                qs.at[4 * (to % 4) + to // 4],
                rb.at[me],
                qss.at[i],
                qsr.at[i],
                (to // 4, to % 4, z, k),
            )
        )
    hit0, hit1 = slot_hits(ids_n)
    part_of = jnp.where(hit0, wts[0:1, :], 0.0) + jnp.where(hit1, wts[1:2, :], 0.0)
    coarse = part_of.astype(BF)
    fine = (part_of - coarse.astype(F32)).astype(BF)

    @pl.when(low != x)
    def _():
        handed.wait()

    @pl.when(low == x)
    def _():
        kept.wait()

    own_back.wait()
    for i in range(1, 16):
        ref = rb.at[(me - i + 16) % 16]
        remote(ref, ref, qss.at[i], qsr.at[i], peer).wait_recv()
    back = rb[...].astype(F32).reshape(SLOTS, FEAT).astype(BF)
    dims = (((0,), (0,)), ((), ()))
    mixture = lax.dot_general(coarse, back, dims, preferred_element_type=F32)
    mixture += lax.dot_general(fine, back, dims, preferred_element_type=F32)
    o_ref[...] = (hn[...].astype(F32) + mixture).astype(BF)
    for cp in sent:
        cp.wait_send()
    total.finish()


def dma(*shape):
    return pltpu.SemaphoreType.DMA(shape)


def ring_scratch(rows):
    half = rows // 2
    return [
        pltpu.VMEM((8, rows, FEAT), BF),
        pltpu.VMEM((8, rows, FEAT), BF),
        pltpu.VMEM((8, rows, FEAT), BF),
        pltpu.VMEM((2, 4, 2, half, FEAT), BF),
        pltpu.VMEM((2, 4, 2, half, FEAT), BF),
    ]


VM = pl.BlockSpec(memory_space=pltpu.VMEM)
SM = pl.BlockSpec(memory_space=pltpu.SMEM)
ANY = pl.BlockSpec(memory_space=pl.ANY)


def shards(
    residual, query_rows, key_rows, value_rows, head_rates, doc_lengths, attn_gain, out_weight,
    moe_gain, expert_ids, expert_weights, gate_weight, up_weight, down_weight,
):
    ids = expert_ids.T
    h, ids_p, gains = pl.pallas_call(
        mixer,
        out_shape=(
            jax.ShapeDtypeStruct((ROWS, FEAT), BF),
            jax.ShapeDtypeStruct((2, ROWS), jnp.int32),
            jax.ShapeDtypeStruct((16, 1, FEAT), F32),
        ),
        in_specs=[SM, SM] + [VM] * 8,
        out_specs=(VM, VM, VM),
        scratch_shapes=[
            pltpu.VMEM((4, 512, FEAT), BF),
            pltpu.VMEM((4, ROWS, 512), BF),
            pltpu.VMEM((512, HD), BF),
            pltpu.VMEM((16, 32, HD), BF),
            pltpu.VMEM((16, 32, HD), BF),
            pltpu.VMEM((16, 32, HD), BF),
            pltpu.VMEM((ROWS, FEAT), BF),
            pltpu.VMEM((ROWS, 512), F32),
            *ring_scratch(ROWS),
            dma(2, 3), dma(2, 3), dma(2, 3), dma(2, 3),
            dma(16), dma(16), dma(16), dma(16), dma(16), dma(16),
            dma(2), dma(2), dma(8), dma(8), dma(2, 4, 2), dma(2, 4, 2), dma(6),
        ],
        compiler_params=pltpu.CompilerParams(
            collective_id=0, has_side_effects=True, vmem_limit_bytes=40 << 20
        ),
        name="mixer",
    )(
        head_rates, doc_lengths, query_rows, key_rows, value_rows, attn_gain.reshape(1, -1),
        out_weight, residual, moe_gain.reshape(1, -1), ids,
    )
    return pl.pallas_call(
        experts,
        out_shape=jax.ShapeDtypeStruct((ROWS, FEAT), BF),
        in_specs=[VM] * 5 + [ANY] * 3,
        out_specs=VM,
        scratch_shapes=[
            pltpu.VMEM((FEAT + HID, D), BF),
            pltpu.VMEM((HID, D), BF),
            pltpu.VMEM((BLOCKS, CAP, FEAT), BF),
            pltpu.VMEM((16, BLOCKS, CAP, FEAT), BF),
            pltpu.VMEM((SLOTS, 4 * FEAT), BF),
            pltpu.VMEM((SLOTS, FEAT + HID), F32),
            pltpu.VMEM((SLOTS, 128), F32),
            pltpu.VMEM((SLOTS, HID), BF),
            pltpu.VMEM((ROWS, FEAT), BF),
            pltpu.VMEM((BLOCKS, CAP, FEAT), BF),
            pltpu.VMEM((BLOCKS, CAP, FEAT), BF),
            *ring_scratch(SLOTS),
            dma(16), dma(16), dma(2, 4, 2), dma(2, 4, 2), dma(8, 2), dma(8, 2),
            dma(16), dma(16), dma(1), dma(1), dma(8), dma(8), dma(2, 4, 2), dma(2, 4, 2), dma(6),
        ],
        compiler_params=pltpu.CompilerParams(
            collective_id=1, has_side_effects=True, vmem_limit_bytes=60 << 20
        ),
        name="experts",
    )(
        h, ids_p, gains, ids, expert_weights.T,
        gate_weight[0].T, up_weight[0].T, down_weight[0],
    )


def solution(mesh):
    finer = Mesh(mesh.devices.reshape(4, 4, 8, 2), AXES)
    placed = (
        P(CTX, TP), P(CTX, TP), P(CTX, TP), P(CTX, TP), P(), P(), P(TP), P(TP, CTX), P(TP),
        P(CTX, None), P(CTX, None), P(CTX, None, TP), P(CTX, None, TP), P(CTX, TP, None),
    )
    return jax.shard_map(shards, mesh=finer, in_specs=placed, out_specs=P(CTX, TP), check_vma=False)
```

```python
import jax
import jax.numpy as jnp
from jax import lax
from jax.experimental import pallas as pl
from jax.experimental.pallas import tpu as pltpu
from jax.sharding import Mesh
from jax.sharding import PartitionSpec as P

D = 6144
HD = 128
CAP = 24
BLOCKS = 16
ROWS = 128
FEAT = 384
HID = 288
SLOTS = BLOCKS * CAP
CTX = ("ctx_0", "ctx_1")
TP = ("tp_0", "tp_1")
AXES = CTX + TP
ORDER = (4, 3, 5, 2, 6, 1, 7, 0)
BF = jnp.bfloat16
F32 = jnp.float32


def remote(src, dst, send_sem, recv_sem, to):
    return pltpu.make_async_remote_copy(
        src_ref=src,
        dst_ref=dst,
        send_sem=send_sem,
        recv_sem=recv_sem,
        device_id=to,
        device_id_type=pl.DeviceIdType.MESH,
    )


def place():
    return tuple(lax.axis_index(a) for a in AXES)


def partner_of(y, x, z, k):
    low = 2 * (z % 2) + k
    return low, (y, low, 2 * (z // 2) + x // 2, x % 2)


def greet(y, x, z, k):
    sem = pltpu.get_barrier_semaphore()
    for i in range(1, 16):
        c = (4 * y + x + i) % 16
        pl.semaphore_signal(
            sem, inc=1, device_id=(c // 4, c % 4, z, k), device_id_type=pl.DeviceIdType.MESH
        )
    for i in range(1, 16):
        t = (2 * z + k + i) % 16
        pl.semaphore_signal(
            sem, inc=1, device_id=(y, x, t // 2, t % 2), device_id_type=pl.DeviceIdType.MESH
        )
    low, partner = partner_of(y, x, z, k)

    @pl.when(low != x)
    def _():
        pl.semaphore_signal(sem, inc=1, device_id=partner, device_id_type=pl.DeviceIdType.MESH)

    pl.semaphore_wait(sem, 30 + ((low - x + 4) % 4 + 3) // 4)


class RingGather:
    def __init__(self, buf, ssem, rsem, me, device_at, half):
        self.buf, self.ssem, self.rsem = buf, ssem, rsem
        self.me, self.at, self.half = me, device_at, half

    def piece(self, member, part):
        return self.buf.at[member % 4, pl.ds(part * self.half, self.half)]

    def first(self, part, own):
        out = []
        for d, step in enumerate((1, -1)):
            cp = remote(
                own.at[pl.ds(part * self.half, self.half)],
                self.piece(self.me, part),
                self.ssem.at[d, part],
                self.rsem.at[d, part],
                self.at((self.me + step) % 4),
            )
            cp.start()
            out.append(cp)
        return out

    def arrived(self, d, part):
        step = (1, -1)[d]
        ref = self.piece(self.me + 4 - step, part)
        remote(
            ref, ref, self.ssem.at[d, part], self.rsem.at[d, part], self.at((self.me + step) % 4)
        ).wait_recv()

    def forward(self, d):
        step = (1, -1)[d]
        ref = self.piece(self.me + 4 - step, d)
        cp = remote(
            ref, ref, self.ssem.at[d, 2], self.rsem.at[d, 2], self.at((self.me + step) % 4)
        )
        cp.start()
        return cp

    def forwarded(self, d):
        step = (1, -1)[d]
        ref = self.piece(self.me + 2, d)
        remote(
            ref, ref, self.ssem.at[d, 2], self.rsem.at[d, 2], self.at((self.me + step) % 4)
        ).wait_recv()


class RingSum:
    def __init__(self, spot, rows, own, out, got, tbuf, rbuf, xs, xr, ssem, rsem):
        self.y, self.x, self.z, self.k = spot
        self.half = rows // 2
        self.own, self.out, self.got = own, out, got
        self.tbuf, self.rbuf = tbuf, rbuf
        self.xs, self.xr, self.ssem, self.rsem = xs, xr, ssem, rsem
        self.sent = []

    def swap(self, i):
        d = ORDER[i]
        cp = remote(
            self.out.at[i],
            self.got.at[i],
            self.xs.at[i],
            self.xr.at[i],
            (self.y, self.x, self.z, 1 - self.k),
        )
        cp.start()
        self.sent.append(cp)

    def swapped(self, i):
        remote(
            self.out.at[i],
            self.got.at[i],
            self.xs.at[i],
            self.xr.at[i],
            (self.y, self.x, self.z, 1 - self.k),
        ).wait_recv()

    def local(self, i, part):
        rows = pl.ds(part * self.half, self.half)
        return self.own[i, rows, :].astype(F32) + self.got[i, rows, :].astype(F32)

    def hop(self, d, s, part):
        to = (self.z + (1, 7)[d]) % 8
        return remote(
            self.tbuf.at[d, s, part],
            self.rbuf.at[d, s, part],
            self.ssem.at[d, s, part],
            self.rsem.at[d, s, part],
            (self.y, self.x, to, self.k),
        )

    def send(self, d, s, part, value):
        self.tbuf[d, s, part] = value.astype(BF)
        cp = self.hop(d, s, part)
        cp.start()
        self.sent.append(cp)

    def run(self, produce):
        produce(0)
        self.swap(0)
        produce(1)
        self.swap(1)
        produce(2)
        self.swap(2)
        self.swapped(0)
        self.send(0, 0, 0, self.local(0, 0))
        self.send(1, 0, 1, self.local(0, 1))
        self.swapped(1)
        self.send(0, 1, 1, self.local(1, 1))
        self.swapped(2)
        self.send(1, 1, 0, self.local(2, 0))
        for i in range(3, 8):
            produce(i)
            self.swap(i)
        self.hop(0, 0, 0).wait_recv()
        self.send(0, 1, 0, self.local(1, 0) + self.rbuf[0, 0, 0].astype(F32))
        self.hop(1, 0, 1).wait_recv()
        self.send(1, 1, 1, self.local(2, 1) + self.rbuf[1, 0, 1].astype(F32))
        for s in (2, 3):
            self.swapped(2 * s - 1)
            self.swapped(2 * s)
            for j in range(2):
                for d in range(2):
                    part = (1 - j) if d == 0 else j
                    self.hop(d, s - 1, part).wait_recv()
                    self.send(
                        d,
                        s,
                        part,
                        self.local(2 * s - 1 + d, part) + self.rbuf[d, s - 1, part].astype(F32),
                    )
        self.swapped(7)

    def result(self, part):
        self.hop(0, 3, part).wait_recv()
        self.hop(1, 3, part).wait_recv()
        return (
            self.local(7, part)
            + self.rbuf[0, 3, part].astype(F32)
            + self.rbuf[1, 3, part].astype(F32)
        )


def mixer(
    rates_hbm, docs_hbm, q_hbm, k_hbm, v_hbm, again_hbm, w, res, mgain, ids,
    rates, docs, q, k_in, v, again,
    h_out, ids_all, gain_out,
    wbuf, hbuf, state, arrived, onward, incoming, resbuf, within,
    own, out, got, tbuf, rbuf,
    wss, wrs, hss, hrs, a1s, a1r, a2s, a2r, gs, gr, ps, pr, ids_s, ids_r, xs, xr, ts, tr, loc, start_weights,
):
    spot = y, x, z, k = place()
    me, t = 4 * y + x, 2 * z + k
    low, partner = partner_of(*spot)
    sent = []
    loads = [
        pltpu.make_async_copy(a, b, loc.at[6 + i])
        for i, (a, b) in enumerate(
            (
                (k_hbm, k_in), (v_hbm, v), (rates_hbm, rates), (docs_hbm, docs), (q_hbm, q),
                (again_hbm, again),
            )
        )
    ]
    for cp in loads:
        cp.start()
    greet(*spot)

    weights = RingGather(wbuf, wss, wrs, y, lambda i: (i, x, z, k), 256)
    heads = RingGather(hbuf, hss, hrs, x, lambda i: (y, i, z, k), 64)
    own_w = pltpu.make_async_copy(w, wbuf.at[y], loc.at[0])
    own_w.start()
    sent += weights.first(0, w)

    handed = remote(res, resbuf, ps.at[0], pr.at[0], partner)
    kept = pltpu.make_async_copy(res, resbuf, loc.at[1])

    @pl.when(low != x)
    def _():
        handed.start()

    @pl.when(low == x)
    def _():
        kept.start()

    own_ids = pltpu.make_async_copy(ids, ids_all.at[x], loc.at[2])
    own_ids.start()
    for i in range(1, 4):
        cp = remote(ids, ids_all.at[x], ids_s.at[i], ids_r.at[i], (y, (x + i) % 4, z, k))
        cp.start()
        sent.append(cp)

    own_gain = pltpu.make_async_copy(mgain, gain_out.at[t, 0], loc.at[3])
    own_gain.start()
    for i in range(1, 16):
        to = (t + i) % 16
        cp = remote(mgain, gain_out.at[t, 0], gs.at[i], gr.at[i], (y, x, to // 2, to % 2))
        cp.start()
        sent.append(cp)

    start_weights()
    for cp in loads[:4]:
        cp.wait()
    start1 = docs[0]
    start2 = start1 + docs[1]
    start3 = start2 + docs[2]

    def seg(p):
        def past(s):
            return jnp.where(p >= s, 1, 0)

        base = jnp.where(p >= 0, 0, -1)
        return base + past(start1) + past(start2) + past(start3)

    first = me * ROWS
    last_seg = seg(first + ROWS - 1)
    before = seg(first - 1)
    row = lax.broadcasted_iota(jnp.int32, (ROWS, HD), 0)
    col = lax.broadcasted_iota(jnp.int32, (ROWS, HD), 1)
    seg_row, seg_col = seg(first + row), seg(first + col)
    rowf = row.astype(F32)
    at_end = jnp.where(seg_row == last_seg, 1.0, 0.0)
    for h in range(4):
        rate = rates[4 * t + h]
        cols = slice(h * HD, (h + 1) * HD)
        fading = at_end * jnp.exp(-rate * (ROWS - 1.0 - rowf))
        faded = (k_in[:, cols].astype(F32) * fading).astype(BF)
        state[h * HD : (h + 1) * HD, :] = lax.dot_general(
            faded, v[:, cols], (((0,), (0,)), ((), ())), preferred_element_type=F32
        ).astype(BF)

    own_state = pltpu.make_async_copy(
        state.at[pl.ds(pl.multiple_of(me * 32, 32), 32)], arrived.at[me], loc.at[4]
    )
    own_state.start()
    for i in range(1, 16):
        to = (me + i) % 16
        cp = remote(
            state.at[pl.ds(pl.multiple_of(to * 32, 32), 32)],
            arrived.at[me],
            a1s.at[i],
            a1r.at[i],
            (to // 4, to % 4, z, k),
        )
        cp.start()
        sent.append(cp)
    sent += weights.first(1, w)

    loads[4].wait()
    loads[5].wait()
    allowed = jnp.where((row >= col) & (seg_row == seg_col), 1.0, 0.0)
    gap = jnp.maximum(row - col, 0).astype(F32)
    for h in range(4):
        rate = rates[4 * t + h]
        cols = slice(h * HD, (h + 1) * HD)
        scores = lax.dot_general(
            q[:, cols], k_in[:, cols], (((1,), (1,)), ((), ())), preferred_element_type=F32
        )
        mixed = (scores * (allowed * jnp.exp(-rate * gap))).astype(BF)
        within[:, cols] = jnp.dot(mixed, v[:, cols], preferred_element_type=F32)

    own_state.wait()
    for i in range(1, 16):
        ref = arrived.at[(me - i + 16) % 16]
        remote(ref, ref, a1s.at[i], a1r.at[i], (y, x, z, 1 - k)).wait_recv()
    decay = jnp.exp(jnp.zeros((32, HD), F32) - rates[4 * t + y] * ROWS)
    running = jnp.zeros((32, HD), F32)
    for b in range(BLOCKS):
        onward[b] = running.astype(BF)
        same = seg(jnp.int32(b * ROWS + ROWS - 1)) == seg(jnp.int32(b * ROWS - 1))
        running = running * (decay * jnp.where(same, 1.0, 0.0)) + arrived[b].astype(F32)
    own_onward = pltpu.make_async_copy(onward.at[me], incoming.at[me], loc.at[5])
    own_onward.start()
    for i in range(1, 16):
        to = (me + i) % 16
        cp = remote(
            onward.at[to], incoming.at[me], a2s.at[i], a2r.at[i], (to // 4, to % 4, z, k)
        )
        cp.start()
        sent.append(cp)
    for d in range(2):
        for part in range(2):
            weights.arrived(d, part)
    for d in range(2):
        sent.append(weights.forward(d))
    own_onward.wait()
    for i in range(1, 16):
        ref = incoming.at[(me - i + 16) % 16]
        remote(ref, ref, a2s.at[i], a2r.at[i], (y, x, z, 1 - k)).wait_recv()

    reached = jnp.where(seg_row == before, 1.0, 0.0)
    for h in range(4):
        rate = rates[4 * t + h]
        cols = slice(h * HD, (h + 1) * HD)
        inc = incoming[4 * h : 4 * h + 4].reshape(HD, HD)
        inter = jnp.dot(q[:, cols], inc, preferred_element_type=F32)
        both = within[:, cols] + inter * (reached * jnp.exp(-rate * (rowf + 1.0)))
        scale = lax.rsqrt(jnp.mean(both * both, axis=1, keepdims=True) + 1e-06)
        within[:, cols] = both * scale * again[:, cols]
    hbuf[x] = within[...].astype(BF)
    sent += heads.first(0, hbuf.at[x])
    sent += heads.first(1, hbuf.at[x])
    heads.arrived(0, 0)
    sent.append(heads.forward(0))
    heads.arrived(1, 1)
    sent.append(heads.forward(1))
    heads.arrived(0, 1)
    heads.arrived(1, 0)
    own_w.wait()
    for d in range(2):
        weights.forwarded(d)
    for d in range(2):
        heads.forwarded(d)

    total = RingSum(spot, ROWS, own, out, got, tbuf, rbuf, xs, xr, ts, tr)

    def produce(i):
        chunk = (z + ORDER[i]) % 8
        pair = 2 * (chunk % 2)
        wide = wbuf[chunk // 2]
        out[i] = jnp.dot(hbuf[pair + 1 - k], wide, preferred_element_type=F32).astype(BF)
        own[i] = jnp.dot(hbuf[pair + k], wide, preferred_element_type=F32).astype(BF)

    total.run(produce)

    @pl.when(low != x)
    def _():
        handed.wait()

    @pl.when(low == x)
    def _():
        kept.wait()

    for part in range(2):
        rows = slice(part * 64, part * 64 + 64)
        h_out[rows, :] = (resbuf[rows, :].astype(F32) + total.result(part)).astype(BF)
    own_gain.wait()
    for i in range(1, 16):
        ref = gain_out.at[(t - i + 16) % 16, 0]
        remote(ref, ref, gs.at[i], gr.at[i], (y, x, z, 1 - k)).wait_recv()
    own_ids.wait()
    for i in range(1, 4):
        ref = ids_all.at[(x - i + 4) % 4]
        remote(ref, ref, ids_s.at[i], ids_r.at[i], (y, x, z, 1 - k)).wait_recv()
    return sent + total.sent


def slot_hits(ids):
    expert = lax.broadcasted_iota(jnp.int32, (BLOCKS, CAP, ROWS), 0).reshape(SLOTS, ROWS)
    place_in = lax.broadcasted_iota(jnp.int32, (BLOCKS, CAP, ROWS), 1).reshape(SLOTS, ROWS)
    hit0 = expert == ids[0:1, :]
    hit1 = expert == ids[1:2, :]
    named = jnp.where(hit0 | hit1, 1.0, 0.0)
    earlier = lax.broadcasted_iota(jnp.int32, (ROWS, ROWS), 0)
    later = lax.broadcasted_iota(jnp.int32, (ROWS, ROWS), 1)
    rank = jnp.dot(
        named.astype(BF),
        jnp.where(earlier < later, 1.0, 0.0).astype(BF),
        preferred_element_type=F32,
    )
    here = rank == place_in.astype(F32)
    return hit0 & here, hit1 & here


def experts(
    wts, wgu, wd, weight_loads, h, ids_all, gains,
    o_ref,
    ds, xb, lhs, acc, squares, act, hn, qs, rb,
    own, out, got, tbuf, rbuf,
    dss, dsr, fs, fr, cs, cr, qss, qsr, ps, pr, xs, xr, ts, tr, loc,
):
    spot = y, x, z, k = place()
    me, t = 4 * y + x, 2 * z + k
    low, partner = partner_of(*spot)
    peer = (y, x, z, 1 - k)
    sent = []
    hit0, hit1 = slot_hits(ids_all[low])
    pick = jnp.where(hit0 | hit1, 1.0, 0.0).astype(BF)
    picked = jnp.dot(pick, h[...], preferred_element_type=F32)
    ds[...] = picked.reshape(BLOCKS, CAP, FEAT).astype(BF)

    mine = 4 * x + y
    own_rows = pltpu.make_async_copy(ds.at[me], xb.at[t, mine], loc.at[3])
    own_rows.start()
    for i in range(1, 16):
        to = (me + i) % 16
        cp = remote(ds.at[to], xb.at[t, mine], dss.at[i], dsr.at[i], (to // 4, to % 4, z, k))
        cp.start()
        sent.append(cp)
    handed = remote(h, hn, ps.at[0], pr.at[0], partner)
    kept = pltpu.make_async_copy(h, hn, loc.at[4])

    @pl.when(low != x)
    def _():
        handed.start()

    @pl.when(low == x)
    def _():
        kept.start()

    own_rows.wait()
    for i in range(1, 16):
        c = (me - i + 16) % 16
        ref = xb.at[t, 4 * (c % 4) + c // 4]
        remote(ref, ref, dss.at[i], dsr.at[i], peer).wait_recv()

    def half(zz, kk, part):
        return xb.at[2 * ((zz + 8) % 8) + kk, pl.ds(part * 8, 8)]

    def ring(d, s, part, ref):
        to = (z + (1, 7)[d]) % 8
        return remote(ref, ref, fs.at[d, s, part], fr.at[d, s, part], (y, x, to, k))

    def over(slot, part, ref):
        return remote(ref, ref, cs.at[slot, part], cr.at[slot, part], peer)

    def push(cp):
        cp.start()
        sent.append(cp)

    def crossed(slot, dist):
        for part in range(2):
            over(slot, part, half(z + dist, 1 - k, part)).wait_recv()

    for part in range(2):
        ref = half(z, k, part)
        push(ring(0, 0, part, ref))
        push(ring(1, 0, part, ref))
        push(over(0, part, ref))

    wgu[HID:FEAT, :] = jnp.zeros((FEAT - HID, D), BF)
    acc[...] = jnp.zeros_like(acc)
    squares[...] = jnp.zeros_like(squares)

    def multiply(group):
        for xx in range(4):
            gain = gains[4 * group + xx]
            for xp in range(4):
                rows = slice(96 * xp, 96 * xp + 96)
                piece = xb[4 * group + xp, 4 * xx : 4 * xx + 4].astype(F32).reshape(96, FEAT)
                sq = piece * piece
                squares[rows, :] += sq[:, 0:128] + sq[:, 128:256] + sq[:, 256:384]
                lhs[rows, xx * FEAT : (xx + 1) * FEAT] = (piece * gain).astype(BF)
        cols = pl.ds(pl.multiple_of(group * 1536, 1536), 1536)
        acc[...] += lax.dot_general(
            lhs[...], wgu[:, cols], (((1,), (1,)), ((), ())), preferred_element_type=F32
        )

    side = jnp.where(z % 2 == 0, 3, 1)
    pair = z // 2
    for s in (1, 2, 3):
        for part in range(2):
            for d in range(2):
                behind = -s if d == 0 else s
                ref = half(z + behind, k, part)
                ring(d, s - 1, part, ref).wait_recv()
                if s < 3 or part == d:
                    push(ring(d, s, part, ref))
                push(over(2 * s - 1 + d, part, ref))
        if s == 1:
            crossed(0, 0)
            crossed(1, -1)
            crossed(2, 1)
            weight_loads[0].wait()
            weight_loads[1].wait()
            multiply(pair)
        elif s == 2:
            crossed(3, -2)
            crossed(4, 2)
            multiply((pair + side) % 4)
        else:
            crossed(5, -3)
            crossed(6, 3)
            multiply((pair + 4 - side) % 4)
    for d in range(2):
        ref = half(z + 4, k, d)
        ring(d, 3, d, ref).wait_recv()
        push(over(7, d, ref))
    crossed(7, 4)
    multiply((pair + 2) % 4)

    total_sq = jnp.sum(squares[...], axis=1, keepdims=True)
    scale = lax.rsqrt(total_sq / D + 1e-05)
    gate = acc[:, :HID] * scale
    lifted = acc[:, FEAT:] * scale
    act[...] = (gate / (1.0 + jnp.exp(-gate)) * lifted).astype(BF)
    weight_loads[2].wait()

    total = RingSum(spot, SLOTS, own, out, got, tbuf, rbuf, xs, xr, ts, tr)

    def produce(i):
        chunk = (z + ORDER[i]) % 8

        def tile(lane):
            cols = pl.ds(pl.multiple_of((2 * chunk + lane) * FEAT, FEAT), FEAT)
            return jnp.dot(act[...], wd[:, cols], preferred_element_type=F32).astype(BF)

        out[i] = tile(1 - k)
        own[i] = tile(k)

    total.run(produce)
    for part in range(2):
        qs[part * 8 : part * 8 + 8] = total.result(part).reshape(8, CAP, FEAT).astype(BF)
    own_back = pltpu.make_async_copy(qs.at[mine], rb.at[me], loc.at[5])
    own_back.start()
    for i in range(1, 16):
        to = (me + i) % 16
        push(
            remote(
                qs.at[4 * (to % 4) + to // 4],
                rb.at[me],
                qss.at[i],
                qsr.at[i],
                (to // 4, to % 4, z, k),
            )
        )
    weight_loads[3].wait()
    hit0, hit1 = slot_hits(ids_all[x])
    part_of = jnp.where(hit0, wts[0:1, :], 0.0) + jnp.where(hit1, wts[1:2, :], 0.0)
    coarse = part_of.astype(BF)
    fine = (part_of - coarse.astype(F32)).astype(BF)

    @pl.when(low != x)
    def _():
        handed.wait()

    @pl.when(low == x)
    def _():
        kept.wait()

    own_back.wait()
    for i in range(1, 16):
        ref = rb.at[(me - i + 16) % 16]
        remote(ref, ref, qss.at[i], qsr.at[i], peer).wait_recv()
    back = rb[...].astype(F32).reshape(SLOTS, FEAT).astype(BF)
    dims = (((0,), (0,)), ((), ()))
    mixture = lax.dot_general(coarse, back, dims, preferred_element_type=F32)
    mixture += lax.dot_general(fine, back, dims, preferred_element_type=F32)
    o_ref[...] = (hn[...].astype(F32) + mixture).astype(BF)
    return sent + total.sent


def layer(*refs):
    ins, o_ref, refs = refs[:14], refs[14], list(refs[15:])

    def take(n):
        taken = refs[:n]
        del refs[:n]
        return taken

    wg_hbm, wu_hbm, wd_hbm, wts_hbm = ins[10:]
    wgu, wd, wts, weight_sems = take(4)
    early = take(6)
    passed = h, ids_all, gains = take(3)
    mix_scratch = take(8)
    mix_ring = take(5)
    mix_sems = take(19)
    moe_scratch = take(9)
    moe_ring = take(5)
    moe_sems = take(15)
    weight_loads = [
        pltpu.make_async_copy(wg_hbm, wgu.at[pl.ds(0, HID)], weight_sems.at[0]),
        pltpu.make_async_copy(wu_hbm, wgu.at[pl.ds(FEAT, HID)], weight_sems.at[1]),
        pltpu.make_async_copy(wd_hbm, wd, weight_sems.at[2]),
        pltpu.make_async_copy(wts_hbm, wts, weight_sems.at[3]),
    ]

    def start_weights():
        for cp in weight_loads:
            cp.start()

    sent = mixer(
        *ins[:10], *early, *passed, *mix_scratch, *mix_ring, *mix_sems, start_weights
    )
    sent += experts(
        wts, wgu, wd, weight_loads, *passed, o_ref, *moe_scratch, *moe_ring, *moe_sems
    )
    for cp in sent:
        cp.wait_send()


def dma(*shape):
    return pltpu.SemaphoreType.DMA(shape)


def ring_scratch(rows):
    half = rows // 2
    return [
        pltpu.VMEM((8, rows, FEAT), BF),
        pltpu.VMEM((8, rows, FEAT), BF),
        pltpu.VMEM((8, rows, FEAT), BF),
        pltpu.VMEM((2, 4, 2, half, FEAT), BF),
        pltpu.VMEM((2, 4, 2, half, FEAT), BF),
    ]


ANY = pl.BlockSpec(memory_space=pl.ANY)


def shards(
    residual, query_rows, key_rows, value_rows, head_rates, doc_lengths, attn_gain, out_weight,
    moe_gain, expert_ids, expert_weights, gate_weight, up_weight, down_weight,
):
    return pl.pallas_call(
        layer,
        out_shape=jax.ShapeDtypeStruct((ROWS, FEAT), BF),
        in_specs=[ANY] * 14,
        out_specs=pl.BlockSpec(memory_space=pltpu.VMEM),
        scratch_shapes=[
            pltpu.VMEM((FEAT + HID, D), BF),
            pltpu.VMEM((HID, D), BF),
            pltpu.VMEM((2, ROWS), F32),
            dma(4),
            pltpu.SMEM((64,), F32),
            pltpu.SMEM((4,), jnp.int32),
            pltpu.VMEM((ROWS, 512), BF),
            pltpu.VMEM((ROWS, 512), BF),
            pltpu.VMEM((ROWS, 512), BF),
            pltpu.VMEM((1, 512), F32),
            pltpu.VMEM((ROWS, FEAT), BF),
            pltpu.VMEM((4, 2, ROWS), jnp.int32),
            pltpu.VMEM((16, 1, FEAT), F32),
            pltpu.VMEM((4, 512, FEAT), BF),
            pltpu.VMEM((4, ROWS, 512), BF),
            pltpu.VMEM((512, HD), BF),
            pltpu.VMEM((16, 32, HD), BF),
            pltpu.VMEM((16, 32, HD), BF),
            pltpu.VMEM((16, 32, HD), BF),
            pltpu.VMEM((ROWS, FEAT), BF),
            pltpu.VMEM((ROWS, 512), F32),
            *ring_scratch(ROWS),
            dma(2, 3), dma(2, 3), dma(2, 3), dma(2, 3),
            dma(16), dma(16), dma(16), dma(16), dma(16), dma(16),
            dma(1), dma(1), dma(4), dma(4), dma(8), dma(8), dma(2, 4, 2), dma(2, 4, 2), dma(12),
            pltpu.VMEM((BLOCKS, CAP, FEAT), BF),
            pltpu.VMEM((16, BLOCKS, CAP, FEAT), BF),
            pltpu.VMEM((SLOTS, 4 * FEAT), BF),
            pltpu.VMEM((SLOTS, FEAT + HID), F32),
            pltpu.VMEM((SLOTS, 128), F32),
            pltpu.VMEM((SLOTS, HID), BF),
            pltpu.VMEM((ROWS, FEAT), BF),
            pltpu.VMEM((BLOCKS, CAP, FEAT), BF),
            pltpu.VMEM((BLOCKS, CAP, FEAT), BF),
            *ring_scratch(SLOTS),
            dma(16), dma(16), dma(2, 4, 2), dma(2, 4, 2), dma(8, 2), dma(8, 2),
            dma(16), dma(16), dma(1), dma(1), dma(8), dma(8), dma(2, 4, 2), dma(2, 4, 2), dma(6),
        ],
        compiler_params=pltpu.CompilerParams(
            collective_id=0, has_side_effects=True, vmem_limit_bytes=67043328
        ),
        name="layer",
    )(
        head_rates, doc_lengths, query_rows, key_rows, value_rows, attn_gain.reshape(1, -1),
        out_weight, residual, moe_gain, expert_ids.T,
        gate_weight[0].T, up_weight[0].T, down_weight[0], expert_weights.T,
    )


def solution(mesh):
    finer = Mesh(mesh.devices.reshape(4, 4, 8, 2), AXES)
    placed = (
        P(CTX, TP), P(CTX, TP), P(CTX, TP), P(CTX, TP), P(), P(), P(TP), P(TP, CTX), P(TP),
        P(CTX, None), P(CTX, None), P(CTX, None, TP), P(CTX, None, TP), P(CTX, TP, None),
    )
    return jax.shard_map(shards, mesh=finer, in_specs=placed, out_specs=P(CTX, TP), check_vma=False)
```

```python
import jax
import jax.numpy as jnp
from jax import lax
from jax.experimental import pallas as pl
from jax.experimental.pallas import tpu as pltpu
from jax.sharding import Mesh
from jax.sharding import PartitionSpec as P

D = 6144
HD = 128
CAP = 24
BLOCKS = 16
ROWS = 128
FEAT = 384
NEAR = 256
FAR = 128
HID = 288
SLOTS = BLOCKS * CAP
CTX = ("ctx_0", "ctx_1")
TP = ("tp_0", "tp_1")
AXES = CTX + TP
ORDER = (4, 3, 5, 2, 6, 1, 7, 0)
BF = jnp.bfloat16
F32 = jnp.float32


def remote(src, dst, send_sem, recv_sem, to):
    return pltpu.make_async_remote_copy(
        src_ref=src,
        dst_ref=dst,
        send_sem=send_sem,
        recv_sem=recv_sem,
        device_id=to,
        device_id_type=pl.DeviceIdType.MESH,
    )


def place():
    return tuple(lax.axis_index(a) for a in AXES)


def partner_of(y, x, z, k):
    low = 2 * (z % 2) + k
    return low, (y, low, 2 * (z // 2) + x // 2, x % 2)


def greet(y, x, z, k):
    sem = pltpu.get_barrier_semaphore()
    for i in range(1, 16):
        c = (4 * y + x + i) % 16
        pl.semaphore_signal(
            sem, inc=1, device_id=(c // 4, c % 4, z, k), device_id_type=pl.DeviceIdType.MESH
        )
    for i in range(1, 16):
        t = (2 * z + k + i) % 16
        pl.semaphore_signal(
            sem, inc=1, device_id=(y, x, t // 2, t % 2), device_id_type=pl.DeviceIdType.MESH
        )
    low, partner = partner_of(y, x, z, k)

    @pl.when(low != x)
    def _():
        pl.semaphore_signal(sem, inc=1, device_id=partner, device_id_type=pl.DeviceIdType.MESH)

    pl.semaphore_wait(sem, 30 + ((low - x + 4) % 4 + 3) // 4)


class RingGather:
    def __init__(self, buf, ssem, rsem, me, device_at, half):
        self.buf, self.ssem, self.rsem = buf, ssem, rsem
        self.me, self.at, self.half = me, device_at, half

    def piece(self, member, part):
        return self.buf.at[member % 4, pl.ds(part * self.half, self.half)]

    def first(self, part, own):
        out = []
        for d, step in enumerate((1, -1)):
            cp = remote(
                own.at[pl.ds(part * self.half, self.half)],
                self.piece(self.me, part),
                self.ssem.at[d, part],
                self.rsem.at[d, part],
                self.at((self.me + step) % 4),
            )
            cp.start()
            out.append(cp)
        return out

    def arrived(self, d, part):
        step = (1, -1)[d]
        ref = self.piece(self.me + 4 - step, part)
        remote(
            ref, ref, self.ssem.at[d, part], self.rsem.at[d, part], self.at((self.me + step) % 4)
        ).wait_recv()

    def forward(self, d):
        step = (1, -1)[d]
        ref = self.piece(self.me + 4 - step, d)
        cp = remote(
            ref, ref, self.ssem.at[d, 2], self.rsem.at[d, 2], self.at((self.me + step) % 4)
        )
        cp.start()
        return cp

    def forwarded(self, d):
        step = (1, -1)[d]
        ref = self.piece(self.me + 2, d)
        remote(
            ref, ref, self.ssem.at[d, 2], self.rsem.at[d, 2], self.at((self.me + step) % 4)
        ).wait_recv()


class RingSum:
    def __init__(self, spot, rows, own, out, got, tbuf, rbuf, xs, xr, ssem, rsem):
        self.y, self.x, self.z, self.k = spot
        self.half = rows // 2
        self.own, self.out, self.got = own, out, got
        self.tbuf, self.rbuf = tbuf, rbuf
        self.xs, self.xr, self.ssem, self.rsem = xs, xr, ssem, rsem
        self.sent = []

    def swap(self, i):
        d = ORDER[i]
        cp = remote(
            self.out.at[i],
            self.got.at[i],
            self.xs.at[i],
            self.xr.at[i],
            (self.y, self.x, self.z, 1 - self.k),
        )
        cp.start()
        self.sent.append(cp)

    def swapped(self, i):
        remote(
            self.out.at[i],
            self.got.at[i],
            self.xs.at[i],
            self.xr.at[i],
            (self.y, self.x, self.z, 1 - self.k),
        ).wait_recv()

    def local(self, i, part):
        rows = pl.ds(part * self.half, self.half)
        return self.own[i, rows, :].astype(F32) + self.got[i, rows, :].astype(F32)

    def hop(self, d, s, part):
        to = (self.z + (1, 7)[d]) % 8
        return remote(
            self.tbuf.at[d, s, part],
            self.rbuf.at[d, s, part],
            self.ssem.at[d, s, part],
            self.rsem.at[d, s, part],
            (self.y, self.x, to, self.k),
        )

    def send(self, d, s, part, value):
        self.tbuf[d, s, part] = value.astype(BF)
        cp = self.hop(d, s, part)
        cp.start()
        self.sent.append(cp)

    def begin(self, produce):
        produce(0)
        self.swap(0)
        produce(1)
        self.swap(1)
        produce(2)
        self.swap(2)
        self.swapped(0)
        self.send(0, 0, 0, self.local(0, 0))
        self.send(1, 0, 1, self.local(0, 1))
        self.swapped(1)
        self.send(0, 1, 1, self.local(1, 1))
        self.swapped(2)
        self.send(1, 1, 0, self.local(2, 0))

    def rest(self, produce):
        for i in range(3, 8):
            produce(i)
            self.swap(i)
        self.hop(0, 0, 0).wait_recv()
        self.send(0, 1, 0, self.local(1, 0) + self.rbuf[0, 0, 0].astype(F32))
        self.hop(1, 0, 1).wait_recv()
        self.send(1, 1, 1, self.local(2, 1) + self.rbuf[1, 0, 1].astype(F32))
        for s in (2, 3):
            self.swapped(2 * s - 1)
            self.swapped(2 * s)
            for j in range(2):
                for d in range(2):
                    part = (1 - j) if d == 0 else j
                    self.hop(d, s - 1, part).wait_recv()
                    self.send(
                        d,
                        s,
                        part,
                        self.local(2 * s - 1 + d, part) + self.rbuf[d, s - 1, part].astype(F32),
                    )
        self.swapped(7)

    def result(self, part):
        self.hop(0, 3, part).wait_recv()
        self.hop(1, 3, part).wait_recv()
        return (
            self.local(7, part)
            + self.rbuf[0, 3, part].astype(F32)
            + self.rbuf[1, 3, part].astype(F32)
        )


def mixer(
    rates_hbm, docs_hbm, q_hbm, k_hbm, v_hbm, again_hbm, w, res, mgain, ids,
    rates, docs, q, k_in, v, again,
    h_out, ids_all, gain_out,
    wbuf, hbuf, state, arrived, onward, incoming, resbuf, within,
    own, out, got, tbuf, rbuf,
    wss, wrs, hss, hrs, a1s, a1r, a2s, a2r, gs, gr, ps, pr, ids_s, ids_r, xs, xr, ts, tr, loc, start_weights,
):
    spot = y, x, z, k = place()
    me, t = 4 * y + x, 2 * z + k
    low, partner = partner_of(*spot)
    sent = []
    loads = [
        pltpu.make_async_copy(a, b, loc.at[6 + i])
        for i, (a, b) in enumerate(
            (
                (k_hbm, k_in), (v_hbm, v), (rates_hbm, rates), (docs_hbm, docs), (q_hbm, q),
                (again_hbm, again),
            )
        )
    ]
    for cp in loads:
        cp.start()
    greet(*spot)

    weights = RingGather(wbuf, wss, wrs, y, lambda i: (i, x, z, k), 256)
    heads = RingGather(hbuf, hss, hrs, x, lambda i: (y, i, z, k), 64)
    own_w = pltpu.make_async_copy(w, wbuf.at[y], loc.at[0])
    own_w.start()

    handed = remote(res, resbuf, ps.at[0], pr.at[0], partner)
    kept = pltpu.make_async_copy(res, resbuf, loc.at[1])

    @pl.when(low != x)
    def _():
        handed.start()

    @pl.when(low == x)
    def _():
        kept.start()

    own_ids = pltpu.make_async_copy(ids, ids_all.at[x], loc.at[2])
    own_ids.start()
    for i in range(1, 4):
        cp = remote(ids, ids_all.at[x], ids_s.at[i], ids_r.at[i], (y, (x + i) % 4, z, k))
        cp.start()
        sent.append(cp)

    own_gain = pltpu.make_async_copy(mgain, gain_out.at[t, 0], loc.at[3])
    own_gain.start()
    for i in range(1, 16):
        to = (t + i) % 16
        cp = remote(mgain, gain_out.at[t, 0], gs.at[i], gr.at[i], (y, x, to // 2, to % 2))
        cp.start()
        sent.append(cp)

    start_weights()
    for cp in loads[:4]:
        cp.wait()
    start1 = docs[0]
    start2 = start1 + docs[1]
    start3 = start2 + docs[2]

    def seg(p):
        def past(s):
            return jnp.where(p >= s, 1, 0)

        base = jnp.where(p >= 0, 0, -1)
        return base + past(start1) + past(start2) + past(start3)

    first = me * ROWS
    last_seg = seg(first + ROWS - 1)
    before = seg(first - 1)
    row = lax.broadcasted_iota(jnp.int32, (ROWS, HD), 0)
    col = lax.broadcasted_iota(jnp.int32, (ROWS, HD), 1)
    seg_row, seg_col = seg(first + row), seg(first + col)
    rowf = row.astype(F32)
    at_end = jnp.where(seg_row == last_seg, 1.0, 0.0)
    for h in range(4):
        rate = rates[4 * t + h]
        cols = slice(h * HD, (h + 1) * HD)
        fading = at_end * jnp.exp(-rate * (ROWS - 1.0 - rowf))
        faded = (k_in[:, cols].astype(F32) * fading).astype(BF)
        state[h * HD : (h + 1) * HD, :] = lax.dot_general(
            faded, v[:, cols], (((0,), (0,)), ((), ())), preferred_element_type=F32
        ).astype(BF)

    own_state = pltpu.make_async_copy(
        state.at[pl.ds(pl.multiple_of(me * 32, 32), 32)], arrived.at[me], loc.at[4]
    )
    own_state.start()
    for i in range(1, 16):
        to = (me + i) % 16
        cp = remote(
            state.at[pl.ds(pl.multiple_of(to * 32, 32), 32)],
            arrived.at[me],
            a1s.at[i],
            a1r.at[i],
            (to // 4, to % 4, z, k),
        )
        cp.start()
        sent.append(cp)
    sent += weights.first(0, w)

    loads[4].wait()
    loads[5].wait()
    allowed = jnp.where((row >= col) & (seg_row == seg_col), 1.0, 0.0)
    gap = jnp.maximum(row - col, 0).astype(F32)
    for h in range(4):
        rate = rates[4 * t + h]
        cols = slice(h * HD, (h + 1) * HD)
        scores = lax.dot_general(
            q[:, cols], k_in[:, cols], (((1,), (1,)), ((), ())), preferred_element_type=F32
        )
        mixed = (scores * (allowed * jnp.exp(-rate * gap))).astype(BF)
        within[:, cols] = jnp.dot(mixed, v[:, cols], preferred_element_type=F32)

    own_state.wait()
    for i in range(1, 16):
        ref = arrived.at[(me - i + 16) % 16]
        remote(ref, ref, a1s.at[i], a1r.at[i], (y, x, z, 1 - k)).wait_recv()
    decay = jnp.exp(jnp.zeros((32, HD), F32) - rates[4 * t + y] * ROWS)
    running = jnp.zeros((32, HD), F32)
    for b in range(BLOCKS):
        onward[b] = running.astype(BF)
        same = seg(jnp.int32(b * ROWS + ROWS - 1)) == seg(jnp.int32(b * ROWS - 1))
        running = running * (decay * jnp.where(same, 1.0, 0.0)) + arrived[b].astype(F32)
    own_onward = pltpu.make_async_copy(onward.at[me], incoming.at[me], loc.at[5])
    own_onward.start()
    for i in range(1, 16):
        to = (me + i) % 16
        cp = remote(
            onward.at[to], incoming.at[me], a2s.at[i], a2r.at[i], (to // 4, to % 4, z, k)
        )
        cp.start()
        sent.append(cp)
    sent += weights.first(1, w)
    weights.arrived(0, 0)
    sent.append(weights.forward(0))
    own_onward.wait()
    for i in range(1, 16):
        ref = incoming.at[(me - i + 16) % 16]
        remote(ref, ref, a2s.at[i], a2r.at[i], (y, x, z, 1 - k)).wait_recv()

    reached = jnp.where(seg_row == before, 1.0, 0.0)
    for h in range(4):
        rate = rates[4 * t + h]
        cols = slice(h * HD, (h + 1) * HD)
        inc = incoming[4 * h : 4 * h + 4].reshape(HD, HD)
        inter = jnp.dot(q[:, cols], inc, preferred_element_type=F32)
        both = within[:, cols] + inter * (reached * jnp.exp(-rate * (rowf + 1.0)))
        scale = lax.rsqrt(jnp.mean(both * both, axis=1, keepdims=True) + 1e-06)
        within[:, cols] = both * scale * again[:, cols]
    hbuf[x] = within[...].astype(BF)
    sent += heads.first(0, hbuf.at[x])
    sent += heads.first(1, hbuf.at[x])
    weights.arrived(1, 1)
    sent.append(weights.forward(1))
    heads.arrived(0, 0)
    sent.append(heads.forward(0))
    heads.arrived(1, 1)
    sent.append(heads.forward(1))
    heads.arrived(0, 1)
    heads.arrived(1, 0)
    own_w.wait()
    weights.arrived(0, 1)
    weights.arrived(1, 0)
    for d in range(2):
        weights.forwarded(d)
    for d in range(2):
        heads.forwarded(d)

    total = RingSum(spot, ROWS, own, out, got, tbuf, rbuf, xs, xr, ts, tr)

    def produce(i):
        chunk = (z + ORDER[i]) % 8
        pair = 2 * (chunk % 2)
        wide = wbuf[chunk // 2]
        out[i] = jnp.dot(hbuf[pair + 1 - k], wide, preferred_element_type=F32).astype(BF)
        own[i] = jnp.dot(hbuf[pair + k], wide, preferred_element_type=F32).astype(BF)

    total.begin(produce)
    total.rest(produce)

    @pl.when(low != x)
    def _():
        handed.wait()

    @pl.when(low == x)
    def _():
        kept.wait()

    for part in range(2):
        rows = slice(part * 64, part * 64 + 64)
        h_out[rows, :] = (resbuf[rows, :].astype(F32) + total.result(part)).astype(BF)
    own_gain.wait()
    for i in range(1, 16):
        ref = gain_out.at[(t - i + 16) % 16, 0]
        remote(ref, ref, gs.at[i], gr.at[i], (y, x, z, 1 - k)).wait_recv()
    own_ids.wait()
    for i in range(1, 4):
        ref = ids_all.at[(x - i + 4) % 4]
        remote(ref, ref, ids_s.at[i], ids_r.at[i], (y, x, z, 1 - k)).wait_recv()
    return sent + total.sent


def slot_hits(ids):
    expert = lax.broadcasted_iota(jnp.int32, (BLOCKS, CAP, ROWS), 0).reshape(SLOTS, ROWS)
    place_in = lax.broadcasted_iota(jnp.int32, (BLOCKS, CAP, ROWS), 1).reshape(SLOTS, ROWS)
    hit0 = expert == ids[0:1, :]
    hit1 = expert == ids[1:2, :]
    named = jnp.where(hit0 | hit1, 1.0, 0.0)
    earlier = lax.broadcasted_iota(jnp.int32, (ROWS, ROWS), 0)
    later = lax.broadcasted_iota(jnp.int32, (ROWS, ROWS), 1)
    rank = jnp.dot(
        named.astype(BF),
        jnp.where(earlier < later, 1.0, 0.0).astype(BF),
        preferred_element_type=F32,
    )
    here = rank == place_in.astype(F32)
    return hit0 & here, hit1 & here


def experts(
    wts, wga, wgb, wda, wdb, weights_here, h, ids_all, gains,
    o_ref,
    pick, ds, xb, hz, dsb, xb2, lhs, acc, squares, act, hn, qs, rb,
    ownb, outb, gotb, qsb, rb2, pb, gb,
    own, out, got, tbuf, rbuf,
    dss, dsr, fs, fr, cs, cr, qss, qsr, ps, pr, xs, xr, ts, tr, loc,
    b1s, b1r, b2s, b2r, os, osr, ws, wr, b3s, b3r, b4s, b4r,
):
    spot = y, x, z, k = place()
    me, t = 4 * y + x, 2 * z + k
    low, partner = partner_of(*spot)
    peer = (y, x, z, 1 - k)
    sent = []

    def push(cp):
        cp.start()
        sent.append(cp)

    def at_ctx(c):
        return (c // 4, c % 4, z, k)

    def column_major(c):
        return 4 * (c % 4) + c // 4

    hz[z] = h[:, NEAR:]
    for i in range(1, 8):
        push(remote(hz.at[z], hz.at[z], b1s.at[i], b1r.at[i], (y, x, (z + i) % 8, k)))

    for j in range(2):
        hit0, hit1 = slot_hits(ids_all[2 * j + k])
        pick[j] = jnp.where(hit0 | hit1, 1.0, 0.0).astype(BF)
    picked = jnp.dot(pick[z % 2], h[:, :NEAR], preferred_element_type=F32)
    ds[...] = picked.reshape(BLOCKS, CAP, NEAR).astype(BF)

    mine = 4 * x + y
    own_rows = pltpu.make_async_copy(ds.at[me], xb.at[t, mine], loc.at[3])
    own_rows.start()
    for i in range(1, 16):
        to = (me + i) % 16
        push(remote(ds.at[to], xb.at[t, mine], dss.at[i], dsr.at[i], at_ctx(to)))
    handed = remote(h, hn, ps.at[0], pr.at[0], partner)
    kept = pltpu.make_async_copy(h, hn, loc.at[4])

    @pl.when(low != x)
    def _():
        handed.start()

    @pl.when(low == x)
    def _():
        kept.start()

    own_rows.wait()
    for i in range(1, 16):
        ref = xb.at[t, column_major((me - i + 16) % 16)]
        remote(ref, ref, dss.at[i], dsr.at[i], peer).wait_recv()

    def half(zz, kk, part):
        return xb.at[2 * ((zz + 8) % 8) + kk, pl.ds(part * 8, 8)]

    def ring(d, s, part, ref):
        to = (z + (1, 7)[d]) % 8
        return remote(ref, ref, fs.at[d, s, part], fr.at[d, s, part], (y, x, to, k))

    def over(slot, part, ref):
        return remote(ref, ref, cs.at[slot, part], cr.at[slot, part], peer)

    def crossed(slot, dist):
        for part in range(2):
            over(slot, part, half(z + dist, 1 - k, part)).wait_recv()

    for part in range(2):
        ref = half(z, k, part)
        push(ring(0, 0, part, ref))
        push(ring(1, 0, part, ref))
        push(over(0, part, ref))

    for i in range(1, 8):
        ref = hz.at[(z - i + 8) % 8]
        remote(ref, ref, b1s.at[i], b1r.at[i], peer).wait_recv()
    for j in range(2):
        wide = jnp.concatenate([hz[2 * i + j] for i in range(4)], axis=1)
        chosen = jnp.dot(pick[j], wide, preferred_element_type=F32)
        dsb[:, j] = chosen.reshape(BLOCKS, CAP, 4 * FAR).astype(BF)
    own_far = pltpu.make_async_copy(dsb.at[me], xb2.at[k, mine], loc.at[0])
    own_far.start()
    for i in range(1, 16):
        to = (me + i) % 16
        push(remote(dsb.at[to], xb2.at[k, mine], b2s.at[i], b2r.at[i], at_ctx(to)))

    for w in (wga, wgb):
        w[HID:FEAT, :] = jnp.zeros((FEAT - HID, w.shape[1]), BF)
    acc[...] = jnp.zeros_like(acc)
    squares[...] = jnp.zeros_like(squares)

    def load_rows(piece, xp, gain, first):
        rows = slice(96 * xp, 96 * xp + 96)
        width = gain.shape[1]
        piece = piece.astype(F32).reshape(96, width)
        sq = piece * piece
        add = sq[:, 0:128]
        for i in range(1, width // 128):
            add += sq[:, 128 * i : 128 * i + 128]
        squares[rows, :] += add
        lhs[rows, first : first + width] = (piece * gain).astype(BF)

    def product(depth, w):
        acc[...] += lax.dot_general(
            lhs[:, :depth], w, (((1,), (1,)), ((), ())), preferred_element_type=F32
        )

    def multiply(group):
        for xx in range(4):
            gain = gains[4 * group + xx][:, :NEAR]
            for xp in range(4):
                load_rows(xb[4 * group + xp, 4 * xx : 4 * xx + 4], xp, gain, xx * NEAR)
        cols = pl.ds(pl.multiple_of(group * 4 * NEAR, 4 * NEAR), 4 * NEAR)
        product(4 * NEAR, wga[:, cols])

    def multiply_far():
        for xx in range(4):
            gain = jnp.concatenate([gains[4 * i + xx][:, NEAR:] for i in range(4)], axis=1)
            for xp in range(4):
                piece = xb2[xp % 2, 4 * xx : 4 * xx + 4, xp // 2]
                load_rows(piece, xp, gain, xx * 4 * FAR)
        product(16 * FAR, wgb[...])

    side = jnp.where(z % 2 == 0, 3, 1)
    pair = z // 2
    for s in (1, 2, 3):
        for part in range(2):
            for d in range(2):
                behind = -s if d == 0 else s
                ref = half(z + behind, k, part)
                ring(d, s - 1, part, ref).wait_recv()
                if s < 3 or part == d:
                    push(ring(d, s, part, ref))
                push(over(2 * s - 1 + d, part, ref))
        if s == 1:
            crossed(0, 0)
            crossed(1, -1)
            crossed(2, 1)
            weights_here(0)
            multiply(pair)
        elif s == 2:
            crossed(3, -2)
            crossed(4, 2)
            multiply((pair + side) % 4)
        else:
            own_far.wait()
            ref = xb2.at[k, mine]
            push(remote(ref, ref, os.at[0], osr.at[0], peer))
            for i in range(1, 16):
                ref = xb2.at[k, column_major((me - i + 16) % 16)]
                remote(ref, ref, b2s.at[i], b2r.at[i], peer).wait_recv()
                push(remote(ref, ref, os.at[i], osr.at[i], peer))
            crossed(5, -3)
            crossed(6, 3)
            multiply((pair + 4 - side) % 4)
    for d in range(2):
        ref = half(z + 4, k, d)
        ring(d, 3, d, ref).wait_recv()
        push(over(7, d, ref))
    for i in range(16):
        ref = xb2.at[1 - k, column_major((me - i + 16) % 16)]
        remote(ref, ref, os.at[i], osr.at[i], peer).wait_recv()
    multiply_far()
    crossed(7, 4)
    multiply((pair + 2) % 4)

    total_sq = jnp.sum(squares[...], axis=1, keepdims=True)
    scale = lax.rsqrt(total_sq / D + 1e-05)
    gate = acc[:, :HID] * scale
    lifted = acc[:, FEAT:] * scale
    act[...] = (gate / (1.0 + jnp.exp(-gate)) * lifted).astype(BF)
    weights_here(1)

    def far_tile(lane):
        cols = pl.ds(pl.multiple_of(lane * 8 * FAR, 8 * FAR), 8 * FAR)
        return jnp.dot(act[...], wdb[:, cols], preferred_element_type=F32).astype(BF)

    outb[...] = far_tile(1 - k)
    swap = remote(outb, gotb, ws.at[0], wr.at[0], peer)
    push(swap)
    ownb[...] = far_tile(k)

    total = RingSum(spot, SLOTS, own, out, got, tbuf, rbuf, xs, xr, ts, tr)

    def produce(i):
        chunk = (z + ORDER[i]) % 8

        def tile(lane):
            cols = pl.ds(pl.multiple_of((2 * chunk + lane) * NEAR, NEAR), NEAR)
            return jnp.dot(act[...], wda[:, cols], preferred_element_type=F32).astype(BF)

        out[i] = tile(1 - k)
        own[i] = tile(k)

    total.begin(produce)
    swap.wait_recv()
    summed = ownb[...].astype(F32) + gotb[...].astype(F32)
    qsb[...] = summed.reshape(BLOCKS, CAP, 8 * FAR).astype(BF)
    own_home = pltpu.make_async_copy(qsb.at[mine], rb2.at[me], loc.at[1])
    own_home.start()
    for i in range(1, 16):
        to = (me + i) % 16
        push(remote(qsb.at[column_major(to)], rb2.at[me], b3s.at[i], b3r.at[i], at_ctx(to)))
    total.rest(produce)

    weights_here(2)
    hit0, hit1 = slot_hits(ids_all[x])
    part_of = jnp.where(hit0, wts[0:1, :], 0.0) + jnp.where(hit1, wts[1:2, :], 0.0)
    coarse = part_of.astype(BF)
    fine = (part_of - coarse.astype(F32)).astype(BF)

    def combine(ref):
        back = ref[...].astype(F32).reshape(SLOTS, ref.shape[2]).astype(BF)
        dims = (((0,), (0,)), ((), ()))
        mixture = lax.dot_general(coarse, back, dims, preferred_element_type=F32)
        return mixture + lax.dot_general(fine, back, dims, preferred_element_type=F32)

    own_home.wait()
    for i in range(1, 16):
        ref = rb2.at[(me - i + 16) % 16]
        remote(ref, ref, b3s.at[i], b3r.at[i], peer).wait_recv()
    far_mix = combine(rb2)
    for i in range(8):
        pb[i] = far_mix[:, FAR * i : FAR * i + FAR].astype(BF)
    for i in range(1, 8):
        to = (z + i) % 8
        push(remote(pb.at[to], gb.at[i], b4s.at[i], b4r.at[i], (y, x, to, k)))

    for part in range(2):
        qs[part * 8 : part * 8 + 8] = total.result(part).reshape(8, CAP, NEAR).astype(BF)
    own_back = pltpu.make_async_copy(qs.at[mine], rb.at[me], loc.at[5])
    own_back.start()
    for i in range(1, 16):
        to = (me + i) % 16
        push(remote(qs.at[column_major(to)], rb.at[me], qss.at[i], qsr.at[i], at_ctx(to)))

    @pl.when(low != x)
    def _():
        handed.wait()

    @pl.when(low == x)
    def _():
        kept.wait()

    far_sum = hn[:, NEAR:].astype(F32) + pb[z].astype(F32)
    for i in range(1, 8):
        remote(gb.at[i], gb.at[i], b4s.at[i], b4r.at[i], peer).wait_recv()
        far_sum += gb[i].astype(F32)
    o_ref[:, NEAR:] = far_sum.astype(BF)
    own_back.wait()
    for i in range(1, 16):
        ref = rb.at[(me - i + 16) % 16]
        remote(ref, ref, qss.at[i], qsr.at[i], peer).wait_recv()
    o_ref[:, :NEAR] = (hn[:, :NEAR].astype(F32) + combine(rb)).astype(BF)
    return sent + total.sent


def layer(*refs):
    ins, o_ref, refs = refs[:14], refs[14], list(refs[15:])

    def take(n):
        taken = refs[:n]
        del refs[:n]
        return taken

    wg_hbm, wu_hbm, wd_hbm, wts_hbm = ins[10:]
    wga, wgb, wda, wdb, wts, wsem = take(6)
    early = take(6)
    passed = h, ids_all, gains = take(3)
    mix_scratch = take(8)
    mix_ring = take(5)
    mix_sems = take(19)
    moe_scratch = take(20)
    moe_ring = take(5)
    moe_sems = take(27)
    stages = ([], [], [])

    def load(stage, src, dst):
        n = sum(len(a) for a in stages)
        stages[stage].append(pltpu.make_async_copy(src, dst, wsem.at[n]))

    for c in range(16):
        near, far = pl.ds(FEAT * c, NEAR), pl.ds(FEAT * c + NEAR, FAR)
        spot = FAR * (4 * (c % 4) + c // 4)
        for src, row in ((wg_hbm, 0), (wu_hbm, FEAT)):
            rows = pl.ds(row, HID)
            load(0, src.at[:, near], wga.at[rows, pl.ds(NEAR * c, NEAR)])
            load(0, src.at[:, far], wgb.at[rows, pl.ds(spot, FAR)])
        load(1, wd_hbm.at[:, near], wda.at[:, pl.ds(NEAR * c, NEAR)])
        spot = FAR * (8 * (c % 2) + c // 2)
        load(1, wd_hbm.at[:, far], wdb.at[:, pl.ds(spot, FAR)])
    load(2, wts_hbm, wts)

    def start_weights():
        for stage in stages:
            for cp in stage:
                cp.start()

    def weights_here(stage):
        for cp in stages[stage]:
            cp.wait()

    sent = mixer(
        *ins[:10], *early, *passed, *mix_scratch, *mix_ring, *mix_sems, start_weights
    )
    sent += experts(
        wts, wga, wgb, wda, wdb, weights_here, *passed, o_ref, *moe_scratch, *moe_ring, *moe_sems
    )
    for cp in sent:
        cp.wait_send()


def dma(*shape):
    return pltpu.SemaphoreType.DMA(shape)


def ring_scratch(rows, width):
    half = rows // 2
    return [
        pltpu.VMEM((8, rows, width), BF),
        pltpu.VMEM((8, rows, width), BF),
        pltpu.VMEM((8, rows, width), BF),
        pltpu.VMEM((2, 4, 2, half, width), BF),
        pltpu.VMEM((2, 4, 2, half, width), BF),
    ]


ANY = pl.BlockSpec(memory_space=pl.ANY)


def shards(
    residual, query_rows, key_rows, value_rows, head_rates, doc_lengths, attn_gain, out_weight,
    moe_gain, expert_ids, expert_weights, gate_weight, up_weight, down_weight,
):
    return pl.pallas_call(
        layer,
        out_shape=jax.ShapeDtypeStruct((ROWS, FEAT), BF),
        in_specs=[ANY] * 14,
        out_specs=pl.BlockSpec(memory_space=pltpu.VMEM),
        scratch_shapes=[
            pltpu.VMEM((FEAT + HID, 16 * NEAR), BF),
            pltpu.VMEM((FEAT + HID, 16 * FAR), BF),
            pltpu.VMEM((HID, 16 * NEAR), BF),
            pltpu.VMEM((HID, 16 * FAR), BF),
            pltpu.VMEM((2, ROWS), F32),
            dma(97),
            pltpu.SMEM((64,), F32),
            pltpu.SMEM((4,), jnp.int32),
            pltpu.VMEM((ROWS, 512), BF),
            pltpu.VMEM((ROWS, 512), BF),
            pltpu.VMEM((ROWS, 512), BF),
            pltpu.VMEM((1, 512), F32),
            pltpu.VMEM((ROWS, FEAT), BF),
            pltpu.VMEM((4, 2, ROWS), jnp.int32),
            pltpu.VMEM((16, 1, FEAT), F32),
            pltpu.VMEM((4, 512, FEAT), BF),
            pltpu.VMEM((4, ROWS, 512), BF),
            pltpu.VMEM((512, HD), BF),
            pltpu.VMEM((16, 32, HD), BF),
            pltpu.VMEM((16, 32, HD), BF),
            pltpu.VMEM((16, 32, HD), BF),
            pltpu.VMEM((ROWS, FEAT), BF),
            pltpu.VMEM((ROWS, 512), F32),
            *ring_scratch(ROWS, FEAT),
            dma(2, 3), dma(2, 3), dma(2, 3), dma(2, 3),
            dma(16), dma(16), dma(16), dma(16), dma(16), dma(16),
            dma(1), dma(1), dma(4), dma(4), dma(8), dma(8), dma(2, 4, 2), dma(2, 4, 2), dma(12),
            pltpu.VMEM((2, SLOTS, ROWS), BF),
            pltpu.VMEM((BLOCKS, CAP, NEAR), BF),
            pltpu.VMEM((16, BLOCKS, CAP, NEAR), BF),
            pltpu.VMEM((8, ROWS, FAR), BF),
            pltpu.VMEM((BLOCKS, 2, CAP, 4 * FAR), BF),
            pltpu.VMEM((2, BLOCKS, 2, CAP, 4 * FAR), BF),
            pltpu.VMEM((SLOTS, 16 * FAR), BF),
            pltpu.VMEM((SLOTS, FEAT + HID), F32),
            pltpu.VMEM((SLOTS, 128), F32),
            pltpu.VMEM((SLOTS, HID), BF),
            pltpu.VMEM((ROWS, FEAT), BF),
            pltpu.VMEM((BLOCKS, CAP, NEAR), BF),
            pltpu.VMEM((BLOCKS, CAP, NEAR), BF),
            pltpu.VMEM((SLOTS, 8 * FAR), BF),
            pltpu.VMEM((SLOTS, 8 * FAR), BF),
            pltpu.VMEM((SLOTS, 8 * FAR), BF),
            pltpu.VMEM((BLOCKS, CAP, 8 * FAR), BF),
            pltpu.VMEM((BLOCKS, CAP, 8 * FAR), BF),
            pltpu.VMEM((8, ROWS, FAR), BF),
            pltpu.VMEM((8, ROWS, FAR), BF),
            *ring_scratch(SLOTS, NEAR),
            dma(16), dma(16), dma(2, 4, 2), dma(2, 4, 2), dma(8, 2), dma(8, 2),
            dma(16), dma(16), dma(1), dma(1), dma(8), dma(8), dma(2, 4, 2), dma(2, 4, 2), dma(6),
            dma(8), dma(8), dma(16), dma(16), dma(16), dma(16), dma(1), dma(1),
            dma(16), dma(16), dma(8), dma(8),
        ],
        compiler_params=pltpu.CompilerParams(
            collective_id=0, has_side_effects=True, vmem_limit_bytes=67043328
        ),
        name="layer",
    )(
        head_rates, doc_lengths, query_rows, key_rows, value_rows, attn_gain.reshape(1, -1),
        out_weight, residual, moe_gain, expert_ids.T,
        gate_weight[0].T, up_weight[0].T, down_weight[0], expert_weights.T,
    )


def solution(mesh):
    finer = Mesh(mesh.devices.reshape(4, 4, 8, 2), AXES)
    placed = (
        P(CTX, TP), P(CTX, TP), P(CTX, TP), P(CTX, TP), P(), P(), P(TP), P(TP, CTX), P(TP),
        P(CTX, None), P(CTX, None), P(CTX, None, TP), P(CTX, None, TP), P(CTX, TP, None),
    )
    return jax.shard_map(shards, mesh=finer, in_specs=placed, out_specs=P(CTX, TP), check_vma=False)
```

```python
import jax
import jax.numpy as jnp
from jax import lax
from jax.experimental import pallas as pl
from jax.experimental.pallas import tpu as pltpu
from jax.sharding import Mesh
from jax.sharding import PartitionSpec as P

D = 6144
HD = 128
CAP = 24
BLOCKS = 16
ROWS = 128
FEAT = 384
NEAR = 256
FAR = 128
HID = 288
SLOTS = BLOCKS * CAP
CTX = ("ctx_0", "ctx_1")
TP = ("tp_0", "tp_1")
AXES = CTX + TP
ORDER = (4, 3, 5, 2, 6, 1, 7, 0)
HOPS = [(d, s, p) for d in range(2) for s in range(4) for p in range(2) if s > 0 or p == d]
STEPS = [(d, s, p) for d in range(2) for s in range(4) for p in range(2) if s < 3 or p == d]
BF = jnp.bfloat16
F32 = jnp.float32


def remote(src, dst, send_sem, recv_sem, to):
    return pltpu.make_async_remote_copy(
        src_ref=src,
        dst_ref=dst,
        send_sem=send_sem,
        recv_sem=recv_sem,
        device_id=to,
        device_id_type=pl.DeviceIdType.MESH,
    )


def place():
    return tuple(lax.axis_index(a) for a in AXES)


def partner_of(y, x, z, k):
    low = 2 * (z % 2) + k
    return low, (y, low, 2 * (z // 2) + x // 2, x % 2)


def greet(y, x, z, k):
    sem = pltpu.get_barrier_semaphore()
    for i in range(1, 16):
        c = (4 * y + x + i) % 16
        pl.semaphore_signal(
            sem, inc=1, device_id=(c // 4, c % 4, z, k), device_id_type=pl.DeviceIdType.MESH
        )
    for i in range(1, 16):
        t = (2 * z + k + i) % 16
        pl.semaphore_signal(
            sem, inc=1, device_id=(y, x, t // 2, t % 2), device_id_type=pl.DeviceIdType.MESH
        )
    low, partner = partner_of(y, x, z, k)

    @pl.when(low != x)
    def _():
        pl.semaphore_signal(sem, inc=1, device_id=partner, device_id_type=pl.DeviceIdType.MESH)

    pl.semaphore_wait(sem, 30 + ((low - x + 4) % 4 + 3) // 4)


class Sends:
    def __init__(self):
        self.open = []

    def drain_later(self, ref, sem):
        self.open.append((ref, sem))

    def drain(self, to):
        for ref, sem in self.open:
            remote(ref, ref, sem, sem, to).wait_send()


class RingGather:
    def __init__(self, buf, ssem, rsem, me, device_at, half, sends):
        self.buf, self.ssem, self.rsem = buf, ssem, rsem
        self.me, self.at, self.half = me, device_at, half
        sends.drain_later(buf.at[pl.ds(0, 3)], ssem.at[0])

    def piece(self, member, part):
        return self.buf.at[member % 4, pl.ds(part * self.half, self.half)]

    def first(self, d, part, own):
        remote(
            own.at[pl.ds(part * self.half, self.half)],
            self.piece(self.me, part),
            self.ssem.at[0],
            self.rsem.at[d, part],
            self.at((self.me + (1, -1)[d]) % 4),
        ).start()

    def along(self, d, slot, ref):
        return remote(
            ref, ref, self.ssem.at[0], self.rsem.at[d, slot], self.at((self.me + (1, -1)[d]) % 4)
        )

    def arrived(self, d, part):
        self.along(d, part, self.piece(self.me + 4 - (1, -1)[d], part)).wait_recv()

    def forward(self, d):
        self.along(d, 2, self.piece(self.me + 4 - (1, -1)[d], d)).start()

    def forwarded(self, d):
        self.along(d, 2, self.piece(self.me + 2, d)).wait_recv()


class RingSum:
    def __init__(self, spot, rows, own, out, got, tbuf, rbuf, xs, xr, ssem, rsem, sends):
        self.y, self.x, self.z, self.k = spot
        self.half = rows // 2
        self.own, self.out, self.got = own, out, got
        self.tbuf, self.rbuf = tbuf, rbuf
        self.xs, self.xr, self.ssem, self.rsem = xs, xr, ssem, rsem
        sends.drain_later(out, xs.at[0])
        sends.drain_later(tbuf, ssem.at[0])

    def swap(self, i):
        self.swapping(i).start()

    def swapping(self, i):
        return remote(
            self.out.at[i],
            self.got.at[i],
            self.xs.at[0],
            self.xr.at[i],
            (self.y, self.x, self.z, 1 - self.k),
        )

    def swapped(self, i):
        self.swapping(i).wait_recv()

    def local(self, i, part):
        rows = pl.ds(part * self.half, self.half)
        return self.own[i, rows, :].astype(F32) + self.got[i, rows, :].astype(F32)

    def hop(self, d, s, part):
        to = (self.z + (1, 7)[d]) % 8
        return remote(
            self.tbuf.at[HOPS.index((d, s, part))],
            self.rbuf.at[HOPS.index((d, s, part))],
            self.ssem.at[0],
            self.rsem.at[HOPS.index((d, s, part))],
            (self.y, self.x, to, self.k),
        )

    def send(self, d, s, part, value):
        self.tbuf[HOPS.index((d, s, part))] = value.astype(BF)
        self.hop(d, s, part).start()

    def came(self, d, s, part):
        return self.rbuf[HOPS.index((d, s, part))].astype(F32)

    def begin(self, produce):
        produce(0)
        self.swap(0)
        produce(1)
        self.swap(1)
        produce(2)
        self.swap(2)
        self.swapped(0)
        self.send(0, 0, 0, self.local(0, 0))
        self.send(1, 0, 1, self.local(0, 1))
        self.swapped(1)
        self.send(0, 1, 1, self.local(1, 1))
        self.swapped(2)
        self.send(1, 1, 0, self.local(2, 0))

    def rest(self, produce):
        for i in range(3, 8):
            produce(i)
            self.swap(i)
        self.hop(0, 0, 0).wait_recv()
        self.send(0, 1, 0, self.local(1, 0) + self.came(0, 0, 0))
        self.hop(1, 0, 1).wait_recv()
        self.send(1, 1, 1, self.local(2, 1) + self.came(1, 0, 1))
        for s in (2, 3):
            self.swapped(2 * s - 1)
            self.swapped(2 * s)
            for j in range(2):
                for d in range(2):
                    part = (1 - j) if d == 0 else j
                    self.hop(d, s - 1, part).wait_recv()
                    self.send(
                        d,
                        s,
                        part,
                        self.local(2 * s - 1 + d, part) + self.came(d, s - 1, part),
                    )
        self.swapped(7)

    def result(self, part):
        self.hop(0, 3, part).wait_recv()
        self.hop(1, 3, part).wait_recv()
        return (
            self.local(7, part)
            + self.came(0, 3, part)
            + self.came(1, 3, part)
        )


def mixer(
    rates_hbm, docs_hbm, q_hbm, k_hbm, v_hbm, again_hbm, w, res, mgain, ids,
    rates, docs, q, k_in, v, again,
    h_out, ids_all, gain_out,
    wbuf, hbuf, state, arrived, onward, incoming, resbuf, within,
    own, out, got, tbuf, rbuf,
    wss, wrs, hss, hrs, a1s, a1r, a2s, a2r, gs, gr, ps, pr, ids_s, ids_r, xs, xr, ts, tr, loc, start_weights, sends,
):
    spot = y, x, z, k = place()
    me, t = 4 * y + x, 2 * z + k
    low, partner = partner_of(*spot)
    loads = [
        pltpu.make_async_copy(a, b, loc.at[6 + i])
        for i, (a, b) in enumerate(
            (
                (k_hbm, k_in), (v_hbm, v), (rates_hbm, rates), (docs_hbm, docs), (q_hbm, q),
                (again_hbm, again),
            )
        )
    ]
    for cp in loads:
        cp.start()
    greet(*spot)

    weights = RingGather(wbuf, wss, wrs, y, lambda i: (i, x, z, k), 256, sends)
    heads = RingGather(hbuf, hss, hrs, x, lambda i: (y, i, z, k), 64, sends)
    own_w = pltpu.make_async_copy(w, wbuf.at[y], loc.at[0])
    own_w.start()

    handed = remote(res, resbuf, ps.at[0], pr.at[0], partner)
    kept = pltpu.make_async_copy(res, resbuf, loc.at[1])

    @pl.when(low != x)
    def _():
        handed.start()

    @pl.when(low == x)
    def _():
        kept.start()

    own_ids = pltpu.make_async_copy(ids, ids_all.at[x], loc.at[2])
    own_ids.start()
    for i in range(1, 4):
        remote(ids, ids_all.at[x], ids_s.at[0], ids_r.at[0], (y, (x + i) % 4, z, k)).start()
    sends.drain_later(ids_all.at[pl.ds(0, 3)], ids_s.at[0])

    own_gain = pltpu.make_async_copy(mgain, gain_out.at[t, 0], loc.at[3])
    own_gain.start()
    for i in range(1, 16):
        to = (t + i) % 16
        remote(mgain, gain_out.at[t, 0], gs.at[0], gr.at[0], (y, x, to // 2, to % 2)).start()
    sends.drain_later(gain_out.at[pl.ds(0, 15)], gs.at[0])

    start_weights()
    for cp in loads[:4]:
        cp.wait()
    start1 = docs[0]
    start2 = start1 + docs[1]
    start3 = start2 + docs[2]

    def seg(p):
        def past(s):
            return jnp.where(p >= s, 1, 0)

        base = jnp.where(p >= 0, 0, -1)
        return base + past(start1) + past(start2) + past(start3)

    first = me * ROWS
    last_seg = seg(first + ROWS - 1)
    before = seg(first - 1)
    row = lax.broadcasted_iota(jnp.int32, (ROWS, HD), 0)
    col = lax.broadcasted_iota(jnp.int32, (ROWS, HD), 1)
    seg_row, seg_col = seg(first + row), seg(first + col)
    rowf = row.astype(F32)
    at_end = jnp.where(seg_row == last_seg, 1.0, 0.0)
    for h in range(4):
        rate = rates[4 * t + h]
        cols = slice(h * HD, (h + 1) * HD)
        fading = at_end * jnp.exp(-rate * (ROWS - 1.0 - rowf))
        faded = (k_in[:, cols].astype(F32) * fading).astype(BF)
        state[h * HD : (h + 1) * HD, :] = lax.dot_general(
            faded, v[:, cols], (((0,), (0,)), ((), ())), preferred_element_type=F32
        ).astype(BF)

    own_state = pltpu.make_async_copy(
        state.at[pl.ds(pl.multiple_of(me * 32, 32), 32)], arrived.at[me], loc.at[4]
    )
    own_state.start()
    for i in range(1, 16):
        to = (me + i) % 16
        remote(
            state.at[pl.ds(pl.multiple_of(to * 32, 32), 32)],
            arrived.at[me],
            a1s.at[0],
            a1r.at[0],
            (to // 4, to % 4, z, k),
        ).start()
    sends.drain_later(arrived.at[pl.ds(0, 15)], a1s.at[0])
    weights.first(0, 0, w)
    weights.first(1, 1, w)

    loads[4].wait()
    loads[5].wait()
    allowed = jnp.where((row >= col) & (seg_row == seg_col), 1.0, 0.0)
    gap = jnp.maximum(row - col, 0).astype(F32)
    for h in range(4):
        rate = rates[4 * t + h]
        cols = slice(h * HD, (h + 1) * HD)
        scores = lax.dot_general(
            q[:, cols], k_in[:, cols], (((1,), (1,)), ((), ())), preferred_element_type=F32
        )
        mixed = (scores * (allowed * jnp.exp(-rate * gap))).astype(BF)
        within[:, cols] = jnp.dot(mixed, v[:, cols], preferred_element_type=F32)

    own_state.wait()
    peer = (y, x, z, 1 - k)

    def receive(ref, sem):
        remote(ref, ref, sem, sem, peer).wait_recv()

    receive(arrived.at[pl.ds(0, 15)], a1r.at[0])
    decay = jnp.exp(jnp.zeros((32, HD), F32) - rates[4 * t + y] * ROWS)
    running = jnp.zeros((32, HD), F32)
    for b in range(BLOCKS):
        onward[b] = running.astype(BF)
        same = seg(jnp.int32(b * ROWS + ROWS - 1)) == seg(jnp.int32(b * ROWS - 1))
        running = running * (decay * jnp.where(same, 1.0, 0.0)) + arrived[b].astype(F32)
    own_onward = pltpu.make_async_copy(onward.at[me], incoming.at[me], loc.at[5])
    own_onward.start()
    for i in range(1, 16):
        to = (me + i) % 16
        remote(
            onward.at[to], incoming.at[me], a2s.at[0], a2r.at[0], (to // 4, to % 4, z, k)
        ).start()
    sends.drain_later(onward.at[pl.ds(0, 15)], a2s.at[0])
    for d in range(2):
        weights.arrived(d, d)
        weights.forward(d)
    for d in range(2):
        weights.first(d, 1 - d, w)
    own_onward.wait()
    receive(incoming.at[pl.ds(0, 15)], a2r.at[0])

    reached = jnp.where(seg_row == before, 1.0, 0.0)
    for h in range(4):
        rate = rates[4 * t + h]
        cols = slice(h * HD, (h + 1) * HD)
        inc = incoming[4 * h : 4 * h + 4].reshape(HD, HD)
        inter = jnp.dot(q[:, cols], inc, preferred_element_type=F32)
        both = within[:, cols] + inter * (reached * jnp.exp(-rate * (rowf + 1.0)))
        scale = lax.rsqrt(jnp.mean(both * both, axis=1, keepdims=True) + 1e-06)
        within[:, cols] = both * scale * again[:, cols]
    hbuf[x] = within[...].astype(BF)
    for part in range(2):
        for d in range(2):
            heads.first(d, part if d == 0 else 1 - part, hbuf.at[x])
    for d in range(2):
        heads.arrived(d, d)
        heads.forward(d)
    for d in range(2):
        heads.arrived(d, 1 - d)
    own_w.wait()
    for d in range(2):
        weights.arrived(d, 1 - d)
        weights.forwarded(d)
    for d in range(2):
        heads.forwarded(d)

    total = RingSum(spot, ROWS, own, out, got, tbuf, rbuf, xs, xr, ts, tr, sends)

    def produce(i):
        chunk = (z + ORDER[i]) % 8
        pair = 2 * (chunk % 2)
        wide = wbuf[chunk // 2]
        out[i] = jnp.dot(hbuf[pair + 1 - k], wide, preferred_element_type=F32).astype(BF)
        own[i] = jnp.dot(hbuf[pair + k], wide, preferred_element_type=F32).astype(BF)

    total.begin(produce)
    total.rest(produce)

    @pl.when(low != x)
    def _():
        handed.wait()

    @pl.when(low == x)
    def _():
        kept.wait()

    for part in range(2):
        rows = slice(part * 64, part * 64 + 64)
        h_out[rows, :] = (resbuf[rows, :].astype(F32) + total.result(part)).astype(BF)
    own_gain.wait()
    receive(gain_out.at[pl.ds(0, 15)], gr.at[0])
    own_ids.wait()
    receive(ids_all.at[pl.ds(0, 3)], ids_r.at[0])


def slot_hits(ids):
    expert = lax.broadcasted_iota(jnp.int32, (BLOCKS, CAP, ROWS), 0).reshape(SLOTS, ROWS)
    place_in = lax.broadcasted_iota(jnp.int32, (BLOCKS, CAP, ROWS), 1).reshape(SLOTS, ROWS)
    hit0 = expert == ids[0:1, :]
    hit1 = expert == ids[1:2, :]
    named = jnp.where(hit0 | hit1, 1.0, 0.0)
    earlier = lax.broadcasted_iota(jnp.int32, (ROWS, ROWS), 0)
    later = lax.broadcasted_iota(jnp.int32, (ROWS, ROWS), 1)
    rank = jnp.dot(
        named.astype(BF),
        jnp.where(earlier < later, 1.0, 0.0).astype(BF),
        preferred_element_type=F32,
    )
    here = rank == place_in.astype(F32)
    return hit0 & here, hit1 & here


def experts(
    wts, wgu, wd, loads, h, ids_all, gains,
    o_ref,
    pick, ds, xb, hz, dsb, xb2, lhs, acc, squares, act, hn, qs, rb,
    ownb, outb, gotb, qsb, rb2, pb, gb,
    own, out, got, tbuf, rbuf,
    dss, dsr, fs, fr, cs, cr, qss, qsr, ps, pr, xs, xr, ts, tr, loc,
    b1s, b1r, b2s, b2r, os, osr, ws, wr, b3s, b3r, b4s, b4r,
    sends,
):
    spot = y, x, z, k = place()
    me, t = 4 * y + x, 2 * z + k
    low, partner = partner_of(*spot)
    peer = (y, x, z, 1 - k)

    def receive(ref, sem):
        remote(ref, ref, sem, sem, peer).wait_recv()

    def at_ctx(c):
        return (c // 4, c % 4, z, k)

    def column_major(c):
        return 4 * (c % 4) + c // 4

    hz[z] = h[:, NEAR:]
    for i in range(1, 8):
        remote(hz.at[z], hz.at[z], b1s.at[0], b1r.at[0], (y, x, (z + i) % 8, k)).start()
    sends.drain_later(hz.at[pl.ds(0, 7)], b1s.at[0])

    for j in range(2):
        hit0, hit1 = slot_hits(ids_all[2 * j + k])
        pick[j] = jnp.where(hit0 | hit1, 1.0, 0.0).astype(BF)
    picked = jnp.dot(pick[z % 2], h[:, :NEAR], preferred_element_type=F32)
    ds[...] = picked.reshape(BLOCKS, CAP, NEAR).astype(BF)

    mine = 4 * x + y
    own_rows = pltpu.make_async_copy(ds.at[me], xb.at[t, mine], loc.at[3])
    own_rows.start()
    for i in range(1, 16):
        to = (me + i) % 16
        remote(ds.at[to], xb.at[t, mine], dss.at[0], dsr.at[0], at_ctx(to)).start()
    sends.drain_later(ds.at[pl.ds(0, 15)], dss.at[0])
    handed = remote(h, hn, ps.at[0], pr.at[0], partner)
    kept = pltpu.make_async_copy(h, hn, loc.at[4])

    @pl.when(low != x)
    def _():
        handed.start()

    @pl.when(low == x)
    def _():
        kept.start()

    own_rows.wait()
    receive(xb.at[t, pl.ds(0, 15)], dsr.at[0])

    def half(zz, kk, part):
        return xb.at[2 * ((zz + 8) % 8) + kk, pl.ds(part * 8, 8)]

    def ring(d, s, part, ref):
        to = (z + (1, 7)[d]) % 8
        return remote(
            ref, ref, fs.at[0], fr.at[STEPS.index((d, s, part))], (y, x, to, k)
        )

    def over(slot, ref):
        remote(ref, ref, cs.at[0], cr.at[slot], peer).start()

    def crossed(slot, dist):
        receive(xb.at[2 * ((z + dist + 8) % 8) + 1 - k], cr.at[slot])

    sends.drain_later(xb.at[pl.ds(0, 7)], fs.at[0])
    sends.drain_later(xb.at[pl.ds(0, 8)], cs.at[0])
    for part in range(2):
        ref = half(z, k, part)
        ring(0, 0, part, ref).start()
        ring(1, 0, part, ref).start()
        over(0, ref)

    receive(hz.at[pl.ds(0, 7)], b1r.at[0])
    for j in range(2):
        wide = jnp.concatenate([hz[2 * i + j] for i in range(4)], axis=1)
        chosen = jnp.dot(pick[j], wide, preferred_element_type=F32)
        dsb[:, j] = chosen.reshape(BLOCKS, CAP, 4 * FAR).astype(BF)
    own_far = pltpu.make_async_copy(dsb.at[me], xb2.at[k, mine], loc.at[0])
    own_far.start()
    for i in range(1, 16):
        to = (me + i) % 16
        remote(dsb.at[to], xb2.at[k, mine], b2s.at[0], b2r.at[0], at_ctx(to)).start()
    sends.drain_later(dsb.at[pl.ds(0, 15)], b2s.at[0])

    wgu[HID:FEAT, :] = jnp.zeros((FEAT - HID, D), BF)
    acc[...] = jnp.zeros_like(acc)
    squares[...] = jnp.zeros_like(squares)

    def columns(ref, tile, first, width):
        return ref[:, pl.ds(pl.multiple_of(tile * FEAT + first, 128), width)]

    def load_rows(piece, xp, gain, first):
        rows = slice(96 * xp, 96 * xp + 96)
        width = gain.shape[1]
        piece = piece.astype(F32).reshape(96, width)
        sq = piece * piece
        add = sq[:, 0:128]
        for i in range(1, width // 128):
            add += sq[:, 128 * i : 128 * i + 128]
        squares[rows, :] += add
        lhs[rows, first : first + width] = (piece * gain).astype(BF)

    def product(depth, w):
        acc[...] += lax.dot_general(
            lhs[:, :depth], w, (((1,), (1,)), ((), ())), preferred_element_type=F32
        )

    def multiply(group):
        for xx in range(4):
            gain = gains[4 * group + xx][:, :NEAR]
            for xp in range(4):
                load_rows(xb[4 * group + xp, 4 * xx : 4 * xx + 4], xp, gain, xx * NEAR)
        product(
            4 * NEAR,
            jnp.concatenate([columns(wgu, 4 * group + xx, 0, NEAR) for xx in range(4)], axis=1),
        )

    def multiply_far():
        for xx in range(4):
            gain = jnp.concatenate([gains[4 * i + xx][:, NEAR:] for i in range(4)], axis=1)
            for xp in range(4):
                piece = xb2[xp % 2, 4 * xx : 4 * xx + 4, xp // 2]
                load_rows(piece, xp, gain, xx * 4 * FAR)
        product(
            16 * FAR,
            jnp.concatenate(
                [columns(wgu, 4 * i + xx, NEAR, FAR) for xx in range(4) for i in range(4)], axis=1
            ),
        )

    side = jnp.where(z % 2 == 0, 3, 1)
    pair = z // 2
    def step(s):
        for part in range(2):
            for d in range(2):
                ref = half(z + (-s if d == 0 else s), k, part)
                ring(d, s - 1, part, ref).wait_recv()
                if s < 3 or part == d:
                    ring(d, s, part, ref).start()
                over(2 * s - 1 + d, ref)

    step(1)
    step(2)
    loads[0].wait()
    loads[1].wait()
    crossed(0, 0)
    crossed(1, -1)
    crossed(2, 1)
    multiply(pair)
    step(3)
    crossed(3, -2)
    crossed(4, 2)
    multiply((pair + side) % 4)
    own_far.wait()
    receive(xb2.at[k, pl.ds(0, 15)], b2r.at[0])
    hand_over = remote(xb2.at[k], xb2.at[k], os.at[0], osr.at[0], peer)
    hand_over.start()
    sends.drain_later(xb2.at[k], os.at[0])
    crossed(5, -3)
    crossed(6, 3)
    multiply((pair + 4 - side) % 4)
    for d in range(2):
        ref = half(z + 4, k, d)
        ring(d, 3, d, ref).wait_recv()
        over(7, ref)
    receive(xb2.at[1 - k], osr.at[0])
    multiply_far()
    crossed(7, 4)
    multiply((pair + 2) % 4)

    total_sq = jnp.sum(squares[...], axis=1, keepdims=True)
    scale = lax.rsqrt(total_sq / D + 1e-05)
    gate = acc[:, :HID] * scale
    lifted = acc[:, FEAT:] * scale
    act[...] = (gate / (1.0 + jnp.exp(-gate)) * lifted).astype(BF)
    loads[2].wait()

    def far_tile(lane):
        cols = jnp.concatenate([columns(wd, 2 * i + lane, NEAR, FAR) for i in range(8)], axis=1)
        return jnp.dot(act[...], cols, preferred_element_type=F32).astype(BF)

    outb[...] = far_tile(1 - k)
    swap = remote(outb, gotb, ws.at[0], wr.at[0], peer)
    swap.start()
    sends.drain_later(outb, ws.at[0])
    ownb[...] = far_tile(k)

    total = RingSum(spot, SLOTS, own, out, got, tbuf, rbuf, xs, xr, ts, tr, sends)

    def produce(i):
        chunk = (z + ORDER[i]) % 8

        def tile(lane):
            cols = columns(wd, 2 * chunk + lane, 0, NEAR)
            return jnp.dot(act[...], cols, preferred_element_type=F32).astype(BF)

        out[i] = tile(1 - k)
        own[i] = tile(k)

    total.begin(produce)
    swap.wait_recv()
    summed = ownb[...].astype(F32) + gotb[...].astype(F32)
    qsb[...] = summed.reshape(BLOCKS, CAP, 8 * FAR).astype(BF)
    own_home = pltpu.make_async_copy(qsb.at[mine], rb2.at[me], loc.at[1])
    own_home.start()
    for i in range(1, 16):
        to = (me + i) % 16
        remote(qsb.at[column_major(to)], rb2.at[me], b3s.at[0], b3r.at[0], at_ctx(to)).start()
    sends.drain_later(qsb.at[pl.ds(0, 15)], b3s.at[0])
    total.rest(produce)

    loads[3].wait()
    hit0, hit1 = slot_hits(ids_all[x])
    part_of = jnp.where(hit0, wts[0:1, :], 0.0) + jnp.where(hit1, wts[1:2, :], 0.0)
    coarse = part_of.astype(BF)
    fine = (part_of - coarse.astype(F32)).astype(BF)

    def combine(ref):
        back = ref[...].astype(F32).reshape(SLOTS, ref.shape[2]).astype(BF)
        dims = (((0,), (0,)), ((), ()))
        mixture = lax.dot_general(coarse, back, dims, preferred_element_type=F32)
        return mixture + lax.dot_general(fine, back, dims, preferred_element_type=F32)

    own_home.wait()
    receive(rb2.at[pl.ds(0, 15)], b3r.at[0])
    far_mix = combine(rb2)
    for i in range(8):
        pb[i] = far_mix[:, FAR * i : FAR * i + FAR].astype(BF)
    for i in range(1, 8):
        to = (z + i) % 8
        remote(pb.at[to], gb.at[i], b4s.at[0], b4r.at[0], (y, x, to, k)).start()
    sends.drain_later(pb.at[pl.ds(0, 7)], b4s.at[0])

    for part in range(2):
        qs[part * 8 : part * 8 + 8] = total.result(part).reshape(8, CAP, NEAR).astype(BF)
    own_back = pltpu.make_async_copy(qs.at[mine], rb.at[me], loc.at[5])
    own_back.start()
    for i in range(1, 16):
        to = (me + i) % 16
        remote(qs.at[column_major(to)], rb.at[me], qss.at[0], qsr.at[0], at_ctx(to)).start()
    sends.drain_later(qs.at[pl.ds(0, 15)], qss.at[0])

    @pl.when(low != x)
    def _():
        handed.wait()

    @pl.when(low == x)
    def _():
        kept.wait()

    far_sum = hn[:, NEAR:].astype(F32) + pb[z].astype(F32)
    receive(gb.at[pl.ds(1, 7)], b4r.at[0])
    for i in range(1, 8):
        far_sum += gb[i].astype(F32)
    o_ref[:, NEAR:] = far_sum.astype(BF)
    own_back.wait()
    receive(rb.at[pl.ds(0, 15)], qsr.at[0])
    o_ref[:, :NEAR] = (hn[:, :NEAR].astype(F32) + combine(rb)).astype(BF)


def layer(*refs):
    ins, o_ref, refs = refs[:14], refs[14], list(refs[15:])

    def take(n):
        taken = refs[:n]
        del refs[:n]
        return taken

    wg_hbm, wu_hbm, wd_hbm, wts_hbm = ins[10:]
    wgu, wd, wts, wsem = take(4)
    early = take(6)
    passed = h, ids_all, gains = take(3)
    mix_scratch = take(8)
    mix_ring = take(5)
    mix_sems = take(19)
    moe_scratch = take(20)
    moe_ring = take(5)
    moe_sems = take(27)
    loads = [
        pltpu.make_async_copy(wg_hbm, wgu.at[pl.ds(0, HID)], wsem.at[0]),
        pltpu.make_async_copy(wu_hbm, wgu.at[pl.ds(FEAT, HID)], wsem.at[1]),
        pltpu.make_async_copy(wd_hbm, wd, wsem.at[2]),
        pltpu.make_async_copy(wts_hbm, wts, wsem.at[3]),
    ]

    def start_weights():
        for cp in loads:
            cp.start()

    sends = Sends()
    mixer(
        *ins[:10], *early, *passed, *mix_scratch, *mix_ring, *mix_sems, start_weights, sends
    )
    experts(wts, wgu, wd, loads, *passed, o_ref, *moe_scratch, *moe_ring, *moe_sems, sends)
    y, x, z, k = place()
    sends.drain((y, x, z, 1 - k))


def dma(*shape):
    return pltpu.SemaphoreType.DMA(shape)


def ring_scratch(rows, width):
    half = rows // 2
    return [
        pltpu.VMEM((8, rows, width), BF),
        pltpu.VMEM((8, rows, width), BF),
        pltpu.VMEM((8, rows, width), BF),
        pltpu.VMEM((14, half, width), BF),
        pltpu.VMEM((14, half, width), BF),
    ]


ANY = pl.BlockSpec(memory_space=pl.ANY)


def shards(
    residual, query_rows, key_rows, value_rows, head_rates, doc_lengths, attn_gain, out_weight,
    moe_gain, expert_ids, expert_weights, gate_weight, up_weight, down_weight,
):
    return pl.pallas_call(
        layer,
        out_shape=jax.ShapeDtypeStruct((ROWS, FEAT), BF),
        in_specs=[ANY] * 14,
        out_specs=pl.BlockSpec(memory_space=pltpu.VMEM),
        scratch_shapes=[
            pltpu.VMEM((FEAT + HID, D), BF),
            pltpu.VMEM((HID, D), BF),
            pltpu.VMEM((2, ROWS), F32),
            dma(4),
            pltpu.SMEM((64,), F32),
            pltpu.SMEM((4,), jnp.int32),
            pltpu.VMEM((ROWS, 512), BF),
            pltpu.VMEM((ROWS, 512), BF),
            pltpu.VMEM((ROWS, 512), BF),
            pltpu.VMEM((1, 512), F32),
            pltpu.VMEM((ROWS, FEAT), BF),
            pltpu.VMEM((4, 2, ROWS), jnp.int32),
            pltpu.VMEM((16, 1, FEAT), F32),
            pltpu.VMEM((4, 512, FEAT), BF),
            pltpu.VMEM((4, ROWS, 512), BF),
            pltpu.VMEM((512, HD), BF),
            pltpu.VMEM((16, 32, HD), BF),
            pltpu.VMEM((16, 32, HD), BF),
            pltpu.VMEM((16, 32, HD), BF),
            pltpu.VMEM((ROWS, FEAT), BF),
            pltpu.VMEM((ROWS, 512), F32),
            *ring_scratch(ROWS, FEAT),
            dma(1), dma(2, 3), dma(1), dma(2, 3),
            dma(1), dma(1), dma(1), dma(1), dma(1), dma(1),
            dma(1), dma(1), dma(1), dma(1), dma(1), dma(8), dma(1), dma(14), dma(12),
            pltpu.VMEM((2, SLOTS, ROWS), BF),
            pltpu.VMEM((BLOCKS, CAP, NEAR), BF),
            pltpu.VMEM((16, BLOCKS, CAP, NEAR), BF),
            pltpu.VMEM((8, ROWS, FAR), BF),
            pltpu.VMEM((BLOCKS, 2, CAP, 4 * FAR), BF),
            pltpu.VMEM((2, BLOCKS, 2, CAP, 4 * FAR), BF),
            pltpu.VMEM((SLOTS, 16 * FAR), BF),
            pltpu.VMEM((SLOTS, FEAT + HID), F32),
            pltpu.VMEM((SLOTS, 128), F32),
            pltpu.VMEM((SLOTS, HID), BF),
            pltpu.VMEM((ROWS, FEAT), BF),
            pltpu.VMEM((BLOCKS, CAP, NEAR), BF),
            pltpu.VMEM((BLOCKS, CAP, NEAR), BF),
            pltpu.VMEM((SLOTS, 8 * FAR), BF),
            pltpu.VMEM((SLOTS, 8 * FAR), BF),
            pltpu.VMEM((SLOTS, 8 * FAR), BF),
            pltpu.VMEM((BLOCKS, CAP, 8 * FAR), BF),
            pltpu.VMEM((BLOCKS, CAP, 8 * FAR), BF),
            pltpu.VMEM((8, ROWS, FAR), BF),
            pltpu.VMEM((8, ROWS, FAR), BF),
            *ring_scratch(SLOTS, NEAR),
            dma(1), dma(1), dma(1), dma(14), dma(1), dma(8),
            dma(1), dma(1), dma(1), dma(1), dma(1), dma(8), dma(1), dma(14), dma(6),
            dma(1), dma(1), dma(1), dma(1), dma(1), dma(1), dma(1), dma(1),
            dma(1), dma(1), dma(1), dma(1),
        ],
        compiler_params=pltpu.CompilerParams(
            collective_id=0, has_side_effects=True, vmem_limit_bytes=67043328
        ),
        name="layer",
    )(
        head_rates, doc_lengths, query_rows, key_rows, value_rows, attn_gain.reshape(1, -1),
        out_weight, residual, moe_gain, expert_ids.T,
        gate_weight[0].T, up_weight[0].T, down_weight[0], expert_weights.T,
    )


def solution(mesh):
    finer = Mesh(mesh.devices.reshape(4, 4, 8, 2), AXES)
    placed = (
        P(CTX, TP), P(CTX, TP), P(CTX, TP), P(CTX, TP), P(), P(), P(TP), P(TP, CTX), P(TP),
        P(CTX, None), P(CTX, None), P(CTX, None, TP), P(CTX, None, TP), P(CTX, TP, None),
    )
    return jax.shard_map(shards, mesh=finer, in_specs=placed, out_specs=P(CTX, TP), check_vma=False)
```

```python
import jax
import jax.numpy as jnp
from jax import lax
from jax.experimental import pallas as pl
from jax.experimental.pallas import tpu as pltpu
from jax.sharding import Mesh
from jax.sharding import PartitionSpec as P

D = 6144
HD = 128
CAP = 24
BLOCKS = 16
ROWS = 128
FEAT = 384
NEAR = 256
FAR = 128
HID = 288
SLOTS = BLOCKS * CAP
CTX = ("ctx_0", "ctx_1")
TP = ("tp_0", "tp_1")
AXES = CTX + TP
ORDER = (4, 3, 5, 2, 6, 1, 7, 0)
HOPS = [(d, s, p) for d in range(2) for s in range(4) for p in range(4) if s > 0 or p // 2 == d]
STEPS = [(d, s, p) for d in range(2) for s in range(4) for p in range(2) if s < 3 or p == d]
BF = jnp.bfloat16
F32 = jnp.float32


def remote(src, dst, send_sem, recv_sem, to):
    return pltpu.make_async_remote_copy(
        src_ref=src,
        dst_ref=dst,
        send_sem=send_sem,
        recv_sem=recv_sem,
        device_id=to,
        device_id_type=pl.DeviceIdType.MESH,
    )


def place():
    return tuple(lax.axis_index(a) for a in AXES)


def partner_of(y, x, z, k):
    low = 2 * (z % 2) + k
    return low, (y, low, 2 * (z // 2) + x // 2, x % 2)


def greet(y, x, z, k):
    sem = pltpu.get_barrier_semaphore()
    for i in range(1, 16):
        c = (4 * y + x + i) % 16
        pl.semaphore_signal(
            sem, inc=1, device_id=(c // 4, c % 4, z, k), device_id_type=pl.DeviceIdType.MESH
        )
    for i in range(1, 16):
        t = (2 * z + k + i) % 16
        pl.semaphore_signal(
            sem, inc=1, device_id=(y, x, t // 2, t % 2), device_id_type=pl.DeviceIdType.MESH
        )
    low, partner = partner_of(y, x, z, k)

    @pl.when(low != x)
    def _():
        pl.semaphore_signal(sem, inc=1, device_id=partner, device_id_type=pl.DeviceIdType.MESH)

    pl.semaphore_wait(sem, 30 + ((low - x + 4) % 4 + 3) // 4)


class Sends:
    def __init__(self):
        self.open = []

    def drain_later(self, ref, sem):
        self.open.append((ref, sem))

    def drain(self, to):
        for ref, sem in self.open:
            remote(ref, ref, sem, sem, to).wait_send()


class RingGather:
    def __init__(self, buf, ssem, rsem, me, device_at, half, sends):
        self.buf, self.ssem, self.rsem = buf, ssem, rsem
        self.me, self.at, self.half = me, device_at, half
        sends.drain_later(buf.at[pl.ds(0, 3)], ssem.at[0])

    def piece(self, member, part):
        return self.buf.at[member % 4, pl.ds(part * self.half, self.half)]

    def first(self, d, part, own):
        remote(
            own.at[pl.ds(part * self.half, self.half)],
            self.piece(self.me, part),
            self.ssem.at[0],
            self.rsem.at[d, part],
            self.at((self.me + (1, -1)[d]) % 4),
        ).start()

    def along(self, d, slot, ref):
        return remote(
            ref, ref, self.ssem.at[0], self.rsem.at[d, slot], self.at((self.me + (1, -1)[d]) % 4)
        )

    def arrived(self, d, part):
        self.along(d, part, self.piece(self.me + 4 - (1, -1)[d], part)).wait_recv()

    def forward(self, d):
        self.along(d, 2, self.piece(self.me + 4 - (1, -1)[d], d)).start()

    def forwarded(self, d):
        self.along(d, 2, self.piece(self.me + 2, d)).wait_recv()


class RingSum:
    def __init__(self, spot, rows, own, out, got, tbuf, rbuf, xs, xr, ssem, rsem, sends):
        self.y, self.x, self.z, self.k = spot
        self.quarter = rows // 4
        self.own, self.out, self.got = own, out, got
        self.tbuf, self.rbuf = tbuf, rbuf
        self.xs, self.xr, self.ssem, self.rsem = xs, xr, ssem, rsem
        sends.drain_later(out, xs.at[0])
        sends.drain_later(tbuf, ssem.at[0])

    def swap(self, i):
        self.swapping(i).start()

    def swapping(self, i):
        return remote(
            self.out.at[i],
            self.got.at[i],
            self.xs.at[0],
            self.xr.at[i],
            (self.y, self.x, self.z, 1 - self.k),
        )

    def swapped(self, i):
        self.swapping(i).wait_recv()

    def local(self, i, part):
        rows = pl.ds(part * self.quarter, self.quarter)
        return self.own[i, rows, :].astype(F32) + self.got[i, rows, :].astype(F32)

    def hop(self, d, s, part):
        to = (self.z + (1, 7)[d]) % 8
        return remote(
            self.tbuf.at[HOPS.index((d, s, part))],
            self.rbuf.at[HOPS.index((d, s, part))],
            self.ssem.at[0],
            self.rsem.at[HOPS.index((d, s, part))],
            (self.y, self.x, to, self.k),
        )

    def send(self, d, s, part, value):
        self.tbuf[HOPS.index((d, s, part))] = value.astype(BF)
        self.hop(d, s, part).start()

    def came(self, d, s, part):
        return self.rbuf[HOPS.index((d, s, part))].astype(F32)

    def begin(self, tile, aside=None, later=None):
        self.make(tile, 0)
        self.out[1] = tile(1, False)
        self.swap(1)
        if aside:
            aside()
        self.swapped(0)
        for j in range(2):
            for d in range(2):
                self.send(d, 0, 2 * d + j, self.local(0, 2 * d + j))
        self.own[1] = tile(1, True)
        self.make(tile, 2)
        if later:
            later()
        for d in range(2):
            self.swapped(1 + d)
            for j in range(2):
                part = 2 * (1 - d) + j
                self.send(d, 1, part, self.local(1 + d, part))

    def make(self, tile, i):
        self.out[i] = tile(i, False)
        self.swap(i)
        self.own[i] = tile(i, True)

    def rest(self, tile):
        for s in (1, 2, 3):
            for i in range(2 * s + 1, min(2 * s + 3, 8)):
                self.make(tile, i)
            if s > 1:
                self.swapped(2 * s - 1)
                self.swapped(2 * s)
            for j in range(4):
                for d in range(2):
                    part = (j + 2 * (1 - d)) % 4
                    if s == 1 and part // 2 != d:
                        continue
                    self.hop(d, s - 1, part).wait_recv()
                    value = self.local(2 * s - 1 + d, part) + self.came(d, s - 1, part)
                    self.send(d, s, part, value)
        self.swapped(7)

    def result(self, part):
        self.hop(0, 3, part).wait_recv()
        self.hop(1, 3, part).wait_recv()
        return (
            self.local(7, part)
            + self.came(0, 3, part)
            + self.came(1, 3, part)
        )


def mixer(
    rates_hbm, docs_hbm, q_hbm, k_hbm, v_hbm, again_hbm, w, res, mgain, ids,
    rates, docs, q, k_in, v, again,
    h_out, ids_all, gain_out,
    wbuf, hbuf, state, arrived, onward, incoming, resbuf, within,
    own, out, got, tbuf, rbuf,
    wss, wrs, hss, hrs, a1s, a1r, a2s, a2r, gs, gr, ps, pr, ids_s, ids_r, xs, xr, ts, tr, loc, start_weights, sends,
):
    spot = y, x, z, k = place()
    me, t = 4 * y + x, 2 * z + k
    low, partner = partner_of(*spot)
    loads = [
        pltpu.make_async_copy(a, b, loc.at[6 + i])
        for i, (a, b) in enumerate(
            (
                (k_hbm, k_in), (v_hbm, v), (rates_hbm, rates), (docs_hbm, docs), (q_hbm, q),
                (again_hbm, again),
            )
        )
    ]
    for cp in loads:
        cp.start()
    greet(*spot)

    weights = RingGather(wbuf, wss, wrs, y, lambda i: (i, x, z, k), 256, sends)
    heads = RingGather(hbuf, hss, hrs, x, lambda i: (y, i, z, k), 64, sends)
    own_w = pltpu.make_async_copy(w, wbuf.at[y], loc.at[0])
    own_w.start()

    handed = remote(res, resbuf, ps.at[0], pr.at[0], partner)
    kept = pltpu.make_async_copy(res, resbuf, loc.at[1])

    @pl.when(low != x)
    def _():
        handed.start()

    @pl.when(low == x)
    def _():
        kept.start()

    own_ids = pltpu.make_async_copy(ids, ids_all.at[x], loc.at[2])
    own_ids.start()
    for i in range(1, 4):
        remote(ids, ids_all.at[x], ids_s.at[0], ids_r.at[0], (y, (x + i) % 4, z, k)).start()
    sends.drain_later(ids_all.at[pl.ds(0, 3)], ids_s.at[0])

    own_gain = pltpu.make_async_copy(mgain, gain_out.at[t, 0], loc.at[3])
    own_gain.start()
    for i in range(1, 16):
        to = (t + i) % 16
        remote(mgain, gain_out.at[t, 0], gs.at[0], gr.at[0], (y, x, to // 2, to % 2)).start()
    sends.drain_later(gain_out.at[pl.ds(0, 15)], gs.at[0])

    start_weights()
    for cp in loads[:4]:
        cp.wait()
    start1 = docs[0]
    start2 = start1 + docs[1]
    start3 = start2 + docs[2]

    def seg(p):
        def past(s):
            return jnp.where(p >= s, 1, 0)

        base = jnp.where(p >= 0, 0, -1)
        return base + past(start1) + past(start2) + past(start3)

    first = me * ROWS
    last_seg = seg(first + ROWS - 1)
    before = seg(first - 1)
    row = lax.broadcasted_iota(jnp.int32, (ROWS, HD), 0)
    col = lax.broadcasted_iota(jnp.int32, (ROWS, HD), 1)
    seg_row, seg_col = seg(first + row), seg(first + col)
    rowf = row.astype(F32)
    at_end = jnp.where(seg_row == last_seg, 1.0, 0.0)
    for h in range(4):
        rate = rates[4 * t + h]
        cols = slice(h * HD, (h + 1) * HD)
        fading = at_end * jnp.exp(-rate * (ROWS - 1.0 - rowf))
        faded = (k_in[:, cols].astype(F32) * fading).astype(BF)
        state[h * HD : (h + 1) * HD, :] = lax.dot_general(
            faded, v[:, cols], (((0,), (0,)), ((), ())), preferred_element_type=F32
        ).astype(BF)

    own_state = pltpu.make_async_copy(
        state.at[pl.ds(pl.multiple_of(me * 32, 32), 32)], arrived.at[me], loc.at[4]
    )
    own_state.start()
    for i in range(1, 16):
        to = (me + i) % 16
        remote(
            state.at[pl.ds(pl.multiple_of(to * 32, 32), 32)],
            arrived.at[me],
            a1s.at[0],
            a1r.at[0],
            (to // 4, to % 4, z, k),
        ).start()
    sends.drain_later(arrived.at[pl.ds(0, 15)], a1s.at[0])
    weights.first(0, 0, w)
    weights.first(1, 1, w)

    loads[4].wait()
    loads[5].wait()
    allowed = jnp.where((row >= col) & (seg_row == seg_col), 1.0, 0.0)
    gap = jnp.maximum(row - col, 0).astype(F32)
    for h in range(4):
        rate = rates[4 * t + h]
        cols = slice(h * HD, (h + 1) * HD)
        scores = lax.dot_general(
            q[:, cols], k_in[:, cols], (((1,), (1,)), ((), ())), preferred_element_type=F32
        )
        mixed = (scores * (allowed * jnp.exp(-rate * gap))).astype(BF)
        within[:, cols] = jnp.dot(mixed, v[:, cols], preferred_element_type=F32)

    own_state.wait()
    peer = (y, x, z, 1 - k)

    def receive(ref, sem):
        remote(ref, ref, sem, sem, peer).wait_recv()

    receive(arrived.at[pl.ds(0, 15)], a1r.at[0])
    decay = jnp.exp(jnp.zeros((32, HD), F32) - rates[4 * t + y] * ROWS)
    running = jnp.zeros((32, HD), F32)
    for b in range(BLOCKS):
        onward[b] = running.astype(BF)
        same = seg(jnp.int32(b * ROWS + ROWS - 1)) == seg(jnp.int32(b * ROWS - 1))
        running = running * (decay * jnp.where(same, 1.0, 0.0)) + arrived[b].astype(F32)
    own_onward = pltpu.make_async_copy(onward.at[me], incoming.at[me], loc.at[5])
    own_onward.start()
    for i in range(1, 16):
        to = (me + i) % 16
        remote(
            onward.at[to], incoming.at[me], a2s.at[0], a2r.at[0], (to // 4, to % 4, z, k)
        ).start()
    sends.drain_later(onward.at[pl.ds(0, 15)], a2s.at[0])
    for d in range(2):
        weights.arrived(d, d)
        weights.forward(d)
    for d in range(2):
        weights.first(d, 1 - d, w)
    own_onward.wait()
    receive(incoming.at[pl.ds(0, 15)], a2r.at[0])

    reached = jnp.where(seg_row == before, 1.0, 0.0)
    for h in range(4):
        rate = rates[4 * t + h]
        cols = slice(h * HD, (h + 1) * HD)
        inc = incoming[4 * h : 4 * h + 4].reshape(HD, HD)
        inter = jnp.dot(q[:, cols], inc, preferred_element_type=F32)
        both = within[:, cols] + inter * (reached * jnp.exp(-rate * (rowf + 1.0)))
        scale = lax.rsqrt(jnp.mean(both * both, axis=1, keepdims=True) + 1e-06)
        within[:, cols] = both * scale * again[:, cols]
    hbuf[x] = within[...].astype(BF)
    for part in range(2):
        for d in range(2):
            heads.first(d, part if d == 0 else 1 - part, hbuf.at[x])
    for d in range(2):
        heads.arrived(d, d)
        heads.forward(d)
    for d in range(2):
        heads.arrived(d, 1 - d)
    own_w.wait()
    for d in range(2):
        weights.arrived(d, 1 - d)
        weights.forwarded(d)
    for d in range(2):
        heads.forwarded(d)

    total = RingSum(spot, ROWS, own, out, got, tbuf, rbuf, xs, xr, ts, tr, sends)

    def tile(i, mine):
        chunk = (z + ORDER[i]) % 8
        row = 2 * (chunk % 2) + (k if mine else 1 - k)
        return jnp.dot(hbuf[row], wbuf[chunk // 2], preferred_element_type=F32).astype(BF)

    total.begin(tile)
    total.rest(tile)

    @pl.when(low != x)
    def _():
        handed.wait()

    @pl.when(low == x)
    def _():
        kept.wait()

    for part in range(4):
        rows = slice(part * 32, part * 32 + 32)
        h_out[rows, :] = (resbuf[rows, :].astype(F32) + total.result(part)).astype(BF)
    own_gain.wait()
    receive(gain_out.at[pl.ds(0, 15)], gr.at[0])
    own_ids.wait()
    receive(ids_all.at[pl.ds(0, 3)], ids_r.at[0])


def slot_hits(ids):
    expert = lax.broadcasted_iota(jnp.int32, (BLOCKS, CAP, ROWS), 0).reshape(SLOTS, ROWS)
    place_in = lax.broadcasted_iota(jnp.int32, (BLOCKS, CAP, ROWS), 1).reshape(SLOTS, ROWS)
    hit0 = expert == ids[0:1, :]
    hit1 = expert == ids[1:2, :]
    named = jnp.where(hit0 | hit1, 1.0, 0.0)
    earlier = lax.broadcasted_iota(jnp.int32, (ROWS, ROWS), 0)
    later = lax.broadcasted_iota(jnp.int32, (ROWS, ROWS), 1)
    rank = jnp.dot(
        named.astype(BF),
        jnp.where(earlier < later, 1.0, 0.0).astype(BF),
        preferred_element_type=F32,
    )
    here = rank == place_in.astype(F32)
    return hit0 & here, hit1 & here


def experts(
    wts, wgu, wd, loads, h, ids_all, gains,
    o_ref,
    pick, ds, xb, hz, dsb, xb2, lhs, acc, squares, act, hn, qs, rb,
    ownb, outb, gotb, qsb, rb2, pb, gb,
    own, out, got, tbuf, rbuf,
    dss, dsr, fs, fr, cs, cr, qss, qsr, ps, pr, xs, xr, ts, tr, loc,
    b1s, b1r, b2s, b2r, os, osr, ws, wr, b3s, b3r, b4s, b4r,
    sends,
):
    spot = y, x, z, k = place()
    me, t = 4 * y + x, 2 * z + k
    low, partner = partner_of(*spot)
    peer = (y, x, z, 1 - k)

    def receive(ref, sem):
        remote(ref, ref, sem, sem, peer).wait_recv()

    def at_ctx(c):
        return (c // 4, c % 4, z, k)

    def column_major(c):
        return 4 * (c % 4) + c // 4

    hz[z] = h[:, NEAR:]
    def along_z(ref, dist, sem):
        remote(ref, ref, b1s.at[0], b1r.at[sem], (y, x, (z + dist) % 8, k)).start()

    for dist, sem in ((2, 0), (6, 1), (1, 2), (7, 2)):
        along_z(hz.at[z], dist, sem)
    sends.drain_later(hz.at[pl.ds(0, 7)], b1s.at[0])

    for j in range(2):
        hit0, hit1 = slot_hits(ids_all[2 * j + k])
        pick[j] = jnp.where(hit0 | hit1, 1.0, 0.0).astype(BF)
    picked = jnp.dot(pick[z % 2], h[:, :NEAR], preferred_element_type=F32)
    ds[...] = picked.reshape(BLOCKS, CAP, NEAR).astype(BF)

    mine = 4 * x + y
    own_rows = pltpu.make_async_copy(ds.at[me], xb.at[t, mine], loc.at[3])
    own_rows.start()
    for i in range(1, 16):
        to = (me + i) % 16
        remote(ds.at[to], xb.at[t, mine], dss.at[0], dsr.at[0], at_ctx(to)).start()
    sends.drain_later(ds.at[pl.ds(0, 15)], dss.at[0])
    handed = remote(h, hn, ps.at[0], pr.at[0], partner)
    kept = pltpu.make_async_copy(h, hn, loc.at[4])
    for sem, dist in ((0, 6), (1, 2)):
        spot_z = (z + dist) % 8
        receive(hz.at[spot_z], b1r.at[sem])
        along_z(hz.at[spot_z], (1, 7)[sem], 2)
        along_z(hz.at[spot_z, pl.ds(64 * sem, 64)], (2, 6)[sem], 2)
    own_rows.wait()
    receive(xb.at[t, pl.ds(0, 15)], dsr.at[0])

    def half(zz, kk, part):
        return xb.at[2 * ((zz + 8) % 8) + kk, pl.ds(part * 8, 8)]

    def ring(d, s, part, ref):
        to = (z + (1, 7)[d]) % 8
        return remote(
            ref, ref, fs.at[0], fr.at[STEPS.index((d, s, part))], (y, x, to, k)
        )

    def over(slot, ref):
        remote(ref, ref, cs.at[0], cr.at[slot], peer).start()

    def crossed(slot, dist):
        receive(xb.at[2 * ((z + dist + 8) % 8) + 1 - k], cr.at[slot])

    sends.drain_later(xb.at[pl.ds(0, 7)], fs.at[0])
    sends.drain_later(xb.at[pl.ds(0, 8)], cs.at[0])
    for part in range(2):
        ref = half(z, k, part)
        ring(0, 0, part, ref).start()
        ring(1, 0, part, ref).start()
        over(0, ref)

    receive(hz.at[pl.ds(0, 5)], b1r.at[2])
    for j in range(2):
        wide = jnp.concatenate([hz[2 * i + j] for i in range(4)], axis=1)
        chosen = jnp.dot(pick[j], wide, preferred_element_type=F32)
        dsb[:, j] = chosen.reshape(BLOCKS, CAP, 4 * FAR).astype(BF)
    own_far = pltpu.make_async_copy(dsb.at[me], xb2.at[k, mine], loc.at[0])
    own_far.start()
    for i in range(1, 16):
        to = (me + i) % 16
        remote(dsb.at[to], xb2.at[k, mine], b2s.at[0], b2r.at[0], at_ctx(to)).start()
    sends.drain_later(dsb.at[pl.ds(0, 15)], b2s.at[0])

    wgu[HID:FEAT, :] = jnp.zeros((FEAT - HID, D), BF)
    acc[...] = jnp.zeros_like(acc)
    squares[...] = jnp.zeros_like(squares)

    def columns(ref, tile, first, width):
        return ref[:, pl.ds(pl.multiple_of(tile * FEAT + first, 128), width)]

    def load_rows(piece, xp, gain, first):
        rows = slice(96 * xp, 96 * xp + 96)
        width = gain.shape[1]
        piece = piece.astype(F32).reshape(96, width)
        sq = piece * piece
        add = sq[:, 0:128]
        for i in range(1, width // 128):
            add += sq[:, 128 * i : 128 * i + 128]
        squares[rows, :] += add
        lhs[rows, first : first + width] = (piece * gain).astype(BF)

    def product(depth, w):
        acc[...] += lax.dot_general(
            lhs[:, :depth], w, (((1,), (1,)), ((), ())), preferred_element_type=F32
        )

    def multiply(group):
        for xx in range(4):
            gain = gains[4 * group + xx][:, :NEAR]
            for xp in range(4):
                load_rows(xb[4 * group + xp, 4 * xx : 4 * xx + 4], xp, gain, xx * NEAR)
        product(
            4 * NEAR,
            jnp.concatenate([columns(wgu, 4 * group + xx, 0, NEAR) for xx in range(4)], axis=1),
        )

    def multiply_far():
        for xx in range(4):
            gain = jnp.concatenate([gains[4 * i + xx][:, NEAR:] for i in range(4)], axis=1)
            for xp in range(4):
                piece = xb2[xp % 2, 4 * xx : 4 * xx + 4, xp // 2]
                load_rows(piece, xp, gain, xx * 4 * FAR)
        product(
            16 * FAR,
            jnp.concatenate(
                [columns(wgu, 4 * i + xx, NEAR, FAR) for xx in range(4) for i in range(4)], axis=1
            ),
        )

    side = jnp.where(z % 2 == 0, 3, 1)
    pair = z // 2
    def step(s):
        for part in range(2):
            for d in range(2):
                ref = half(z + (-s if d == 0 else s), k, part)
                ring(d, s - 1, part, ref).wait_recv()
                if s < 3 or part == d:
                    ring(d, s, part, ref).start()
                over(2 * s - 1 + d, ref)

    step(1)
    step(2)
    loads[0].wait()
    loads[1].wait()
    crossed(0, 0)
    crossed(1, -1)
    crossed(2, 1)
    multiply(pair)
    step(3)

    @pl.when(low != x)
    def _():
        handed.start()

    @pl.when(low == x)
    def _():
        kept.start()

    own_far.wait()
    receive(xb2.at[k, pl.ds(0, 15)], b2r.at[0])
    remote(xb2.at[k], xb2.at[k], os.at[0], osr.at[0], peer).start()
    sends.drain_later(xb2.at[k], os.at[0])
    crossed(3, -2)
    crossed(4, 2)
    multiply((pair + side) % 4)
    crossed(5, -3)
    crossed(6, 3)
    multiply((pair + 4 - side) % 4)
    for d in range(2):
        ref = half(z + 4, k, d)
        ring(d, 3, d, ref).wait_recv()
        over(7, ref)
    receive(xb2.at[1 - k], osr.at[0])
    multiply_far()
    crossed(7, 4)
    multiply((pair + 2) % 4)

    total_sq = jnp.sum(squares[...], axis=1, keepdims=True)
    scale = lax.rsqrt(total_sq / D + 1e-05)
    gate = acc[:, :HID] * scale
    lifted = acc[:, FEAT:] * scale
    act[...] = (gate / (1.0 + jnp.exp(-gate)) * lifted).astype(BF)
    loads[2].wait()

    def far_tile(lane):
        cols = jnp.concatenate([columns(wd, 2 * i + lane, NEAR, FAR) for i in range(8)], axis=1)
        return jnp.dot(act[...], cols, preferred_element_type=F32).astype(BF)

    swap = remote(outb, gotb, ws.at[0], wr.at[0], peer)
    sends.drain_later(outb, ws.at[0])

    def aside():
        outb[...] = far_tile(1 - k)
        swap.start()

    def later():
        ownb[...] = far_tile(k)

    total = RingSum(spot, SLOTS, own, out, got, tbuf, rbuf, xs, xr, ts, tr, sends)

    def tile(i, mine):
        chunk = (z + ORDER[i]) % 8
        cols = columns(wd, 2 * chunk + (k if mine else 1 - k), 0, NEAR)
        return jnp.dot(act[...], cols, preferred_element_type=F32).astype(BF)

    total.begin(tile, aside, later)
    swap.wait_recv()
    summed = ownb[...].astype(F32) + gotb[...].astype(F32)
    qsb[...] = summed.reshape(BLOCKS, CAP, 8 * FAR).astype(BF)
    own_home = pltpu.make_async_copy(qsb.at[mine], rb2.at[me], loc.at[1])
    own_home.start()
    for i in range(1, 16):
        to = (me + i) % 16
        remote(qsb.at[column_major(to)], rb2.at[me], b3s.at[0], b3r.at[0], at_ctx(to)).start()
    sends.drain_later(qsb.at[pl.ds(0, 15)], b3s.at[0])
    total.rest(tile)

    loads[3].wait()
    hit0, hit1 = slot_hits(ids_all[x])
    part_of = jnp.where(hit0, wts[0:1, :], 0.0) + jnp.where(hit1, wts[1:2, :], 0.0)
    coarse = part_of.astype(BF)
    fine = (part_of - coarse.astype(F32)).astype(BF)

    def combine(ref):
        back = ref[...].astype(F32).reshape(SLOTS, ref.shape[2]).astype(BF)
        dims = (((0,), (0,)), ((), ()))
        mixture = lax.dot_general(coarse, back, dims, preferred_element_type=F32)
        return mixture + lax.dot_general(fine, back, dims, preferred_element_type=F32)

    own_home.wait()
    receive(rb2.at[pl.ds(0, 15)], b3r.at[0])
    far_mix = combine(rb2)
    for i in range(8):
        pb[i] = far_mix[:, FAR * i : FAR * i + FAR].astype(BF)
    for i in range(1, 8):
        to = (z + i) % 8
        remote(pb.at[to], gb.at[i], b4s.at[0], b4r.at[0], (y, x, to, k)).start()
    sends.drain_later(pb.at[pl.ds(0, 7)], b4s.at[0])

    own_back = pltpu.make_async_copy(qs.at[mine], rb.at[me], loc.at[5])
    for part in range(4):
        qs[part * 4 : part * 4 + 4] = total.result(part).reshape(4, CAP, NEAR).astype(BF)
        for i in range(4):
            row = (y + i) % 4
            home = remote(
                qs.at[4 * part + row], rb.at[me], qss.at[0], qsr.at[0], (row, part, z, k)
            )
            if i > 0:
                home.start()
            else:
                pl.when(part != x)(home.start)
                pl.when(part == x)(own_back.start)
    sends.drain_later(qs.at[pl.ds(0, 15)], qss.at[0])

    @pl.when(low != x)
    def _():
        handed.wait()

    @pl.when(low == x)
    def _():
        kept.wait()

    far_sum = hn[:, NEAR:].astype(F32) + pb[z].astype(F32)
    receive(gb.at[pl.ds(1, 7)], b4r.at[0])
    for i in range(1, 8):
        far_sum += gb[i].astype(F32)
    o_ref[:, NEAR:] = far_sum.astype(BF)
    own_back.wait()
    receive(rb.at[pl.ds(0, 15)], qsr.at[0])
    o_ref[:, :NEAR] = (hn[:, :NEAR].astype(F32) + combine(rb)).astype(BF)


def layer(*refs):
    ins, o_ref, refs = refs[:14], refs[14], list(refs[15:])

    def take(n):
        taken = refs[:n]
        del refs[:n]
        return taken

    wg_hbm, wu_hbm, wd_hbm, wts_hbm = ins[10:]
    wgu, wd, wts, wsem = take(4)
    early = take(6)
    passed = h, ids_all, gains = take(3)
    mix_scratch = take(8)
    mix_ring = take(5)
    mix_sems = take(19)
    moe_scratch = take(20)
    moe_ring = take(5)
    moe_sems = take(27)
    loads = [
        pltpu.make_async_copy(wg_hbm, wgu.at[pl.ds(0, HID)], wsem.at[0]),
        pltpu.make_async_copy(wu_hbm, wgu.at[pl.ds(FEAT, HID)], wsem.at[1]),
        pltpu.make_async_copy(wd_hbm, wd, wsem.at[2]),
        pltpu.make_async_copy(wts_hbm, wts, wsem.at[3]),
    ]

    def start_weights():
        for cp in loads:
            cp.start()

    sends = Sends()
    mixer(
        *ins[:10], *early, *passed, *mix_scratch, *mix_ring, *mix_sems, start_weights, sends
    )
    experts(wts, wgu, wd, loads, *passed, o_ref, *moe_scratch, *moe_ring, *moe_sems, sends)
    y, x, z, k = place()
    sends.drain((y, x, z, 1 - k))


def dma(*shape):
    return pltpu.SemaphoreType.DMA(shape)


def ring_scratch(rows, width):
    quarter = rows // 4
    return [
        pltpu.VMEM((8, rows, width), BF),
        pltpu.VMEM((8, rows, width), BF),
        pltpu.VMEM((8, rows, width), BF),
        pltpu.VMEM((28, quarter, width), BF),
        pltpu.VMEM((28, quarter, width), BF),
    ]


ANY = pl.BlockSpec(memory_space=pl.ANY)


def shards(
    residual, query_rows, key_rows, value_rows, head_rates, doc_lengths, attn_gain, out_weight,
    moe_gain, expert_ids, expert_weights, gate_weight, up_weight, down_weight,
):
    return pl.pallas_call(
        layer,
        out_shape=jax.ShapeDtypeStruct((ROWS, FEAT), BF),
        in_specs=[ANY] * 14,
        out_specs=pl.BlockSpec(memory_space=pltpu.VMEM),
        scratch_shapes=[
            pltpu.VMEM((FEAT + HID, D), BF),
            pltpu.VMEM((HID, D), BF),
            pltpu.VMEM((2, ROWS), F32),
            dma(4),
            pltpu.SMEM((64,), F32),
            pltpu.SMEM((4,), jnp.int32),
            pltpu.VMEM((ROWS, 512), BF),
            pltpu.VMEM((ROWS, 512), BF),
            pltpu.VMEM((ROWS, 512), BF),
            pltpu.VMEM((1, 512), F32),
            pltpu.VMEM((ROWS, FEAT), BF),
            pltpu.VMEM((4, 2, ROWS), jnp.int32),
            pltpu.VMEM((16, 1, FEAT), F32),
            pltpu.VMEM((4, 512, FEAT), BF),
            pltpu.VMEM((4, ROWS, 512), BF),
            pltpu.VMEM((512, HD), BF),
            pltpu.VMEM((16, 32, HD), BF),
            pltpu.VMEM((16, 32, HD), BF),
            pltpu.VMEM((16, 32, HD), BF),
            pltpu.VMEM((ROWS, FEAT), BF),
            pltpu.VMEM((ROWS, 512), F32),
            *ring_scratch(ROWS, FEAT),
            dma(1), dma(2, 3), dma(1), dma(2, 3),
            dma(1), dma(1), dma(1), dma(1), dma(1), dma(1),
            dma(1), dma(1), dma(1), dma(1), dma(1), dma(8), dma(1), dma(28), dma(12),
            pltpu.VMEM((2, SLOTS, ROWS), BF),
            pltpu.VMEM((BLOCKS, CAP, NEAR), BF),
            pltpu.VMEM((16, BLOCKS, CAP, NEAR), BF),
            pltpu.VMEM((8, ROWS, FAR), BF),
            pltpu.VMEM((BLOCKS, 2, CAP, 4 * FAR), BF),
            pltpu.VMEM((2, BLOCKS, 2, CAP, 4 * FAR), BF),
            pltpu.VMEM((SLOTS, 16 * FAR), BF),
            pltpu.VMEM((SLOTS, FEAT + HID), F32),
            pltpu.VMEM((SLOTS, 128), F32),
            pltpu.VMEM((SLOTS, HID), BF),
            pltpu.VMEM((ROWS, FEAT), BF),
            pltpu.VMEM((BLOCKS, CAP, NEAR), BF),
            pltpu.VMEM((BLOCKS, CAP, NEAR), BF),
            pltpu.VMEM((SLOTS, 8 * FAR), BF),
            pltpu.VMEM((SLOTS, 8 * FAR), BF),
            pltpu.VMEM((SLOTS, 8 * FAR), BF),
            pltpu.VMEM((BLOCKS, CAP, 8 * FAR), BF),
            pltpu.VMEM((BLOCKS, CAP, 8 * FAR), BF),
            pltpu.VMEM((8, ROWS, FAR), BF),
            pltpu.VMEM((8, ROWS, FAR), BF),
            *ring_scratch(SLOTS, NEAR),
            dma(1), dma(1), dma(1), dma(14), dma(1), dma(8),
            dma(1), dma(1), dma(1), dma(1), dma(1), dma(8), dma(1), dma(28), dma(6),
            dma(1), dma(3), dma(1), dma(1), dma(1), dma(1), dma(1), dma(1),
            dma(1), dma(1), dma(1), dma(1),
        ],
        compiler_params=pltpu.CompilerParams(
            collective_id=0, has_side_effects=True, vmem_limit_bytes=67043328
        ),
        name="layer",
    )(
        head_rates, doc_lengths, query_rows, key_rows, value_rows, attn_gain.reshape(1, -1),
        out_weight, residual, moe_gain, expert_ids.T,
        gate_weight[0].T, up_weight[0].T, down_weight[0], expert_weights.T,
    )


def solution(mesh):
    finer = Mesh(mesh.devices.reshape(4, 4, 8, 2), AXES)
    placed = (
        P(CTX, TP), P(CTX, TP), P(CTX, TP), P(CTX, TP), P(), P(), P(TP), P(TP, CTX), P(TP),
        P(CTX, None), P(CTX, None), P(CTX, None, TP), P(CTX, None, TP), P(CTX, TP, None),
    )
    return jax.shard_map(shards, mesh=finer, in_specs=placed, out_specs=P(CTX, TP), check_vma=False)
```

```python
import jax
import jax.numpy as jnp
from jax import lax
from jax.experimental import pallas as pl
from jax.experimental.pallas import tpu as pltpu
from jax.sharding import Mesh
from jax.sharding import PartitionSpec as P

D = 6144
HD = 128
CAP = 24
BLOCKS = 16
ROWS = 128
FEAT = 384
NEAR = 256
FAR = 128
HID = 288
SLOTS = BLOCKS * CAP
CTX = ("ctx_0", "ctx_1")
TP = ("tp_0", "tp_1")
AXES = CTX + TP
ORDER = (4, 3, 5, 2, 6, 1, 7, 0)
HOPS = [(d, s, p) for d in range(2) for s in range(4) for p in range(4) if s > 0 or p // 2 == d]
STEPS = [(d, s, p) for d in range(2) for s in range(4) for p in range(2) if s < 3 or p == d]
OFFSETS = sorted(
    ((dy, dx) for dy in range(4) for dx in range(4) if dy or dx),
    key=lambda o: -(min(o[0], 4 - o[0]) + min(o[1], 4 - o[1])),
)
BF = jnp.bfloat16
F32 = jnp.float32


def remote(src, dst, send_sem, recv_sem, to):
    return pltpu.make_async_remote_copy(
        src_ref=src,
        dst_ref=dst,
        send_sem=send_sem,
        recv_sem=recv_sem,
        device_id=to,
        device_id_type=pl.DeviceIdType.MESH,
    )


def place():
    return tuple(lax.axis_index(a) for a in AXES)


def others(y, x):
    return [((y + dy) % 4, (x + dx) % 4) for dy, dx in OFFSETS]


def partner_of(y, x, z, k):
    low = 2 * (z % 2) + k
    return low, (y, low, 2 * (z // 2) + x // 2, x % 2)


def greet(y, x, z, k):
    sem = pltpu.get_barrier_semaphore()
    for i in range(1, 16):
        c = (4 * y + x + i) % 16
        pl.semaphore_signal(
            sem, inc=1, device_id=(c // 4, c % 4, z, k), device_id_type=pl.DeviceIdType.MESH
        )
    for i in range(1, 16):
        t = (2 * z + k + i) % 16
        pl.semaphore_signal(
            sem, inc=1, device_id=(y, x, t // 2, t % 2), device_id_type=pl.DeviceIdType.MESH
        )
    low, partner = partner_of(y, x, z, k)

    @pl.when(low != x)
    def _():
        pl.semaphore_signal(sem, inc=1, device_id=partner, device_id_type=pl.DeviceIdType.MESH)

    pl.semaphore_wait(sem, 30 + ((low - x + 4) % 4 + 3) // 4)


class Sends:
    def __init__(self):
        self.open = []

    def drain_later(self, ref, sem):
        self.open.append((ref, sem))

    def drain(self, to):
        for ref, sem in self.open:
            remote(ref, ref, sem, sem, to).wait_send()


class RingGather:
    def __init__(self, buf, ssem, rsem, me, device_at, half, sends):
        self.buf, self.ssem, self.rsem = buf, ssem, rsem
        self.me, self.at, self.half = me, device_at, half
        sends.drain_later(buf.at[pl.ds(0, 3)], ssem.at[0])

    def piece(self, member, part):
        return self.buf.at[member % 4, pl.ds(part * self.half, self.half)]

    def first(self, d, part, own):
        remote(
            own.at[pl.ds(part * self.half, self.half)],
            self.piece(self.me, part),
            self.ssem.at[0],
            self.rsem.at[d, part],
            self.at((self.me + (1, -1)[d]) % 4),
        ).start()

    def along(self, d, slot, ref):
        return remote(
            ref, ref, self.ssem.at[0], self.rsem.at[d, slot], self.at((self.me + (1, -1)[d]) % 4)
        )

    def arrived(self, d, part):
        self.along(d, part, self.piece(self.me + 4 - (1, -1)[d], part)).wait_recv()

    def forward(self, d):
        self.along(d, 2, self.piece(self.me + 4 - (1, -1)[d], d)).start()

    def forwarded(self, d):
        self.along(d, 2, self.piece(self.me + 2, d)).wait_recv()


class RingSum:
    def __init__(self, spot, rows, own, out, got, tbuf, rbuf, xs, xr, ssem, rsem, sends):
        self.y, self.x, self.z, self.k = spot
        self.quarter = rows // 4
        self.own, self.out, self.got = own, out, got
        self.tbuf, self.rbuf = tbuf, rbuf
        self.xs, self.xr, self.ssem, self.rsem = xs, xr, ssem, rsem
        sends.drain_later(out, xs.at[0])
        sends.drain_later(tbuf, ssem.at[0])

    def swap(self, i):
        self.swapping(i).start()

    def swapping(self, i):
        return remote(
            self.out.at[i],
            self.got.at[i],
            self.xs.at[0],
            self.xr.at[i],
            (self.y, self.x, self.z, 1 - self.k),
        )

    def swapped(self, i):
        self.swapping(i).wait_recv()

    def local(self, i, part):
        rows = pl.ds(part * self.quarter, self.quarter)
        return self.own[i, rows, :].astype(F32) + self.got[i, rows, :].astype(F32)

    def hop(self, d, s, part):
        to = (self.z + (1, 7)[d]) % 8
        return remote(
            self.tbuf.at[HOPS.index((d, s, part))],
            self.rbuf.at[HOPS.index((d, s, part))],
            self.ssem.at[0],
            self.rsem.at[HOPS.index((d, s, part))],
            (self.y, self.x, to, self.k),
        )

    def send(self, d, s, part, value):
        self.tbuf[HOPS.index((d, s, part))] = value.astype(BF)
        self.hop(d, s, part).start()

    def came(self, d, s, part):
        return self.rbuf[HOPS.index((d, s, part))].astype(F32)

    def begin(self, tile, aside=None, later=None):
        self.make(tile, 0)
        self.out[1] = tile(1, False)
        self.swap(1)
        if aside:
            aside()
        self.swapped(0)
        for j in range(2):
            for d in range(2):
                self.send(d, 0, 2 * d + j, self.local(0, 2 * d + j))
        self.own[1] = tile(1, True)
        self.make(tile, 2)
        if later:
            later()
        for d in range(2):
            self.swapped(1 + d)
            for j in range(2):
                part = 2 * (1 - d) + j
                self.send(d, 1, part, self.local(1 + d, part))

    def make(self, tile, i):
        self.out[i] = tile(i, False)
        self.swap(i)
        self.own[i] = tile(i, True)

    def rest(self, tile):
        for s in (1, 2, 3):
            for i in range(2 * s + 1, min(2 * s + 3, 8)):
                self.make(tile, i)
            if s > 1:
                self.swapped(2 * s - 1)
                self.swapped(2 * s)
            for j in range(4):
                for d in range(2):
                    part = (j + 2 * (1 - d)) % 4
                    if s == 1 and part // 2 != d:
                        continue
                    self.hop(d, s - 1, part).wait_recv()
                    value = self.local(2 * s - 1 + d, part) + self.came(d, s - 1, part)
                    self.send(d, s, part, value)
        self.swapped(7)

    def result(self, part):
        self.hop(0, 3, part).wait_recv()
        self.hop(1, 3, part).wait_recv()
        return (
            self.local(7, part)
            + self.came(0, 3, part)
            + self.came(1, 3, part)
        )


def mixer(
    rates_hbm, docs_hbm, q_hbm, k_hbm, v_hbm, again_hbm, w, res, mgain, ids,
    rates, docs, q, k_in, v, again,
    h_out, ids_all, gain_out,
    wbuf, hbuf, state, arrived, onward, incoming, resbuf, within,
    own, out, got, tbuf, rbuf,
    wss, wrs, hss, hrs, a1s, a1r, a2s, a2r, gs, gr, ps, pr, ids_s, ids_r, xs, xr, ts, tr, loc, start_weights, sends,
):
    spot = y, x, z, k = place()
    me, t = 4 * y + x, 2 * z + k
    low, partner = partner_of(*spot)
    loads = [
        pltpu.make_async_copy(a, b, loc.at[6 + i])
        for i, (a, b) in enumerate(
            (
                (k_hbm, k_in), (v_hbm, v), (rates_hbm, rates), (docs_hbm, docs), (q_hbm, q),
                (again_hbm, again),
            )
        )
    ]
    for cp in loads:
        cp.start()
    greet(*spot)

    weights = RingGather(wbuf, wss, wrs, y, lambda i: (i, x, z, k), 256, sends)
    heads = RingGather(hbuf, hss, hrs, x, lambda i: (y, i, z, k), 64, sends)
    own_w = pltpu.make_async_copy(w, wbuf.at[y], loc.at[0])
    own_w.start()

    handed = remote(res, resbuf, ps.at[0], pr.at[0], partner)
    kept = pltpu.make_async_copy(res, resbuf, loc.at[1])

    @pl.when(low != x)
    def _():
        handed.start()

    @pl.when(low == x)
    def _():
        kept.start()

    own_ids = pltpu.make_async_copy(ids, ids_all.at[x], loc.at[2])
    own_ids.start()
    for i in range(1, 4):
        remote(ids, ids_all.at[x], ids_s.at[0], ids_r.at[0], (y, (x + i) % 4, z, k)).start()
    sends.drain_later(ids_all.at[pl.ds(0, 3)], ids_s.at[0])

    own_gain = pltpu.make_async_copy(mgain, gain_out.at[t, 0], loc.at[3])
    own_gain.start()
    for i in range(1, 16):
        to = (t + i) % 16
        remote(mgain, gain_out.at[t, 0], gs.at[0], gr.at[0], (y, x, to // 2, to % 2)).start()
    sends.drain_later(gain_out.at[pl.ds(0, 15)], gs.at[0])

    start_weights()
    for cp in loads[:4]:
        cp.wait()
    start1 = docs[0]
    start2 = start1 + docs[1]
    start3 = start2 + docs[2]

    def seg(p):
        def past(s):
            return jnp.where(p >= s, 1, 0)

        base = jnp.where(p >= 0, 0, -1)
        return base + past(start1) + past(start2) + past(start3)

    first = me * ROWS
    last_seg = seg(first + ROWS - 1)
    before = seg(first - 1)
    row = lax.broadcasted_iota(jnp.int32, (ROWS, HD), 0)
    col = lax.broadcasted_iota(jnp.int32, (ROWS, HD), 1)
    seg_row, seg_col = seg(first + row), seg(first + col)
    rowf = row.astype(F32)
    at_end = jnp.where(seg_row == last_seg, 1.0, 0.0)
    for h in range(4):
        rate = rates[4 * t + h]
        cols = slice(h * HD, (h + 1) * HD)
        fading = at_end * jnp.exp(-rate * (ROWS - 1.0 - rowf))
        faded = (k_in[:, cols].astype(F32) * fading).astype(BF)
        state[h * HD : (h + 1) * HD, :] = lax.dot_general(
            faded, v[:, cols], (((0,), (0,)), ((), ())), preferred_element_type=F32
        ).astype(BF)

    own_state = pltpu.make_async_copy(
        state.at[pl.ds(pl.multiple_of(me * 32, 32), 32)], arrived.at[me], loc.at[4]
    )
    own_state.start()
    for ty, tx in others(y, x):
        to = 4 * ty + tx
        remote(
            state.at[pl.ds(pl.multiple_of(to * 32, 32), 32)],
            arrived.at[me],
            a1s.at[0],
            a1r.at[0],
            (to // 4, to % 4, z, k),
        ).start()
    sends.drain_later(arrived.at[pl.ds(0, 15)], a1s.at[0])
    weights.first(0, 0, w)
    weights.first(1, 1, w)

    loads[4].wait()
    loads[5].wait()
    allowed = jnp.where((row >= col) & (seg_row == seg_col), 1.0, 0.0)
    gap = jnp.maximum(row - col, 0).astype(F32)
    for h in range(4):
        rate = rates[4 * t + h]
        cols = slice(h * HD, (h + 1) * HD)
        scores = lax.dot_general(
            q[:, cols], k_in[:, cols], (((1,), (1,)), ((), ())), preferred_element_type=F32
        )
        mixed = (scores * (allowed * jnp.exp(-rate * gap))).astype(BF)
        within[:, cols] = jnp.dot(mixed, v[:, cols], preferred_element_type=F32)

    own_state.wait()
    peer = (y, x, z, 1 - k)

    def receive(ref, sem):
        remote(ref, ref, sem, sem, peer).wait_recv()

    receive(arrived.at[pl.ds(0, 15)], a1r.at[0])
    decay = jnp.exp(jnp.zeros((32, HD), F32) - rates[4 * t + y] * ROWS)
    running = jnp.zeros((32, HD), F32)
    for b in range(BLOCKS):
        onward[b] = running.astype(BF)
        same = seg(jnp.int32(b * ROWS + ROWS - 1)) == seg(jnp.int32(b * ROWS - 1))
        running = running * (decay * jnp.where(same, 1.0, 0.0)) + arrived[b].astype(F32)
    own_onward = pltpu.make_async_copy(onward.at[me], incoming.at[me], loc.at[5])
    own_onward.start()
    for ty, tx in others(y, x):
        to = 4 * ty + tx
        remote(
            onward.at[to], incoming.at[me], a2s.at[0], a2r.at[0], (to // 4, to % 4, z, k)
        ).start()
    sends.drain_later(onward.at[pl.ds(0, 15)], a2s.at[0])
    for d in range(2):
        weights.arrived(d, d)
        weights.forward(d)
    for d in range(2):
        weights.first(d, 1 - d, w)
    own_onward.wait()
    receive(incoming.at[pl.ds(0, 15)], a2r.at[0])

    reached = jnp.where(seg_row == before, 1.0, 0.0)
    for h in range(4):
        rate = rates[4 * t + h]
        cols = slice(h * HD, (h + 1) * HD)
        inc = incoming[4 * h : 4 * h + 4].reshape(HD, HD)
        inter = jnp.dot(q[:, cols], inc, preferred_element_type=F32)
        both = within[:, cols] + inter * (reached * jnp.exp(-rate * (rowf + 1.0)))
        scale = lax.rsqrt(jnp.mean(both * both, axis=1, keepdims=True) + 1e-06)
        within[:, cols] = both * scale * again[:, cols]
    hbuf[x] = within[...].astype(BF)
    for part in range(2):
        for d in range(2):
            heads.first(d, part if d == 0 else 1 - part, hbuf.at[x])
    for d in range(2):
        heads.arrived(d, d)
        heads.forward(d)
    for d in range(2):
        heads.arrived(d, 1 - d)
    own_w.wait()
    for d in range(2):
        weights.arrived(d, 1 - d)
        weights.forwarded(d)
    for d in range(2):
        heads.forwarded(d)

    total = RingSum(spot, ROWS, own, out, got, tbuf, rbuf, xs, xr, ts, tr, sends)

    def tile(i, mine):
        chunk = (z + ORDER[i]) % 8
        row = 2 * (chunk % 2) + (k if mine else 1 - k)
        return jnp.dot(hbuf[row], wbuf[chunk // 2], preferred_element_type=F32).astype(BF)

    total.begin(tile)
    total.rest(tile)

    @pl.when(low != x)
    def _():
        handed.wait()

    @pl.when(low == x)
    def _():
        kept.wait()

    for part in range(4):
        rows = slice(part * 32, part * 32 + 32)
        h_out[rows, :] = (resbuf[rows, :].astype(F32) + total.result(part)).astype(BF)
    own_gain.wait()
    receive(gain_out.at[pl.ds(0, 15)], gr.at[0])
    own_ids.wait()
    receive(ids_all.at[pl.ds(0, 3)], ids_r.at[0])


def slot_hits(ids):
    expert = lax.broadcasted_iota(jnp.int32, (BLOCKS, CAP, ROWS), 0).reshape(SLOTS, ROWS)
    place_in = lax.broadcasted_iota(jnp.int32, (BLOCKS, CAP, ROWS), 1).reshape(SLOTS, ROWS)
    hit0 = expert == ids[0:1, :]
    hit1 = expert == ids[1:2, :]
    named = jnp.where(hit0 | hit1, 1.0, 0.0)
    earlier = lax.broadcasted_iota(jnp.int32, (ROWS, ROWS), 0)
    later = lax.broadcasted_iota(jnp.int32, (ROWS, ROWS), 1)
    rank = jnp.dot(
        named.astype(BF),
        jnp.where(earlier < later, 1.0, 0.0).astype(BF),
        preferred_element_type=F32,
    )
    here = rank == place_in.astype(F32)
    return hit0 & here, hit1 & here


def experts(
    wts, wgu, wd, loads, h, ids_all, gains,
    o_ref,
    pick, ds, xb, hz, dsb, xb2, lhs, acc, squares, act, hn, qs, rb,
    ownb, outb, gotb, qsb, rb2, pb, gb, tb,
    own, out, got, tbuf, rbuf,
    dss, dsr, fs, fr, cs, cr, qss, qsr, ps, pr, xs, xr, ts, tr, loc,
    b1s, b1r, b2s, b2r, os, osr, ws, wr, b3s, b3r, b4s, b4r,
    sends,
):
    spot = y, x, z, k = place()
    me, t = 4 * y + x, 2 * z + k
    low, partner = partner_of(*spot)
    peer = (y, x, z, 1 - k)

    def receive(ref, sem):
        remote(ref, ref, sem, sem, peer).wait_recv()

    def at_ctx(c):
        return (c // 4, c % 4, z, k)

    def column_major(c):
        return 4 * (c % 4) + c // 4

    hz[z] = h[:, NEAR:]
    def along_z(ref, dist, sem):
        remote(ref, ref, b1s.at[0], b1r.at[sem], (y, x, (z + dist) % 8, k)).start()

    for dist, sem in ((2, 0), (6, 1), (1, 2), (7, 2)):
        along_z(hz.at[z], dist, sem)
    sends.drain_later(hz.at[pl.ds(0, 7)], b1s.at[0])

    for j in range(2):
        hit0, hit1 = slot_hits(ids_all[2 * j + k])
        pick[j] = jnp.where(hit0 | hit1, 1.0, 0.0).astype(BF)
    picked = jnp.dot(pick[z % 2], h[:, :NEAR], preferred_element_type=F32)
    ds[...] = picked.reshape(BLOCKS, CAP, NEAR).astype(BF)

    mine = 4 * x + y
    own_rows = pltpu.make_async_copy(ds.at[me], xb.at[t, mine], loc.at[3])
    own_rows.start()
    for ty, tx in others(y, x):
        to = 4 * ty + tx
        remote(ds.at[to], xb.at[t, mine], dss.at[0], dsr.at[0], at_ctx(to)).start()
    sends.drain_later(ds.at[pl.ds(0, 15)], dss.at[0])
    handed = remote(h, hn, ps.at[0], pr.at[0], partner)
    kept = pltpu.make_async_copy(h, hn, loc.at[4])
    for sem, dist in ((0, 6), (1, 2)):
        spot_z = (z + dist) % 8
        receive(hz.at[spot_z], b1r.at[sem])
        along_z(hz.at[spot_z], (1, 7)[sem], 2)
        along_z(hz.at[spot_z, pl.ds(64 * sem, 64)], (2, 6)[sem], 2)
    own_rows.wait()
    receive(xb.at[t, pl.ds(0, 15)], dsr.at[0])

    def half(zz, kk, part):
        return xb.at[2 * ((zz + 8) % 8) + kk, pl.ds(part * 8, 8)]

    def ring(d, s, part, ref):
        to = (z + (1, 7)[d]) % 8
        return remote(
            ref, ref, fs.at[0], fr.at[STEPS.index((d, s, part))], (y, x, to, k)
        )

    def over(slot, ref):
        remote(ref, ref, cs.at[0], cr.at[slot], peer).start()

    def crossed(slot, dist):
        receive(xb.at[2 * ((z + dist + 8) % 8) + 1 - k], cr.at[slot])

    sends.drain_later(xb.at[pl.ds(0, 7)], fs.at[0])
    sends.drain_later(xb.at[pl.ds(0, 8)], cs.at[0])
    for part in range(2):
        ref = half(z, k, part)
        ring(0, 0, part, ref).start()
        ring(1, 0, part, ref).start()
        over(0, ref)

    receive(hz.at[pl.ds(0, 5)], b1r.at[2])
    for j in range(2):
        wide = jnp.concatenate([hz[2 * i + j] for i in range(4)], axis=1)
        chosen = jnp.dot(pick[j], wide, preferred_element_type=F32)
        dsb[:, j] = chosen.reshape(BLOCKS, CAP, 4 * FAR).astype(BF)
    own_far = pltpu.make_async_copy(dsb.at[me], xb2.at[k, mine], loc.at[0])
    own_far.start()
    for ty, tx in others(y, x):
        to = 4 * ty + tx
        remote(dsb.at[to], xb2.at[k, mine], b2s.at[0], b2r.at[0], at_ctx(to)).start()
    sends.drain_later(dsb.at[pl.ds(0, 15)], b2s.at[0])

    wgu[HID:FEAT, :] = jnp.zeros((FEAT - HID, D), BF)
    acc[...] = jnp.zeros_like(acc)
    squares[...] = jnp.zeros_like(squares)

    def columns(ref, tile, first, width):
        return ref[:, pl.ds(pl.multiple_of(tile * FEAT + first, 128), width)]

    def load_rows(piece, xp, gain, first):
        rows = slice(96 * xp, 96 * xp + 96)
        width = gain.shape[1]
        piece = piece.astype(F32).reshape(96, width)
        sq = piece * piece
        add = sq[:, 0:128]
        for i in range(1, width // 128):
            add += sq[:, 128 * i : 128 * i + 128]
        squares[rows, :] += add
        lhs[rows, first : first + width] = (piece * gain).astype(BF)

    def product(depth, w):
        acc[...] += lax.dot_general(
            lhs[:, :depth], w, (((1,), (1,)), ((), ())), preferred_element_type=F32
        )

    def multiply(group):
        for xx in range(4):
            gain = gains[4 * group + xx][:, :NEAR]
            for xp in range(4):
                load_rows(xb[4 * group + xp, 4 * xx : 4 * xx + 4], xp, gain, xx * NEAR)
        product(
            4 * NEAR,
            jnp.concatenate([columns(wgu, 4 * group + xx, 0, NEAR) for xx in range(4)], axis=1),
        )

    def multiply_far():
        for xx in range(4):
            gain = jnp.concatenate([gains[4 * i + xx][:, NEAR:] for i in range(4)], axis=1)
            for xp in range(4):
                piece = xb2[xp % 2, 4 * xx : 4 * xx + 4, xp // 2]
                load_rows(piece, xp, gain, xx * 4 * FAR)
        product(
            16 * FAR,
            jnp.concatenate(
                [columns(wgu, 4 * i + xx, NEAR, FAR) for xx in range(4) for i in range(4)], axis=1
            ),
        )

    side = jnp.where(z % 2 == 0, 3, 1)
    pair = z // 2
    def step(s):
        for part in range(2):
            for d in range(2):
                ref = half(z + (-s if d == 0 else s), k, part)
                ring(d, s - 1, part, ref).wait_recv()
                if s < 3 or part == d:
                    ring(d, s, part, ref).start()
                over(2 * s - 1 + d, ref)

    step(1)
    step(2)
    loads[0].wait()
    loads[1].wait()
    crossed(0, 0)
    crossed(1, -1)
    crossed(2, 1)
    multiply(pair)
    step(3)

    @pl.when(low != x)
    def _():
        handed.start()

    @pl.when(low == x)
    def _():
        kept.start()

    own_far.wait()
    receive(xb2.at[k, pl.ds(0, 15)], b2r.at[0])
    remote(xb2.at[k], xb2.at[k], os.at[0], osr.at[0], peer).start()
    sends.drain_later(xb2.at[k], os.at[0])
    crossed(3, -2)
    crossed(4, 2)
    multiply((pair + side) % 4)
    crossed(5, -3)
    crossed(6, 3)
    multiply((pair + 4 - side) % 4)
    for d in range(2):
        ref = half(z + 4, k, d)
        ring(d, 3, d, ref).wait_recv()
        over(7, ref)
    receive(xb2.at[1 - k], osr.at[0])
    multiply_far()
    crossed(7, 4)
    multiply((pair + 2) % 4)

    total_sq = jnp.sum(squares[...], axis=1, keepdims=True)
    scale = lax.rsqrt(total_sq / D + 1e-05)
    gate = acc[:, :HID] * scale
    lifted = acc[:, FEAT:] * scale
    act[...] = (gate / (1.0 + jnp.exp(-gate)) * lifted).astype(BF)
    loads[2].wait()

    def far_tile(lane):
        cols = jnp.concatenate([columns(wd, 2 * i + lane, NEAR, FAR) for i in range(8)], axis=1)
        return jnp.dot(act[...], cols, preferred_element_type=F32).astype(BF)

    swap = remote(outb, gotb, ws.at[0], wr.at[0], peer)
    sends.drain_later(outb, ws.at[0])

    def aside():
        outb[...] = far_tile(1 - k)
        swap.start()

    def later():
        ownb[...] = far_tile(k)

    total = RingSum(spot, SLOTS, own, out, got, tbuf, rbuf, xs, xr, ts, tr, sends)

    def tile(i, mine):
        chunk = (z + ORDER[i]) % 8
        cols = columns(wd, 2 * chunk + (k if mine else 1 - k), 0, NEAR)
        return jnp.dot(act[...], cols, preferred_element_type=F32).astype(BF)

    total.begin(tile, aside, later)
    swap.wait_recv()
    summed = ownb[...].astype(F32) + gotb[...].astype(F32)
    qsb[...] = summed.reshape(BLOCKS, CAP, 8 * FAR).astype(BF)
    own_home = pltpu.make_async_copy(qsb.at[mine], rb2.at[me], loc.at[1])
    own_home.start()
    for ty, tx in others(y, x):
        to = 4 * ty + tx
        remote(qsb.at[column_major(to)], rb2.at[me], b3s.at[0], b3r.at[0], at_ctx(to)).start()
    sends.drain_later(qsb.at[pl.ds(0, 15)], b3s.at[0])
    total.rest(tile)

    loads[3].wait()
    hit0, hit1 = slot_hits(ids_all[x])
    part_of = jnp.where(hit0, wts[0:1, :], 0.0) + jnp.where(hit1, wts[1:2, :], 0.0)
    coarse = part_of.astype(BF)
    fine = (part_of - coarse.astype(F32)).astype(BF)

    def combine(ref):
        back = ref[...].astype(F32).reshape(SLOTS, ref.shape[2]).astype(BF)
        dims = (((0,), (0,)), ((), ()))
        mixture = lax.dot_general(coarse, back, dims, preferred_element_type=F32)
        return mixture + lax.dot_general(fine, back, dims, preferred_element_type=F32)

    own_home.wait()
    receive(rb2.at[pl.ds(0, 15)], b3r.at[0])
    far_mix = combine(rb2)
    for i in range(8):
        pb[i] = far_mix[:, FAR * i : FAR * i + FAR].astype(BF)
    def along(src, dst, sem, dist):
        remote(src, dst, b4s.at[0], b4r.at[sem], (y, x, (z + dist + 8) % 8, k)).start()

    for d, sign in enumerate((1, -1)):
        rows = pl.ds(64 * d, 64)
        along(pb.at[(z + 4) % 8, rows], gb.at[5 + 2 * d, rows], 2 + 2 * d, 2 * sign)
        along(pb.at[(z + 3 * sign + 8) % 8], gb.at[4 + 2 * d], 1 + 2 * d, sign)
        along(pb.at[(z + sign + 8) % 8], gb.at[d], 0, sign)
    sends.drain_later(pb.at[pl.ds(0, 7)], b4s.at[0])

    own_back = pltpu.make_async_copy(qs.at[mine], rb.at[me], loc.at[5])
    for part in range(4):
        qs[part * 4 : part * 4 + 4] = total.result(part).reshape(4, CAP, NEAR).astype(BF)
        for i in range(4):
            row = (y + i) % 4
            home = remote(
                qs.at[4 * part + row], rb.at[me], qss.at[0], qsr.at[0], (row, part, z, k)
            )
            if i > 0:
                home.start()
            else:
                pl.when(part != x)(home.start)
                pl.when(part == x)(own_back.start)
    sends.drain_later(qs.at[pl.ds(0, 15)], qss.at[0])
    for d, sign in enumerate((1, -1)):
        rows = pl.ds(64 * d, 64)
        receive(gb.at[4 + 2 * d], b4r.at[1 + 2 * d])
        tb[d] = (pb[(z + 2 * sign + 8) % 8].astype(F32) + gb[4 + 2 * d].astype(F32)).astype(BF)
        receive(gb.at[5 + 2 * d, rows], b4r.at[2 + 2 * d])
        tb[d, rows, :] = (tb[d, rows, :].astype(F32) + gb[5 + 2 * d, rows, :].astype(F32)).astype(BF)
        along(tb.at[d], gb.at[2 + d], 0, 2 * sign)

    @pl.when(low != x)
    def _():
        handed.wait()

    @pl.when(low == x)
    def _():
        kept.wait()

    far_sum = hn[:, NEAR:].astype(F32) + pb[z].astype(F32)
    receive(gb.at[pl.ds(0, 4)], b4r.at[0])
    for i in range(4):
        far_sum += gb[i].astype(F32)
    o_ref[:, NEAR:] = far_sum.astype(BF)
    own_back.wait()
    receive(rb.at[pl.ds(0, 15)], qsr.at[0])
    o_ref[:, :NEAR] = (hn[:, :NEAR].astype(F32) + combine(rb)).astype(BF)


def layer(*refs):
    ins, o_ref, refs = refs[:14], refs[14], list(refs[15:])

    def take(n):
        taken = refs[:n]
        del refs[:n]
        return taken

    wg_hbm, wu_hbm, wd_hbm, wts_hbm = ins[10:]
    wgu, wd, wts, wsem = take(4)
    early = take(6)
    passed = h, ids_all, gains = take(3)
    mix_scratch = take(8)
    mix_ring = take(5)
    mix_sems = take(19)
    moe_scratch = take(21)
    moe_ring = take(5)
    moe_sems = take(27)
    loads = [
        pltpu.make_async_copy(wg_hbm, wgu.at[pl.ds(0, HID)], wsem.at[0]),
        pltpu.make_async_copy(wu_hbm, wgu.at[pl.ds(FEAT, HID)], wsem.at[1]),
        pltpu.make_async_copy(wd_hbm, wd, wsem.at[2]),
        pltpu.make_async_copy(wts_hbm, wts, wsem.at[3]),
    ]

    def start_weights():
        for cp in loads:
            cp.start()

    sends = Sends()
    mixer(
        *ins[:10], *early, *passed, *mix_scratch, *mix_ring, *mix_sems, start_weights, sends
    )
    experts(wts, wgu, wd, loads, *passed, o_ref, *moe_scratch, *moe_ring, *moe_sems, sends)
    y, x, z, k = place()
    sends.drain((y, x, z, 1 - k))


def dma(*shape):
    return pltpu.SemaphoreType.DMA(shape)


def ring_scratch(rows, width):
    quarter = rows // 4
    return [
        pltpu.VMEM((8, rows, width), BF),
        pltpu.VMEM((8, rows, width), BF),
        pltpu.VMEM((8, rows, width), BF),
        pltpu.VMEM((28, quarter, width), BF),
        pltpu.VMEM((28, quarter, width), BF),
    ]


ANY = pl.BlockSpec(memory_space=pl.ANY)


def shards(
    residual, query_rows, key_rows, value_rows, head_rates, doc_lengths, attn_gain, out_weight,
    moe_gain, expert_ids, expert_weights, gate_weight, up_weight, down_weight,
):
    return pl.pallas_call(
        layer,
        out_shape=jax.ShapeDtypeStruct((ROWS, FEAT), BF),
        in_specs=[ANY] * 14,
        out_specs=pl.BlockSpec(memory_space=pltpu.VMEM),
        scratch_shapes=[
            pltpu.VMEM((FEAT + HID, D), BF),
            pltpu.VMEM((HID, D), BF),
            pltpu.VMEM((2, ROWS), F32),
            dma(4),
            pltpu.SMEM((64,), F32),
            pltpu.SMEM((4,), jnp.int32),
            pltpu.VMEM((ROWS, 512), BF),
            pltpu.VMEM((ROWS, 512), BF),
            pltpu.VMEM((ROWS, 512), BF),
            pltpu.VMEM((1, 512), F32),
            pltpu.VMEM((ROWS, FEAT), BF),
            pltpu.VMEM((4, 2, ROWS), jnp.int32),
            pltpu.VMEM((16, 1, FEAT), F32),
            pltpu.VMEM((4, 512, FEAT), BF),
            pltpu.VMEM((4, ROWS, 512), BF),
            pltpu.VMEM((512, HD), BF),
            pltpu.VMEM((16, 32, HD), BF),
            pltpu.VMEM((16, 32, HD), BF),
            pltpu.VMEM((16, 32, HD), BF),
            pltpu.VMEM((ROWS, FEAT), BF),
            pltpu.VMEM((ROWS, 512), F32),
            *ring_scratch(ROWS, FEAT),
            dma(1), dma(2, 3), dma(1), dma(2, 3),
            dma(1), dma(1), dma(1), dma(1), dma(1), dma(1),
            dma(1), dma(1), dma(1), dma(1), dma(1), dma(8), dma(1), dma(28), dma(12),
            pltpu.VMEM((2, SLOTS, ROWS), BF),
            pltpu.VMEM((BLOCKS, CAP, NEAR), BF),
            pltpu.VMEM((16, BLOCKS, CAP, NEAR), BF),
            pltpu.VMEM((8, ROWS, FAR), BF),
            pltpu.VMEM((BLOCKS, 2, CAP, 4 * FAR), BF),
            pltpu.VMEM((2, BLOCKS, 2, CAP, 4 * FAR), BF),
            pltpu.VMEM((SLOTS, 16 * FAR), BF),
            pltpu.VMEM((SLOTS, FEAT + HID), F32),
            pltpu.VMEM((SLOTS, 128), F32),
            pltpu.VMEM((SLOTS, HID), BF),
            pltpu.VMEM((ROWS, FEAT), BF),
            pltpu.VMEM((BLOCKS, CAP, NEAR), BF),
            pltpu.VMEM((BLOCKS, CAP, NEAR), BF),
            pltpu.VMEM((SLOTS, 8 * FAR), BF),
            pltpu.VMEM((SLOTS, 8 * FAR), BF),
            pltpu.VMEM((SLOTS, 8 * FAR), BF),
            pltpu.VMEM((BLOCKS, CAP, 8 * FAR), BF),
            pltpu.VMEM((BLOCKS, CAP, 8 * FAR), BF),
            pltpu.VMEM((8, ROWS, FAR), BF),
            pltpu.VMEM((8, ROWS, FAR), BF),
            pltpu.VMEM((2, ROWS, FAR), BF),
            *ring_scratch(SLOTS, NEAR),
            dma(1), dma(1), dma(1), dma(14), dma(1), dma(8),
            dma(1), dma(1), dma(1), dma(1), dma(1), dma(8), dma(1), dma(28), dma(6),
            dma(1), dma(3), dma(1), dma(1), dma(1), dma(1), dma(1), dma(1),
            dma(1), dma(1), dma(1), dma(5),
        ],
        compiler_params=pltpu.CompilerParams(
            collective_id=0, has_side_effects=True, vmem_limit_bytes=67043328
        ),
        name="layer",
    )(
        head_rates, doc_lengths, query_rows, key_rows, value_rows, attn_gain.reshape(1, -1),
        out_weight, residual, moe_gain, expert_ids.T,
        gate_weight[0].T, up_weight[0].T, down_weight[0], expert_weights.T,
    )


def solution(mesh):
    finer = Mesh(mesh.devices.reshape(4, 4, 8, 2), AXES)
    placed = (
        P(CTX, TP), P(CTX, TP), P(CTX, TP), P(CTX, TP), P(), P(), P(TP), P(TP, CTX), P(TP),
        P(CTX, None), P(CTX, None), P(CTX, None, TP), P(CTX, None, TP), P(CTX, TP, None),
    )
    return jax.shard_map(shards, mesh=finer, in_specs=placed, out_specs=P(CTX, TP), check_vma=False)
```

```python
import jax
import jax.numpy as jnp
from jax import lax
from jax.experimental import pallas as pl
from jax.experimental.pallas import tpu as pltpu
from jax.sharding import Mesh
from jax.sharding import PartitionSpec as P

D = 6144
HD = 128
CAP = 24
BLOCKS = 16
ROWS = 128
FEAT = 384
NEAR = 256
FAR = 128
HID = 288
SLOTS = BLOCKS * CAP
CTX = ("ctx_0", "ctx_1")
TP = ("tp_0", "tp_1")
AXES = CTX + TP
ORDER = (4, 3, 5, 2, 6, 1, 7, 0)
HOPS = [(d, s, p) for d in range(2) for s in range(4) for p in range(4) if s > 0 or p // 2 == d]
STEPS = [(d, s, p) for d in range(2) for s in range(4) for p in range(2) if s < 3 or p == d]
OFFSETS = sorted(
    ((dy, dx) for dy in range(4) for dx in range(4) if dy or dx),
    key=lambda o: -(min(o[0], 4 - o[0]) + min(o[1], 4 - o[1])),
)
STAND = (0, 2, 1, 3)
BF = jnp.bfloat16
F32 = jnp.float32


def remote(src, dst, send_sem, recv_sem, to):
    return pltpu.make_async_remote_copy(
        src_ref=src,
        dst_ref=dst,
        send_sem=send_sem,
        recv_sem=recv_sem,
        device_id=to,
        device_id_type=pl.DeviceIdType.MESH,
    )


def place():
    return tuple(lax.axis_index(a) for a in AXES)


def others(y, x):
    return [((y + dy) % 4, (x + dx) % 4) for dy, dx in OFFSETS]


def partner_of(y, x, z, k):
    low = 2 * (z % 2) + k
    return low, (y, low, 2 * (z // 2) + x // 2, x % 2)


def greet(y, x, z, k):
    sem = pltpu.get_barrier_semaphore()
    for i in range(1, 16):
        c = (4 * y + x + i) % 16
        pl.semaphore_signal(
            sem, inc=1, device_id=(c // 4, c % 4, z, k), device_id_type=pl.DeviceIdType.MESH
        )
    for i in range(1, 16):
        t = (2 * z + k + i) % 16
        pl.semaphore_signal(
            sem, inc=1, device_id=(y, x, t // 2, t % 2), device_id_type=pl.DeviceIdType.MESH
        )
    low, partner = partner_of(y, x, z, k)

    @pl.when(low != x)
    def _():
        pl.semaphore_signal(sem, inc=1, device_id=partner, device_id_type=pl.DeviceIdType.MESH)

    pl.semaphore_wait(sem, 30 + ((low - x + 4) % 4 + 3) // 4)


class Sends:
    def __init__(self):
        self.open = []

    def drain_later(self, ref, sem):
        self.open.append((ref, sem))

    def drain(self, to):
        for ref, sem in self.open:
            remote(ref, ref, sem, sem, to).wait_send()


class RingGather:
    def __init__(self, buf, ssem, rsem, me, device_at, half, sends):
        self.buf, self.ssem, self.rsem = buf, ssem, rsem
        self.me, self.at, self.half = me, device_at, half
        sends.drain_later(buf.at[pl.ds(0, 3)], ssem.at[0])

    def piece(self, member, part):
        return self.buf.at[member % 4, pl.ds(part * self.half, self.half)]

    def first(self, d, part, own):
        remote(
            own.at[pl.ds(part * self.half, self.half)],
            self.piece(self.me, part),
            self.ssem.at[0],
            self.rsem.at[d, part],
            self.at((self.me + (1, -1)[d]) % 4),
        ).start()

    def along(self, d, slot, ref):
        return remote(
            ref, ref, self.ssem.at[0], self.rsem.at[d, slot], self.at((self.me + (1, -1)[d]) % 4)
        )

    def arrived(self, d, part):
        self.along(d, part, self.piece(self.me + 4 - (1, -1)[d], part)).wait_recv()

    def forward(self, d):
        self.along(d, 2, self.piece(self.me + 4 - (1, -1)[d], d)).start()

    def forwarded(self, d):
        self.along(d, 2, self.piece(self.me + 2, d)).wait_recv()


class RingSum:
    def __init__(self, spot, rows, own, out, got, tbuf, rbuf, xs, xr, ssem, rsem, sends):
        self.y, self.x, self.z, self.k = spot
        self.quarter = rows // 4
        self.own, self.out, self.got = own, out, got
        self.tbuf, self.rbuf = tbuf, rbuf
        self.xs, self.xr, self.ssem, self.rsem = xs, xr, ssem, rsem
        sends.drain_later(out, xs.at[0])
        sends.drain_later(tbuf, ssem.at[0])

    def swap(self, i):
        self.swapping(i).start()

    def swapping(self, i):
        return remote(
            self.out.at[i],
            self.got.at[i],
            self.xs.at[0],
            self.xr.at[i],
            (self.y, self.x, self.z, 1 - self.k),
        )

    def swapped(self, i):
        self.swapping(i).wait_recv()

    def local(self, i, part):
        rows = pl.ds(part * self.quarter, self.quarter)
        return self.own[i, rows, :].astype(F32) + self.got[i, rows, :].astype(F32)

    def hop(self, d, s, part):
        to = (self.z + (1, 7)[d]) % 8
        return remote(
            self.tbuf.at[HOPS.index((d, s, part))],
            self.rbuf.at[HOPS.index((d, s, part))],
            self.ssem.at[0],
            self.rsem.at[HOPS.index((d, s, part))],
            (self.y, self.x, to, self.k),
        )

    def send(self, d, s, part, value):
        self.tbuf[HOPS.index((d, s, part))] = value.astype(BF)
        self.hop(d, s, part).start()

    def came(self, d, s, part):
        return self.rbuf[HOPS.index((d, s, part))].astype(F32)

    def begin(self, tile, aside=None, later=None):
        self.make(tile, 0)
        self.out[1] = tile(1, False)
        self.swap(1)
        if aside:
            aside()
        self.swapped(0)
        for j in range(2):
            for d in range(2):
                self.send(d, 0, 2 * d + j, self.local(0, 2 * d + j))
        self.own[1] = tile(1, True)
        self.make(tile, 2)
        if later:
            later()
        for d in range(2):
            self.swapped(1 + d)
            for j in range(2):
                part = 2 * (1 - d) + j
                self.send(d, 1, part, self.local(1 + d, part))

    def make(self, tile, i):
        self.out[i] = tile(i, False)
        self.swap(i)
        self.own[i] = tile(i, True)

    def rest(self, tile):
        for s in (1, 2, 3):
            for i in range(2 * s + 1, min(2 * s + 3, 8)):
                self.make(tile, i)
            if s > 1:
                self.swapped(2 * s - 1)
                self.swapped(2 * s)
            for j in range(4):
                for d in range(2):
                    part = (j + 2 * (1 - d)) % 4
                    if s == 1 and part // 2 != d:
                        continue
                    self.hop(d, s - 1, part).wait_recv()
                    value = self.local(2 * s - 1 + d, part) + self.came(d, s - 1, part)
                    self.send(d, s, part, value)
        self.swapped(7)

    def result(self, part):
        self.hop(0, 3, part).wait_recv()
        self.hop(1, 3, part).wait_recv()
        return (
            self.local(7, part)
            + self.came(0, 3, part)
            + self.came(1, 3, part)
        )


def mixer(
    rates_hbm, docs_hbm, q_hbm, k_hbm, v_hbm, again_hbm, w, res, mgain, ids,
    rates, docs, q, k_in, v, again,
    h_out, ids_all, gain_out,
    wbuf, hbuf, state, arrived, onward, incoming, resbuf, within,
    own, out, got, tbuf, rbuf,
    wss, wrs, hss, hrs, a1s, a1r, a2s, a2r, gs, gr, ps, pr, ids_s, ids_r, xs, xr, ts, tr, loc, start_weights, sends,
):
    spot = y, x, z, k = place()
    me, t = 4 * y + x, 2 * z + k
    low, partner = partner_of(*spot)
    loads = [
        pltpu.make_async_copy(a, b, loc.at[6 + i])
        for i, (a, b) in enumerate(
            (
                (k_hbm, k_in), (v_hbm, v), (rates_hbm, rates), (docs_hbm, docs), (q_hbm, q),
                (again_hbm, again),
            )
        )
    ]
    for cp in loads:
        cp.start()
    greet(*spot)

    weights = RingGather(wbuf, wss, wrs, y, lambda i: (i, x, z, k), 256, sends)
    heads = RingGather(hbuf, hss, hrs, x, lambda i: (y, i, z, k), 64, sends)
    own_w = pltpu.make_async_copy(w, wbuf.at[y], loc.at[0])
    own_w.start()

    handed = remote(res, resbuf, ps.at[0], pr.at[0], partner)
    kept = pltpu.make_async_copy(res, resbuf, loc.at[1])

    @pl.when(low != x)
    def _():
        handed.start()

    @pl.when(low == x)
    def _():
        kept.start()

    own_ids = pltpu.make_async_copy(ids, ids_all.at[x], loc.at[2])
    own_ids.start()
    for i in range(1, 4):
        remote(ids, ids_all.at[x], ids_s.at[0], ids_r.at[0], (y, (x + i) % 4, z, k)).start()
    sends.drain_later(ids_all.at[pl.ds(0, 3)], ids_s.at[0])

    own_gain = pltpu.make_async_copy(mgain, gain_out.at[t, 0], loc.at[3])
    own_gain.start()
    for i in range(1, 16):
        to = (t + i) % 16
        remote(mgain, gain_out.at[t, 0], gs.at[0], gr.at[0], (y, x, to // 2, to % 2)).start()
    sends.drain_later(gain_out.at[pl.ds(0, 15)], gs.at[0])

    start_weights()
    for cp in loads[:4]:
        cp.wait()
    start1 = docs[0]
    start2 = start1 + docs[1]
    start3 = start2 + docs[2]

    def seg(p):
        def past(s):
            return jnp.where(p >= s, 1, 0)

        base = jnp.where(p >= 0, 0, -1)
        return base + past(start1) + past(start2) + past(start3)

    first = me * ROWS
    last_seg = seg(first + ROWS - 1)
    before = seg(first - 1)
    row = lax.broadcasted_iota(jnp.int32, (ROWS, HD), 0)
    col = lax.broadcasted_iota(jnp.int32, (ROWS, HD), 1)
    seg_row, seg_col = seg(first + row), seg(first + col)
    rowf = row.astype(F32)
    at_end = jnp.where(seg_row == last_seg, 1.0, 0.0)
    for h in range(4):
        rate = rates[4 * t + h]
        cols = slice(h * HD, (h + 1) * HD)
        fading = at_end * jnp.exp(-rate * (ROWS - 1.0 - rowf))
        faded = (k_in[:, cols].astype(F32) * fading).astype(BF)
        state[h * HD : (h + 1) * HD, :] = lax.dot_general(
            faded, v[:, cols], (((0,), (0,)), ((), ())), preferred_element_type=F32
        ).astype(BF)

    own_state = pltpu.make_async_copy(
        state.at[pl.ds(pl.multiple_of(me * 32, 32), 32)], arrived.at[me], loc.at[4]
    )
    own_state.start()
    for ty, tx in others(y, x):
        to = 4 * ty + tx
        remote(
            state.at[pl.ds(pl.multiple_of(to * 32, 32), 32)],
            arrived.at[me],
            a1s.at[0],
            a1r.at[0],
            (to // 4, to % 4, z, k),
        ).start()
    sends.drain_later(arrived.at[pl.ds(0, 15)], a1s.at[0])
    weights.first(0, 0, w)
    weights.first(1, 1, w)

    loads[4].wait()
    loads[5].wait()
    allowed = jnp.where((row >= col) & (seg_row == seg_col), 1.0, 0.0)
    gap = jnp.maximum(row - col, 0).astype(F32)
    for h in range(4):
        rate = rates[4 * t + h]
        cols = slice(h * HD, (h + 1) * HD)
        scores = lax.dot_general(
            q[:, cols], k_in[:, cols], (((1,), (1,)), ((), ())), preferred_element_type=F32
        )
        mixed = (scores * (allowed * jnp.exp(-rate * gap))).astype(BF)
        within[:, cols] = jnp.dot(mixed, v[:, cols], preferred_element_type=F32)

    own_state.wait()
    peer = (y, x, z, 1 - k)

    def receive(ref, sem):
        remote(ref, ref, sem, sem, peer).wait_recv()

    receive(arrived.at[pl.ds(0, 15)], a1r.at[0])
    decay = jnp.exp(jnp.zeros((32, HD), F32) - rates[4 * t + y] * ROWS)
    running = jnp.zeros((32, HD), F32)
    for b in range(BLOCKS):
        onward[b] = running.astype(BF)
        same = seg(jnp.int32(b * ROWS + ROWS - 1)) == seg(jnp.int32(b * ROWS - 1))
        running = running * (decay * jnp.where(same, 1.0, 0.0)) + arrived[b].astype(F32)
    own_onward = pltpu.make_async_copy(onward.at[me], incoming.at[me], loc.at[5])
    own_onward.start()
    for ty, tx in others(y, x):
        to = 4 * ty + tx
        remote(
            onward.at[to], incoming.at[me], a2s.at[0], a2r.at[0], (to // 4, to % 4, z, k)
        ).start()
    sends.drain_later(onward.at[pl.ds(0, 15)], a2s.at[0])
    for d in range(2):
        weights.first(d, 1 - d, w)
    for d in range(2):
        weights.arrived(d, d)
        weights.forward(d)
    own_onward.wait()
    receive(incoming.at[pl.ds(0, 15)], a2r.at[0])

    reached = jnp.where(seg_row == before, 1.0, 0.0)
    for h in range(4):
        rate = rates[4 * t + h]
        cols = slice(h * HD, (h + 1) * HD)
        inc = incoming[4 * h : 4 * h + 4].reshape(HD, HD)
        inter = jnp.dot(q[:, cols], inc, preferred_element_type=F32)
        both = within[:, cols] + inter * (reached * jnp.exp(-rate * (rowf + 1.0)))
        scale = lax.rsqrt(jnp.mean(both * both, axis=1, keepdims=True) + 1e-06)
        within[:, cols] = both * scale * again[:, cols]
    hbuf[x] = within[...].astype(BF)
    for part in range(2):
        for d in range(2):
            heads.first(d, part if d == 0 else 1 - part, hbuf.at[x])
    for d in range(2):
        heads.arrived(d, d)
        heads.forward(d)
    for d in range(2):
        heads.arrived(d, 1 - d)
    own_w.wait()
    for d in range(2):
        weights.arrived(d, 1 - d)
        weights.forwarded(d)
    for d in range(2):
        heads.forwarded(d)

    total = RingSum(spot, ROWS, own, out, got, tbuf, rbuf, xs, xr, ts, tr, sends)

    def tile(i, mine):
        chunk = (z + ORDER[i]) % 8
        row = 2 * (chunk % 2) + (k if mine else 1 - k)
        return jnp.dot(hbuf[row], wbuf[chunk // 2], preferred_element_type=F32).astype(BF)

    total.begin(tile)
    total.rest(tile)

    @pl.when(low != x)
    def _():
        handed.wait()

    @pl.when(low == x)
    def _():
        kept.wait()

    for part in range(4):
        rows = slice(part * 32, part * 32 + 32)
        h_out[rows, :] = (resbuf[rows, :].astype(F32) + total.result(part)).astype(BF)
    own_gain.wait()
    receive(gain_out.at[pl.ds(0, 15)], gr.at[0])
    own_ids.wait()
    receive(ids_all.at[pl.ds(0, 3)], ids_r.at[0])


def slot_hits(ids):
    expert = lax.broadcasted_iota(jnp.int32, (BLOCKS, CAP, ROWS), 0).reshape(SLOTS, ROWS)
    place_in = lax.broadcasted_iota(jnp.int32, (BLOCKS, CAP, ROWS), 1).reshape(SLOTS, ROWS)
    hit0 = expert == ids[0:1, :]
    hit1 = expert == ids[1:2, :]
    named = jnp.where(hit0 | hit1, 1.0, 0.0)
    earlier = lax.broadcasted_iota(jnp.int32, (ROWS, ROWS), 0)
    later = lax.broadcasted_iota(jnp.int32, (ROWS, ROWS), 1)
    rank = jnp.dot(
        named.astype(BF),
        jnp.where(earlier < later, 1.0, 0.0).astype(BF),
        preferred_element_type=F32,
    )
    here = rank == place_in.astype(F32)
    return hit0 & here, hit1 & here


def experts(
    wts, wgu, wd, loads, h, ids_all, gains,
    o_ref,
    pick, ds, xb, hz, dsb, xb2, lhs, acc, squares, act, hn, qs, rb,
    ownb, outb, gotb, qsb, rb2, pb, gb, tb,
    own, out, got, tbuf, rbuf,
    dss, dsr, fs, fr, cs, cr, qss, qsr, ps, pr, xs, xr, ts, tr, loc,
    b1s, b1r, b2s, b2r, os, osr, ws, wr, b3s, b3r, b4s, b4r,
    sends,
):
    spot = y, x, z, k = place()
    me, t = 4 * y + x, 2 * z + k
    low, partner = partner_of(*spot)
    peer = (y, x, z, 1 - k)

    def receive(ref, sem):
        remote(ref, ref, sem, sem, peer).wait_recv()

    def at_ctx(c):
        return (c // 4, c % 4, z, k)

    hz[z] = h[:, NEAR:]
    def along_z(ref, dist, sem):
        remote(ref, ref, b1s.at[0], b1r.at[sem], (y, x, (z + dist) % 8, k)).start()

    for dist, sem in ((2, 0), (6, 1), (1, 2), (7, 2)):
        along_z(hz.at[z], dist, sem)
    sends.drain_later(hz.at[pl.ds(0, 7)], b1s.at[0])

    for j in range(2):
        hit0, hit1 = slot_hits(ids_all[2 * j + k])
        pick[j] = jnp.where(hit0 | hit1, 1.0, 0.0).astype(BF)
    picked = jnp.dot(pick[z % 2], h[:, :NEAR], preferred_element_type=F32)
    ds[...] = picked.reshape(BLOCKS, CAP, NEAR).astype(BF)

    mine = 4 * x + y
    home_row = 4 * (2 * (x % 2) + x // 2) + y
    own_rows = pltpu.make_async_copy(ds.at[me], xb.at[t, mine], loc.at[3])
    own_rows.start()
    for ty, tx in others(y, x):
        to = 4 * ty + tx
        remote(ds.at[to], xb.at[t, mine], dss.at[0], dsr.at[0], at_ctx(to)).start()
    sends.drain_later(ds.at[pl.ds(0, 15)], dss.at[0])
    handed = remote(h, hn, ps.at[0], pr.at[0], partner)
    kept = pltpu.make_async_copy(h, hn, loc.at[4])
    for sem, dist in ((0, 6), (1, 2)):
        spot_z = (z + dist) % 8
        receive(hz.at[spot_z], b1r.at[sem])
        along_z(hz.at[spot_z], (1, 7)[sem], 2)
        along_z(hz.at[spot_z, pl.ds(64 * sem, 64)], (2, 6)[sem], 2)
    own_rows.wait()
    receive(xb.at[t, pl.ds(0, 15)], dsr.at[0])

    def half(zz, kk, part):
        return xb.at[2 * ((zz + 8) % 8) + kk, pl.ds(part * 8, 8)]

    def ring(d, s, part, ref):
        to = (z + (1, 7)[d]) % 8
        return remote(
            ref, ref, fs.at[0], fr.at[STEPS.index((d, s, part))], (y, x, to, k)
        )

    def over(slot, ref):
        remote(ref, ref, cs.at[0], cr.at[slot], peer).start()

    def crossed(slot, dist):
        receive(xb.at[2 * ((z + dist + 8) % 8) + 1 - k], cr.at[slot])

    sends.drain_later(xb.at[pl.ds(0, 7)], fs.at[0])
    sends.drain_later(xb.at[pl.ds(0, 8)], cs.at[0])
    for part in range(2):
        ref = half(z, k, part)
        ring(0, 0, part, ref).start()
        ring(1, 0, part, ref).start()
        over(0, ref)

    receive(hz.at[pl.ds(0, 5)], b1r.at[2])
    for j in range(2):
        wide = jnp.concatenate([hz[2 * i + j] for i in range(4)], axis=1)
        chosen = jnp.dot(pick[j], wide, preferred_element_type=F32)
        dsb[:, j] = chosen.reshape(BLOCKS, CAP, 4 * FAR).astype(BF)
    own_far = pltpu.make_async_copy(dsb.at[me], xb2.at[k, mine], loc.at[0])
    own_far.start()
    for ty, tx in others(y, x):
        to = 4 * ty + tx
        remote(dsb.at[to], xb2.at[k, mine], b2s.at[0], b2r.at[0], at_ctx(to)).start()
    sends.drain_later(dsb.at[pl.ds(0, 15)], b2s.at[0])

    wgu[HID:FEAT, :] = jnp.zeros((FEAT - HID, D), BF)
    acc[...] = jnp.zeros_like(acc)
    squares[...] = jnp.zeros_like(squares)

    def columns(ref, tile, first, width):
        return ref[:, pl.ds(pl.multiple_of(tile * FEAT + first, 128), width)]

    def load_rows(piece, stand, gain, first, into):
        rows = pl.ds(stand * 96, 96)
        width = gain.shape[1]
        piece = piece.astype(F32).reshape(96, width)
        sq = piece * piece
        add = sq[:, 0:128]
        for i in range(1, width // 128):
            add += sq[:, 128 * i : 128 * i + 128]
        squares[rows, :] += add
        lhs[96 * into : 96 * into + 96, first : first + width] = (piece * gain).astype(BF)

    def product(rows, depth, w):
        acc[rows, :] += lax.dot_general(
            lhs[: rows.size, :depth], w, (((1,), (1,)), ((), ())), preferred_element_type=F32
        )

    def multiply(group):
        for xx in range(4):
            gain = gains[4 * group + xx][:, :NEAR]
            for xp in range(4):
                piece = xb[4 * group + xp, 4 * xx : 4 * xx + 4]
                load_rows(piece, STAND[xp], gain, xx * NEAR, STAND[xp])
        product(
            pl.ds(0, SLOTS),
            4 * NEAR,
            jnp.concatenate([columns(wgu, 4 * group + xx, 0, NEAR) for xx in range(4)], axis=1),
        )

    def multiply_far(lane):
        for xx in range(4):
            gain = jnp.concatenate([gains[4 * i + xx][:, NEAR:] for i in range(4)], axis=1)
            for j in range(2):
                piece = xb2[lane, 4 * xx : 4 * xx + 4, j]
                load_rows(piece, 2 * lane + j, gain, xx * 4 * FAR, j)
        product(
            pl.ds(pl.multiple_of(lane * 192, 192), 192),
            16 * FAR,
            jnp.concatenate(
                [columns(wgu, 4 * i + xx, NEAR, FAR) for xx in range(4) for i in range(4)], axis=1
            ),
        )

    side = jnp.where(z % 2 == 0, 3, 1)
    pair = z // 2
    def step(s):
        for part in range(2):
            for d in range(2):
                ref = half(z + (-s if d == 0 else s), k, part)
                ring(d, s - 1, part, ref).wait_recv()
                if s < 3 or part == d:
                    ring(d, s, part, ref).start()
                over(2 * s - 1 + d, ref)

    step(1)
    step(2)
    loads[0].wait()
    loads[1].wait()
    crossed(0, 0)
    crossed(1, -1)
    crossed(2, 1)
    multiply(pair)
    step(3)

    @pl.when(low != x)
    def _():
        handed.start()

    @pl.when(low == x)
    def _():
        kept.start()

    own_far.wait()
    receive(xb2.at[k, pl.ds(0, 15)], b2r.at[0])
    remote(xb2.at[k], xb2.at[k], os.at[0], osr.at[0], peer).start()
    sends.drain_later(xb2.at[k], os.at[0])
    crossed(3, -2)
    crossed(4, 2)
    multiply((pair + side) % 4)
    multiply_far(k)
    crossed(5, -3)
    crossed(6, 3)
    multiply((pair + 4 - side) % 4)
    for d in range(2):
        ref = half(z + 4, k, d)
        ring(d, 3, d, ref).wait_recv()
        over(7, ref)
    receive(xb2.at[1 - k], osr.at[0])
    multiply_far(1 - k)
    crossed(7, 4)
    multiply((pair + 2) % 4)

    total_sq = jnp.sum(squares[...], axis=1, keepdims=True)
    scale = lax.rsqrt(total_sq / D + 1e-05)
    gate = acc[:, :HID] * scale
    lifted = acc[:, FEAT:] * scale
    act[...] = (gate / (1.0 + jnp.exp(-gate)) * lifted).astype(BF)
    loads[2].wait()

    def far_tile(lane):
        cols = jnp.concatenate([columns(wd, 2 * i + lane, NEAR, FAR) for i in range(8)], axis=1)
        return jnp.dot(act[...], cols, preferred_element_type=F32).astype(BF)

    swap = remote(outb, gotb, ws.at[0], wr.at[0], peer)
    sends.drain_later(outb, ws.at[0])

    def aside():
        outb[...] = far_tile(1 - k)
        swap.start()

    def later():
        ownb[...] = far_tile(k)

    total = RingSum(spot, SLOTS, own, out, got, tbuf, rbuf, xs, xr, ts, tr, sends)

    def tile(i, mine):
        chunk = (z + ORDER[i]) % 8
        cols = columns(wd, 2 * chunk + (k if mine else 1 - k), 0, NEAR)
        return jnp.dot(act[...], cols, preferred_element_type=F32).astype(BF)

    total.begin(tile, aside, later)
    swap.wait_recv()
    summed = ownb[...].astype(F32) + gotb[...].astype(F32)
    qsb[...] = summed.reshape(BLOCKS, CAP, 8 * FAR).astype(BF)
    own_home = pltpu.make_async_copy(qsb.at[home_row], rb2.at[me], loc.at[1])
    own_home.start()
    for ty, tx in others(y, x):
        to = 4 * ty + tx
        remote(qsb.at[4 * (2 * (tx % 2) + tx // 2) + ty], rb2.at[me], b3s.at[0], b3r.at[0], at_ctx(to)).start()
    sends.drain_later(qsb.at[pl.ds(0, 15)], b3s.at[0])
    total.rest(tile)

    loads[3].wait()
    hit0, hit1 = slot_hits(ids_all[x])
    part_of = jnp.where(hit0, wts[0:1, :], 0.0) + jnp.where(hit1, wts[1:2, :], 0.0)
    coarse = part_of.astype(BF)
    fine = (part_of - coarse.astype(F32)).astype(BF)

    def combine(ref):
        back = ref[...].astype(F32).reshape(SLOTS, ref.shape[2]).astype(BF)
        dims = (((0,), (0,)), ((), ()))
        mixture = lax.dot_general(coarse, back, dims, preferred_element_type=F32)
        return mixture + lax.dot_general(fine, back, dims, preferred_element_type=F32)

    own_home.wait()
    receive(rb2.at[pl.ds(0, 15)], b3r.at[0])
    far_mix = combine(rb2)
    for i in range(8):
        pb[i] = far_mix[:, FAR * i : FAR * i + FAR].astype(BF)
    def along(src, dst, sem, dist):
        remote(src, dst, b4s.at[0], b4r.at[sem], (y, x, (z + dist + 8) % 8, k)).start()

    for d, sign in enumerate((1, -1)):
        rows = pl.ds(64 * d, 64)
        along(pb.at[(z + 4) % 8, rows], gb.at[5 + 2 * d, rows], 2 + 2 * d, 2 * sign)
        along(pb.at[(z + 3 * sign + 8) % 8], gb.at[4 + 2 * d], 1 + 2 * d, sign)
        along(pb.at[(z + sign + 8) % 8], gb.at[d], 0, sign)
    sends.drain_later(pb.at[pl.ds(0, 7)], b4s.at[0])

    own_back = pltpu.make_async_copy(qs.at[home_row], rb.at[me], loc.at[5])
    for part in range(4):
        qs[part * 4 : part * 4 + 4] = total.result(part).reshape(4, CAP, NEAR).astype(BF)
        for i in range(4):
            row = (y + i) % 4
            home = remote(
                qs.at[4 * part + row], rb.at[me], qss.at[0], qsr.at[0], (row, STAND[part], z, k)
            )
            if i > 0:
                home.start()
            else:
                pl.when(STAND[part] != x)(home.start)
                pl.when(STAND[part] == x)(own_back.start)
    sends.drain_later(qs.at[pl.ds(0, 15)], qss.at[0])
    for d, sign in enumerate((1, -1)):
        rows = pl.ds(64 * d, 64)
        receive(gb.at[4 + 2 * d], b4r.at[1 + 2 * d])
        tb[d] = (pb[(z + 2 * sign + 8) % 8].astype(F32) + gb[4 + 2 * d].astype(F32)).astype(BF)
        receive(gb.at[5 + 2 * d, rows], b4r.at[2 + 2 * d])
        tb[d, rows, :] = (tb[d, rows, :].astype(F32) + gb[5 + 2 * d, rows, :].astype(F32)).astype(BF)
        along(tb.at[d], gb.at[2 + d], 0, 2 * sign)

    @pl.when(low != x)
    def _():
        handed.wait()

    @pl.when(low == x)
    def _():
        kept.wait()

    far_sum = hn[:, NEAR:].astype(F32) + pb[z].astype(F32)
    receive(gb.at[pl.ds(0, 4)], b4r.at[0])
    for i in range(4):
        far_sum += gb[i].astype(F32)
    o_ref[:, NEAR:] = far_sum.astype(BF)
    own_back.wait()
    receive(rb.at[pl.ds(0, 15)], qsr.at[0])
    o_ref[:, :NEAR] = (hn[:, :NEAR].astype(F32) + combine(rb)).astype(BF)


def layer(*refs):
    ins, o_ref, refs = refs[:14], refs[14], list(refs[15:])

    def take(n):
        taken = refs[:n]
        del refs[:n]
        return taken

    wg_hbm, wu_hbm, wd_hbm, wts_hbm = ins[10:]
    wgu, wd, wts, wsem = take(4)
    early = take(6)
    passed = h, ids_all, gains = take(3)
    mix_scratch = take(8)
    mix_ring = take(5)
    mix_sems = take(19)
    moe_scratch = take(21)
    moe_ring = take(5)
    moe_sems = take(27)
    loads = [
        pltpu.make_async_copy(wg_hbm, wgu.at[pl.ds(0, HID)], wsem.at[0]),
        pltpu.make_async_copy(wu_hbm, wgu.at[pl.ds(FEAT, HID)], wsem.at[1]),
        pltpu.make_async_copy(wd_hbm, wd, wsem.at[2]),
        pltpu.make_async_copy(wts_hbm, wts, wsem.at[3]),
    ]

    def start_weights():
        for cp in loads:
            cp.start()

    sends = Sends()
    mixer(
        *ins[:10], *early, *passed, *mix_scratch, *mix_ring, *mix_sems, start_weights, sends
    )
    experts(wts, wgu, wd, loads, *passed, o_ref, *moe_scratch, *moe_ring, *moe_sems, sends)
    y, x, z, k = place()
    sends.drain((y, x, z, 1 - k))


def dma(*shape):
    return pltpu.SemaphoreType.DMA(shape)


def ring_scratch(rows, width):
    quarter = rows // 4
    return [
        pltpu.VMEM((8, rows, width), BF),
        pltpu.VMEM((8, rows, width), BF),
        pltpu.VMEM((8, rows, width), BF),
        pltpu.VMEM((28, quarter, width), BF),
        pltpu.VMEM((28, quarter, width), BF),
    ]


ANY = pl.BlockSpec(memory_space=pl.ANY)


def shards(
    residual, query_rows, key_rows, value_rows, head_rates, doc_lengths, attn_gain, out_weight,
    moe_gain, expert_ids, expert_weights, gate_weight, up_weight, down_weight,
):
    return pl.pallas_call(
        layer,
        out_shape=jax.ShapeDtypeStruct((ROWS, FEAT), BF),
        in_specs=[ANY] * 14,
        out_specs=pl.BlockSpec(memory_space=pltpu.VMEM),
        scratch_shapes=[
            pltpu.VMEM((FEAT + HID, D), BF),
            pltpu.VMEM((HID, D), BF),
            pltpu.VMEM((2, ROWS), F32),
            dma(4),
            pltpu.SMEM((64,), F32),
            pltpu.SMEM((4,), jnp.int32),
            pltpu.VMEM((ROWS, 512), BF),
            pltpu.VMEM((ROWS, 512), BF),
            pltpu.VMEM((ROWS, 512), BF),
            pltpu.VMEM((1, 512), F32),
            pltpu.VMEM((ROWS, FEAT), BF),
            pltpu.VMEM((4, 2, ROWS), jnp.int32),
            pltpu.VMEM((16, 1, FEAT), F32),
            pltpu.VMEM((4, 512, FEAT), BF),
            pltpu.VMEM((4, ROWS, 512), BF),
            pltpu.VMEM((512, HD), BF),
            pltpu.VMEM((16, 32, HD), BF),
            pltpu.VMEM((16, 32, HD), BF),
            pltpu.VMEM((16, 32, HD), BF),
            pltpu.VMEM((ROWS, FEAT), BF),
            pltpu.VMEM((ROWS, 512), F32),
            *ring_scratch(ROWS, FEAT),
            dma(1), dma(2, 3), dma(1), dma(2, 3),
            dma(1), dma(1), dma(1), dma(1), dma(1), dma(1),
            dma(1), dma(1), dma(1), dma(1), dma(1), dma(8), dma(1), dma(28), dma(12),
            pltpu.VMEM((2, SLOTS, ROWS), BF),
            pltpu.VMEM((BLOCKS, CAP, NEAR), BF),
            pltpu.VMEM((16, BLOCKS, CAP, NEAR), BF),
            pltpu.VMEM((8, ROWS, FAR), BF),
            pltpu.VMEM((BLOCKS, 2, CAP, 4 * FAR), BF),
            pltpu.VMEM((2, BLOCKS, 2, CAP, 4 * FAR), BF),
            pltpu.VMEM((SLOTS, 16 * FAR), BF),
            pltpu.VMEM((SLOTS, FEAT + HID), F32),
            pltpu.VMEM((SLOTS, 128), F32),
            pltpu.VMEM((SLOTS, HID), BF),
            pltpu.VMEM((ROWS, FEAT), BF),
            pltpu.VMEM((BLOCKS, CAP, NEAR), BF),
            pltpu.VMEM((BLOCKS, CAP, NEAR), BF),
            pltpu.VMEM((SLOTS, 8 * FAR), BF),
            pltpu.VMEM((SLOTS, 8 * FAR), BF),
            pltpu.VMEM((SLOTS, 8 * FAR), BF),
            pltpu.VMEM((BLOCKS, CAP, 8 * FAR), BF),
            pltpu.VMEM((BLOCKS, CAP, 8 * FAR), BF),
            pltpu.VMEM((8, ROWS, FAR), BF),
            pltpu.VMEM((8, ROWS, FAR), BF),
            pltpu.VMEM((2, ROWS, FAR), BF),
            *ring_scratch(SLOTS, NEAR),
            dma(1), dma(1), dma(1), dma(14), dma(1), dma(8),
            dma(1), dma(1), dma(1), dma(1), dma(1), dma(8), dma(1), dma(28), dma(6),
            dma(1), dma(3), dma(1), dma(1), dma(1), dma(1), dma(1), dma(1),
            dma(1), dma(1), dma(1), dma(5),
        ],
        compiler_params=pltpu.CompilerParams(
            collective_id=0, has_side_effects=True, vmem_limit_bytes=67043328
        ),
        name="layer",
    )(
        head_rates, doc_lengths, query_rows, key_rows, value_rows, attn_gain.reshape(1, -1),
        out_weight, residual, moe_gain, expert_ids.T,
        gate_weight[0].T, up_weight[0].T, down_weight[0], expert_weights.T,
    )


def solution(mesh):
    finer = Mesh(mesh.devices.reshape(4, 4, 8, 2), AXES)
    placed = (
        P(CTX, TP), P(CTX, TP), P(CTX, TP), P(CTX, TP), P(), P(), P(TP), P(TP, CTX), P(TP),
        P(CTX, None), P(CTX, None), P(CTX, None, TP), P(CTX, None, TP), P(CTX, TP, None),
    )
    return jax.shard_map(shards, mesh=finer, in_specs=placed, out_specs=P(CTX, TP), check_vma=False)
```
